32 devices in a mesh: tm: 4 (over y, core), slab: 2 (over x), coarse: 4 (over z).
Axes of the slice: x: 2, y: 2, z: 4, core: 2. Of those that a mesh axis runs over, the one named last changes fastest.
Arguments:
- states: float32 [4, 8, 64, 256], P('tm', 'slab', 'coarse'), may hold values from -6 to 6
- diffusivity: float32 [8, 64, 256], P('slab', 'coarse'), may hold values from 0.25 to 2
- velocity: float32 [3, 8, 64, 256], P(None, 'slab', 'coarse'), may hold values from -0.5 to 0.5
Outputs:
- new_states: float32 [4, 8, 64, 256], P('tm', 'slab', 'coarse')
The draws below stay inside these ranges and needn't reach their ends.
All inputs are finite; a program needn't handle non-finite values.
Results may differ from the reference program's by a relative error of at most 0.0001.
Values sent between devices are 32-bit elements; how exact they have to be, the bound alone decides.
No kernel may reach another device: no remote copies, remote signals or barrier semaphores. Data moves between devices by JAX's collectives and lax.ppermute only.
A program may use at most 64 MiB of HBM per device.

```python
import math
import jax
import jax.numpy as jnp

NY = 256
SECTIONS = 4
FINE_STEPS = 2
SPANS = 4
NZ = 8
NX = 64


def shard_levels(rng, extent, cuts, low, top_value):
    factor_of = 1.0
    for position, parts in cuts:
        heights = jax.random.uniform(jax.random.fold_in(jax.random.fold_in(rng, 6), position), (parts,), jnp.float32, low / len(cuts), top_value / len(cuts))
        factor_of = factor_of * jnp.repeat(jnp.exp(heights), extent[position] // parts).reshape((-1,) + (1,) * (len(extent) - 1 - position))
    return factor_of


def normal_values(own_key, shape, scale, limit, split=(), kind=jnp.bfloat16):
    array = scale * jax.random.normal(own_key, shape, jnp.float32)
    if split:
        array = array * shard_levels(own_key, shape, split, -0.22, 0.18)
    return jnp.clip(array, -limit, limit).astype(kind)


def setup_inputs(seed: int = 0) -> dict:
    key_list = jax.random.split(jax.random.key(seed), 4)
    return {
        "states": normal_values(key_list[0], (SPANS, NZ, NX, NY), 1.0, 6.0, ((0, 4), (1, 2), (2, 4)), jnp.float32),
        "diffusivity": jnp.clip(jnp.exp(math.log(2.0) - 2.0794415 * jax.random.uniform(key_list[1], (NZ, NX, NY), jnp.float32) ** shard_levels(key_list[1], (NZ, NX, NY), ((0, 2), (1, 4)), -0.2, 0.2)), 0.25, 2.0),
        "velocity": jnp.clip(jax.random.uniform(key_list[2], (3, NZ, NX, NY), jnp.float32, -0.5, 0.5) * shard_levels(key_list[2], (3, NZ, NX, NY), ((1, 2), (2, 4)), -0.4, 0.0), -0.5, 0.5),
    }


fine_step = 1.0
relaxation = 0.8


def chebyshev_coefficients(sections):
    damping = 0.05
    centre_point = 1.0 + damping / (sections * sections)
    chebyshev = [1.0, centre_point]
    slopes = [0.0, 1.0]
    for degree in range(2, sections + 1):
        chebyshev.append(2.0 * centre_point * chebyshev[degree - 1] - chebyshev[degree - 2])
        slopes.append(2.0 * chebyshev[degree - 1] + 2.0 * centre_point * slopes[degree - 1] - slopes[degree - 2])
    slope_ratio = chebyshev[sections] / slopes[sections]
    weights = [1.0 / entry for entry in chebyshev]
    scales = [0.0, 0.0]
    carries = [0.0, 0.0]
    tildes = [0.0, slope_ratio / centre_point]
    for degree in range(2, sections + 1):
        scales.append(2.0 * weights[degree] * centre_point / weights[degree - 1])
        carries.append(-weights[degree] / weights[degree - 2])
        tildes.append(2.0 * weights[degree] * slope_ratio / weights[degree - 1])
    return scales, carries, tildes


def stencil(padded, coeffs, spacing):
    centre = padded[1:-1, 1:-1, 1:-1]
    depth_after = padded[2:, 1:-1, 1:-1]
    depth_before = padded[:-2, 1:-1, 1:-1]
    row_after = padded[1:-1, 2:, 1:-1]
    row_before = padded[1:-1, :-2, 1:-1]
    column_after = padded[1:-1, 1:-1, 2:]
    column_before = padded[1:-1, 1:-1, :-2]
    beside_all = depth_after + depth_before + row_after + row_before + column_after + column_before
    spread = coeffs[0] * (beside_all - 6.0 * centre) / (spacing * spacing)
    drifts = (coeffs[1] * (depth_after - depth_before) + coeffs[2] * (row_after - row_before) + coeffs[3] * (column_after - column_before)) / (2.0 * spacing)
    return spread - drifts


def shrink(values):
    return values.reshape(values.shape[0] // 2, 2, values.shape[1] // 2, 2, values.shape[2] // 2, 2).mean(axis=(1, 3, 5))


def expand(values):
    return jnp.repeat(jnp.repeat(jnp.repeat(values, 2, 0), 2, 1), 2, 2)


def padding(values):
    return jnp.pad(values, 1)


def coarse_step(source, coeffs, coarse_coeffs):
    interval = FINE_STEPS * fine_step
    diagonal = 1.0 + 6.0 * interval * coeffs[0]

    def misfit(trial):
        return source - (trial - interval * stencil(padding(trial), coeffs, 1.0))

    smoothed = source + relaxation * misfit(source) / diagonal
    coarse_source = shrink(misfit(smoothed))
    coarse_diagonal = 1.0 + 6.0 * interval * coarse_coeffs[0] / 4.0
    guess_one = relaxation * coarse_source / coarse_diagonal
    coarse_misfit = coarse_source - (guess_one - interval * stencil(padding(guess_one), coarse_coeffs, 2.0))
    guess_two = guess_one + relaxation * coarse_misfit / coarse_diagonal
    second = smoothed + expand(guess_two)
    return second + relaxation * misfit(second) / diagonal


def fine_propagate(start_field, coeffs):
    scales, carries, tildes = chebyshev_coefficients(SECTIONS)
    for repeat in range(FINE_STEPS):
        before = start_field
        current = start_field + tildes[1] * fine_step * stencil(padding(start_field), coeffs, 1.0)
        for degree in range(2, SECTIONS + 1):
            update = scales[degree] * current + carries[degree] * before + tildes[degree] * fine_step * stencil(padding(current), coeffs, 1.0)
            before, current = current, update
        start_field = current
    return start_field


def reference(states, diffusivity, velocity):
    coeffs = jnp.concatenate([diffusivity[None], velocity], 0)
    coarse_coeffs = jnp.stack([shrink(coeffs[number]) for number in range(4)])
    corrections = []
    for period in range(SPANS):
        fine_end = fine_propagate(states[period], coeffs)
        corrections.append(fine_end - coarse_step(states[period], coeffs, coarse_coeffs))
    current = states[0]
    outputs = []
    for period in range(SPANS):
        current = coarse_step(current, coeffs, coarse_coeffs) + corrections[period]
        outputs.append(current)
    return jnp.stack(outputs)
```

```python
import functools

import jax
import jax.numpy as jnp
from jax import lax
from jax.experimental import pallas as pl
from jax.experimental.pallas import tpu as pltpu
from jax.sharding import PartitionSpec as P

SECTIONS = 4
FINE_STEPS = 2
FINE_STEP = 1.0
RELAX = 0.8
INTERVAL = FINE_STEPS * FINE_STEP
LANES = 128
PAD = 8
COARSE_REACH = 6
FINE_REACH = SECTIONS * FINE_STEPS


def chebyshev_coefficients(sections):
    damping = 0.05
    centre_point = 1.0 + damping / (sections * sections)
    chebyshev = [1.0, centre_point]
    slopes = [0.0, 1.0]
    for degree in range(2, sections + 1):
        chebyshev.append(2.0 * centre_point * chebyshev[degree - 1] - chebyshev[degree - 2])
        slopes.append(
            2.0 * chebyshev[degree - 1]
            + 2.0 * centre_point * slopes[degree - 1]
            - slopes[degree - 2]
        )
    slope_ratio = chebyshev[sections] / slopes[sections]
    weights = [1.0 / entry for entry in chebyshev]
    scales = [0.0, 0.0]
    carries = [0.0, 0.0]
    tildes = [0.0, slope_ratio / centre_point]
    for degree in range(2, sections + 1):
        scales.append(2.0 * weights[degree] * centre_point / weights[degree - 1])
        carries.append(-weights[degree] / weights[degree - 2])
        tildes.append(2.0 * weights[degree] * slope_ratio / weights[degree - 1])
    return (scales, carries, tildes)


def round_up(value, unit):
    return -(-value // unit) * unit


class Box:
    def __init__(self, depth, rows, side, columns):
        self.depth, self.rows, self.side, self.columns = depth, rows, side, columns
        self.height = rows + 2 * side
        self.tiles = columns // LANES

    def scratch(self, depth=None):
        depth = self.depth if depth is None else depth
        return pltpu.VMEM(
            (self.tiles, depth + 4, self.height + 2 * PAD, LANES), jnp.float32
        )

    def span(self, margin):
        first = (self.side - margin) // 8 * 8
        last = round_up(self.side + self.rows + margin, 8)
        assert first >= 0 and last <= self.height
        return first, last


CHUNK = 16


def chunks(first, last):
    at = first
    while at < last:
        size = min(CHUNK, last - at)
        yield at, size
        at += size


def each_plane(count, body):
    if count <= 8:
        for plane in range(count):
            body(plane)
    else:
        lax.fori_loop(0, count, lambda plane, _: (body(plane), 0)[1], 0)


def lane_index(size):
    return lax.broadcasted_iota(jnp.int32, (size, LANES), 1)


def row_index(size):
    return lax.broadcasted_iota(jnp.int32, (size, LANES), 0)


def sideways(values, step):
    size = values[0].shape[0]
    lane = lane_index(size)
    back = [pltpu.roll(entry, LANES - step, 1) for entry in values]
    forth = [pltpu.roll(entry, step, 1) for entry in values]
    zero = jnp.zeros_like(values[0])
    count = len(values)
    after = [
        jnp.where(lane >= LANES - step, back[i + 1] if i + 1 < count else zero, back[i])
        for i in range(count)
    ]
    before = [
        jnp.where(lane < step, forth[i - 1] if i else zero, forth[i]) for i in range(count)
    ]
    return after, before


def operator(field, coeff, plane, at, size, step):
    tiles = field.shape[0]
    centre = [field[i, plane + 2, pl.ds(PAD + at, size), :] for i in range(tiles)]
    after, before = sideways(centre, step)
    result = []
    for i in range(tiles):
        deep_after = field[i, plane + 3, pl.ds(PAD + at, size), :]
        deep_before = field[i, plane + 1, pl.ds(PAD + at, size), :]
        row_after = field[i, plane + 2, pl.ds(PAD + at + step, size), :]
        row_before = field[i, plane + 2, pl.ds(PAD + at - step, size), :]
        c = [coeff[k, plane, pl.ds(at, size), i * LANES : (i + 1) * LANES] for k in range(4)]
        total = (deep_after + deep_before) + (row_after + row_before) + (after[i] + before[i])
        spread = c[0] * (total - 6.0 * centre[i])
        drift = (
            c[1] * (deep_after - deep_before)
            + c[2] * (row_after - row_before)
            + c[3] * (after[i] - before[i])
        )
        result.append((spread, drift, centre[i]))
    return result


def clear(field):
    field[...] = jnp.zeros_like(field)


def fine_body(box, margin, start, coeff, end, one, two):
    scales, carries, tildes = chebyshev_coefficients(SECTIONS)
    clear(one)
    clear(two)
    inner = slice(PAD, PAD + box.height)
    for i in range(box.tiles):
        one[i, 2 : 2 + box.depth, inner, :] = start[:, :, i * LANES : (i + 1) * LANES]
    stage = 0
    current, other = one, two
    for repeat in range(FINE_STEPS):
        for degree in range(1, SECTIONS + 1):
            stage += 1
            first, last = box.span(margin + FINE_REACH - stage)

            def plane_body(plane, current=current, other=other, degree=degree):
                for at, size in chunks(first, last):
                    values = operator(current, coeff, plane, at, size, 1)
                    for i, (spread, drift, centre) in enumerate(values):
                        change = tildes[degree] * FINE_STEP * (spread - 0.5 * drift)
                        where = (i, plane + 2, pl.ds(PAD + at, size), slice(None))
                        if degree == 1:
                            other[where] = centre + change
                        else:
                            other[where] = (
                                scales[degree] * centre + carries[degree] * other[where] + change
                            )

            each_plane(box.depth, plane_body)
            current, other = other, current
    first, last = box.span(margin)
    for i in range(box.tiles):
        end[:, :, i * LANES : (i + 1) * LANES] = current[
            i, 2 : 2 + box.depth, PAD + first : PAD + last, :
        ]


def pair_columns(value):
    lane = lane_index(value.shape[0])
    other = jnp.where(
        lane % 2 == 0, pltpu.roll(value, LANES - 1, 1), pltpu.roll(value, 1, 1)
    )
    return value + other


def pair_rows(field, i, plane, at, size):
    row = row_index(size)
    other = jnp.where(
        row % 2 == 0,
        field[i, plane + 2, pl.ds(PAD + at + 1, size), :],
        field[i, plane + 2, pl.ds(PAD + at - 1, size), :],
    )
    return field[i, plane + 2, pl.ds(PAD + at, size), :] + other


def prepare_body(box, coeff, coarse, weight, coarse_weight, work):
    clear(work)
    for k in range(4):

        def columns_body(plane, k=k):
            for at, size in chunks(0, box.height):
                for i in range(box.tiles):
                    cols = slice(i * LANES, (i + 1) * LANES)
                    low = coeff[k, 2 * plane, pl.ds(at, size), cols]
                    high = coeff[k, 2 * plane + 1, pl.ds(at, size), cols]
                    work[i, plane + 2, pl.ds(PAD + at, size), :] = pair_columns(low + high)
                    if k == 0:
                        weight[2 * plane, pl.ds(at, size), cols] = RELAX / (
                            1.0 + 6.0 * INTERVAL * low
                        )
                        weight[2 * plane + 1, pl.ds(at, size), cols] = RELAX / (
                            1.0 + 6.0 * INTERVAL * high
                        )

        each_plane(box.depth // 2, columns_body)

        def rows_body(plane, k=k):
            for at, size in chunks(0, box.height):
                for i in range(box.tiles):
                    cols = slice(i * LANES, (i + 1) * LANES)
                    mean = 0.125 * pair_rows(work, i, plane, at, size)
                    coarse[k, plane, pl.ds(at, size), cols] = mean
                    if k == 0:
                        coarse_weight[plane, pl.ds(at, size), cols] = RELAX / (
                            1.0 + 6.0 * INTERVAL * mean / 4.0
                        )

        each_plane(box.depth // 2, rows_body)


def coarse_step_body(box, margin, source, trial, pairs, guess, residual, params, finish):
    coeff, coarse, weight, coarse_weight = params
    half = box.depth // 2

    def cols(i):
        return slice(i * LANES, (i + 1) * LANES)

    first, last = box.span(margin + 5)

    def smooth(plane):
        for at, size in chunks(first, last):
            values = operator(source, coeff, plane, at, size, 1)
            for i, (spread, drift, centre) in enumerate(values):
                change = INTERVAL * spread - (INTERVAL * 0.5) * drift
                trial[i, plane + 2, pl.ds(PAD + at, size), :] = (
                    centre + weight[plane, pl.ds(at, size), cols(i)] * change
                )

    each_plane(box.depth, smooth)

    first, last = box.span(margin + 4)

    def restrict(plane):
        for at, size in chunks(first, last):
            sums = [None] * box.tiles
            for half_plane in range(2):
                fine_plane = 2 * plane + half_plane
                values = operator(trial, coeff, fine_plane, at, size, 1)
                for i, (spread, drift, centre) in enumerate(values):
                    misfit = (
                        source[i, fine_plane + 2, pl.ds(PAD + at, size), :]
                        - centre
                        + (INTERVAL * spread - (INTERVAL * 0.5) * drift)
                    )
                    sums[i] = misfit if sums[i] is None else sums[i] + misfit
            for i in range(box.tiles):
                pairs[i, plane + 2, pl.ds(PAD + at, size), :] = pair_columns(sums[i])

    each_plane(half, restrict)

    def first_guess(plane):
        for at, size in chunks(first, last):
            for i in range(box.tiles):
                mean = 0.125 * pair_rows(pairs, i, plane, at, size)
                residual[i, plane + 2, pl.ds(PAD + at, size), :] = mean
                guess[i, plane + 2, pl.ds(PAD + at, size), :] = (
                    coarse_weight[plane, pl.ds(at, size), cols(i)] * mean
                )

    each_plane(half, first_guess)

    first, last = box.span(margin + 2)

    def correct(plane):
        for at, size in chunks(first, last):
            values = operator(guess, coarse, plane, at, size, 2)
            for i, (spread, drift, centre) in enumerate(values):
                change = (INTERVAL / 4.0) * (spread - drift)
                rest = residual[i, plane + 2, pl.ds(PAD + at, size), :] - centre + change
                fix = centre + coarse_weight[plane, pl.ds(at, size), cols(i)] * rest
                for half_plane in range(2):
                    where = (i, 2 * plane + half_plane + 2, pl.ds(PAD + at, size), slice(None))
                    trial[where] = trial[where] + fix

    each_plane(half, correct)

    first, last = box.span(margin)

    def smooth_again(plane):
        for at, size in chunks(first, last):
            values = operator(trial, coeff, plane, at, size, 1)
            for i, (spread, drift, centre) in enumerate(values):
                misfit = (
                    source[i, plane + 2, pl.ds(PAD + at, size), :]
                    - centre
                    + (INTERVAL * spread - (INTERVAL * 0.5) * drift)
                )
                finish(
                    plane, i, at, size, centre + weight[plane, pl.ds(at, size), cols(i)] * misfit
                )

    each_plane(box.depth, smooth_again)


def coarse_scratch(box):
    half = box.depth // 2
    return [box.scratch(), box.scratch(half), box.scratch(half), box.scratch(half)]


def pair_body(
    box, low_side, start_end, second_start, second_end, *rest
):
    params, out, (source, trial, pairs, guess, residual) = rest[:4], rest[4], rest[5:]
    clear(source)
    clear(trial)
    clear(pairs)
    clear(guess)
    first, last = box.span(COARSE_REACH)
    for i in range(box.tiles):
        cols = slice(i * LANES, (i + 1) * LANES)
        source[i, 2 : 2 + box.depth, PAD + first : PAD + last, :] = (
            start_end[:, :, cols] - second_start[:, first:last, cols]
        )

    def finish(plane, i, at, size, value):
        cols = slice(i * LANES, (i + 1) * LANES)
        out[plane, pl.ds(at - box.side, size), cols] = (
            value + second_end[plane, pl.ds(at - first, size), cols]
        )

    coarse_step_body(box, 0, source, trial, pairs, guess, residual, params, finish)


def last_body(box, error, *rest):
    params, once, twice, (source, second, trial, pairs, guess, residual) = (
        rest[:4],
        rest[4],
        rest[5],
        rest[6:],
    )
    clear(source)
    clear(second)
    clear(trial)
    clear(pairs)
    clear(guess)
    for i in range(box.tiles):
        cols = slice(i * LANES, (i + 1) * LANES)
        source[i, 2 : 2 + box.depth, PAD : PAD + box.height, :] = error[:, :, cols]

    def finish_once(plane, i, at, size, value):
        second[i, plane + 2, pl.ds(PAD + at, size), :] = value

    coarse_step_body(
        box, COARSE_REACH, source, trial, pairs, guess, residual, params, finish_once
    )
    for i in range(box.tiles):
        cols = slice(i * LANES, (i + 1) * LANES)
        once[:, :, cols] = second[
            i, 2 : 2 + box.depth, PAD + box.side : PAD + box.side + box.rows, :
        ]

    def finish_twice(plane, i, at, size, value):
        cols = slice(i * LANES, (i + 1) * LANES)
        twice[plane, pl.ds(at - box.side, size), cols] = value

    coarse_step_body(box, 0, second, trial, pairs, guess, residual, params, finish_twice)


def run(body, outs, scratch, *args):
    whole = pl.BlockSpec(memory_space=pltpu.VMEM)
    single = not isinstance(outs, list)
    shapes = [outs] if single else outs
    result = pl.pallas_call(
        body,
        out_shape=[jax.ShapeDtypeStruct(shape, jnp.float32) for shape in shapes],
        in_specs=[whole] * len(args),
        out_specs=[whole] * len(shapes),
        scratch_shapes=scratch,
    )(*args)
    return result[0] if single else result


def slab_gathered(block, dim):
    count = lax.axis_size("slab")
    if count == 1:
        return block
    if count != 2:
        return lax.all_gather(block, "slab", axis=dim, tiled=True)
    other = lax.ppermute(block, "slab", [(0, 1), (1, 0)])
    first = lax.axis_index("slab") == 0
    low = jnp.where(first, block, other)
    high = jnp.where(first, other, block)
    return jnp.concatenate([low, high], axis=dim)


def row_slice(block, first, last):
    return lax.slice_in_dim(block, first, last, axis=block.ndim - 2)


def with_rows(block, width, side):
    count = lax.axis_size("coarse")
    rows = block.shape[-2]
    place = lax.axis_index("coarse")
    odd = place % 2 == 1
    one = [(i, i ^ 1) for i in range(count) if i ^ 1 < count]
    two = [(i, i + 1 if i % 2 else i - 1) for i in range(count)]
    two = [(i, j) for i, j in two if 0 <= j < count]
    low, high = [], []
    from_low, from_high = block, block
    left = width
    while left > 0:
        size = min(rows, left)
        up = row_slice(from_low, from_low.shape[-2] - size, from_low.shape[-2])
        down = row_slice(from_high, 0, size)
        got_one = lax.ppermute(jnp.where(odd, down, up), "coarse", one)
        got_two = lax.ppermute(jnp.where(odd, up, down), "coarse", two)
        from_low = jnp.where(odd, got_one, got_two)
        from_high = jnp.where(odd, got_two, got_one)
        low.insert(0, from_low)
        high.append(from_high)
        left -= size
    shape = list(block.shape)
    shape[-2] = side - width
    zeros = jnp.zeros(shape, jnp.float32)
    return jnp.concatenate([zeros, *low, block, *high, zeros], axis=block.ndim - 2)


def core_swapped(block):
    count = lax.axis_size("tm")
    assert count % 2 == 0
    return lax.ppermute(block, "tm", [(i, i ^ 1) for i in range(count)])


def ordered(mine, other, second):
    return jnp.where(second, other, mine), jnp.where(second, mine, other)


def per_device(states, diffusivity, velocity):
    windows = lax.axis_size("tm")
    place = lax.axis_index("tm")
    second = place % 2 == 1
    own_depth = diffusivity.shape[0]
    rows, columns = diffusivity.shape[1:]
    reach = FINE_REACH + COARSE_REACH
    side = round_up(max(reach, 2 * COARSE_REACH), 8)
    depth = own_depth * lax.axis_size("slab")
    box = Box(depth, rows, side, columns)

    coeffs = jnp.concatenate([diffusivity[None], velocity], 0)
    share = jnp.where(second, coeffs[2:], coeffs[:2])
    parcel = jnp.concatenate([states, share], 0)
    parcel = with_rows(slab_gathered(parcel, 1), reach, side)
    other = core_swapped(parcel)
    start = parcel[0]
    first_start, second_start = ordered(start, other[0], second)
    low_coeffs, high_coeffs = ordered(parcel[1:], other[1:], second)
    coeff = jnp.concatenate([low_coeffs, high_coeffs], 0)

    first, last = box.span(COARSE_REACH)
    end = run(
        functools.partial(fine_body, box, COARSE_REACH),
        (depth, last - first, columns),
        [box.scratch(), box.scratch()],
        start,
        coeff,
    )
    half = depth // 2
    params = run(
        functools.partial(prepare_body, box),
        [
            (4, half, box.height, columns),
            (depth, box.height, columns),
            (half, box.height, columns),
        ],
        [box.scratch(half)],
        coeff,
    )
    params = [coeff, *params]
    first_end, second_end = ordered(end, core_swapped(end), second)
    joined = run(
        functools.partial(pair_body, box, first),
        (depth, rows, columns),
        [box.scratch()] + coarse_scratch(box),
        first_end,
        second_start,
        second_end,
        *params,
    )
    own_first = row_slice(first_end, side - first, side - first + rows)
    result_first, result_second = own_first, joined
    leaving = joined
    for turn in range(1, windows // 2):
        arrived = lax.ppermute(
            leaving, "tm", [(i, (i + 2) % windows) for i in range(windows)]
        )
        arrived = with_rows(arrived, 2 * COARSE_REACH, side)
        mine = place // 2 == turn
        error = arrived - first_start
        once, twice = run(
            functools.partial(last_body, box),
            [(depth, rows, columns)] * 2,
            [box.scratch()] * 2 + coarse_scratch(box),
            error,
            *params,
        )
        result_first = jnp.where(mine, own_first + once, result_first)
        leaving = joined + twice
        result_second = jnp.where(mine, leaving, result_second)
    result = jnp.where(second, result_second, result_first)
    return lax.dynamic_slice_in_dim(
        result, lax.axis_index("slab") * own_depth, own_depth, 0
    )[None]


def solution(mesh):
    return jax.shard_map(
        per_device,
        mesh=mesh,
        in_specs=(
            P("tm", "slab", "coarse", None),
            P("slab", "coarse", None),
            P(None, "slab", "coarse", None),
        ),
        out_specs=P("tm", "slab", "coarse", None),
        check_vma=False,
    )
```

```python
import functools

import jax
import jax.numpy as jnp
from jax import lax
from jax.experimental import pallas as pl
from jax.experimental.pallas import tpu as pltpu
from jax.sharding import PartitionSpec as P

SECTIONS = 4
FINE_STEPS = 2
FINE_STEP = 1.0
RELAX = 0.8
INTERVAL = FINE_STEPS * FINE_STEP
LANES = 128
PAD = 8
COARSE_REACH = 6
FINE_REACH = SECTIONS * FINE_STEPS


def chebyshev_coefficients(sections):
    damping = 0.05
    centre_point = 1.0 + damping / (sections * sections)
    chebyshev = [1.0, centre_point]
    slopes = [0.0, 1.0]
    for degree in range(2, sections + 1):
        chebyshev.append(2.0 * centre_point * chebyshev[degree - 1] - chebyshev[degree - 2])
        slopes.append(
            2.0 * chebyshev[degree - 1]
            + 2.0 * centre_point * slopes[degree - 1]
            - slopes[degree - 2]
        )
    slope_ratio = chebyshev[sections] / slopes[sections]
    weights = [1.0 / entry for entry in chebyshev]
    scales = [0.0, 0.0]
    carries = [0.0, 0.0]
    tildes = [0.0, slope_ratio / centre_point]
    for degree in range(2, sections + 1):
        scales.append(2.0 * weights[degree] * centre_point / weights[degree - 1])
        carries.append(-weights[degree] / weights[degree - 2])
        tildes.append(2.0 * weights[degree] * slope_ratio / weights[degree - 1])
    return (scales, carries, tildes)


def round_up(value, unit):
    return -(-value // unit) * unit


class Box:
    def __init__(self, depth, rows, side, columns):
        self.depth, self.rows, self.side, self.columns = depth, rows, side, columns
        self.height = rows + 2 * side
        self.tiles = columns // LANES

    def scratch(self, depth=None):
        depth = self.depth if depth is None else depth
        return pltpu.VMEM(
            (self.tiles, depth + 4, self.height + 2 * PAD, LANES), jnp.float32
        )

    def span(self, margin):
        first = (self.side - margin) // 8 * 8
        last = round_up(self.side + self.rows + margin, 8)
        assert first >= 0 and last <= self.height
        return first, last


CHUNK = 16


def chunks(first, last):
    at = first
    while at < last:
        size = min(CHUNK, last - at)
        yield at, size
        at += size


def each_plane(count, body):
    if count <= 8:
        for plane in range(count):
            body(plane)
    else:
        lax.fori_loop(0, count, lambda plane, _: (body(plane), 0)[1], 0)


def lane_index(size):
    return lax.broadcasted_iota(jnp.int32, (size, LANES), 1)


def row_index(size):
    return lax.broadcasted_iota(jnp.int32, (size, LANES), 0)


def sideways(values, step):
    size = values[0].shape[0]
    lane = lane_index(size)
    back = [pltpu.roll(entry, LANES - step, 1) for entry in values]
    forth = [pltpu.roll(entry, step, 1) for entry in values]
    zero = jnp.zeros_like(values[0])
    count = len(values)
    after = [
        jnp.where(lane >= LANES - step, back[i + 1] if i + 1 < count else zero, back[i])
        for i in range(count)
    ]
    before = [
        jnp.where(lane < step, forth[i - 1] if i else zero, forth[i]) for i in range(count)
    ]
    return after, before


def operator(field, coeff, plane, at, size, step):
    tiles = field.shape[0]
    centre = [field[i, plane + 2, pl.ds(PAD + at, size), :] for i in range(tiles)]
    after, before = sideways(centre, step)
    result = []
    for i in range(tiles):
        deep_after = field[i, plane + 3, pl.ds(PAD + at, size), :]
        deep_before = field[i, plane + 1, pl.ds(PAD + at, size), :]
        row_after = field[i, plane + 2, pl.ds(PAD + at + step, size), :]
        row_before = field[i, plane + 2, pl.ds(PAD + at - step, size), :]
        c = [coeff[k, i, plane, pl.ds(at, size), :] for k in range(4)]
        total = (deep_after + deep_before) + (row_after + row_before) + (after[i] + before[i])
        spread = c[0] * (total - 6.0 * centre[i])
        drift = (
            c[1] * (deep_after - deep_before)
            + c[2] * (row_after - row_before)
            + c[3] * (after[i] - before[i])
        )
        result.append((spread, drift, centre[i]))
    return result


def clear(field):
    field[...] = jnp.zeros_like(field)


def fine_body(box, margin, own_depth, blocks, *refs):
    own, own_halo = refs[:blocks], refs[blocks]
    other, other_halo = refs[blocks + 1 : 2 * blocks + 1], refs[2 * blocks + 1]
    end, starts, coeff, one, two = refs[2 * blocks + 2 :]
    core = lax.axis_index("tm") % 2
    shift = lax.axis_index("slab") if blocks == 2 else 0
    rows, side = box.rows, box.side
    width = own_halo.shape[-2]
    clear(one)
    clear(two)
    inner = slice(PAD, PAD + box.height)
    if width < side:
        zeros = jnp.zeros((box.tiles, box.depth, 8, LANES), jnp.float32)
        for array in range(4):
            coeff[array, :, :, 0:8, :] = zeros
            coeff[array, :, :, box.height - 8 :, :] = zeros
        for array in range(2):
            starts[array, :, :, 0:8, :] = zeros
            starts[array, :, :, box.height - 8 :, :] = zeros
    for pieces, halo, rank in ((own, own_halo, core), (other, other_halo, 1 - core)):
        for block in range(blocks):
            base = (block + shift) % blocks * own_depth
            for plane in range(own_depth):
                for i in range(box.tiles):
                    cols = slice(i * LANES, (i + 1) * LANES)
                    for array in range(3):
                        centre = pieces[block][array, plane, :, cols]
                        low = halo[0, block, array, plane, :, cols]
                        high = halo[1, block, array, plane, :, cols]
                        targets = []
                        if array == 0:
                            targets.append((starts.at[rank, i, base + plane], 0))
                            if pieces is own:
                                targets.append((one.at[i, base + plane + 2], PAD))
                        else:
                            targets.append((coeff.at[2 * rank + array - 1, i, base + plane], 0))
                        for target, at in targets:
                            target[at + side - width : at + side, :] = low
                            target[at + side : at + side + rows, :] = centre
                            target[at + side + rows : at + side + rows + width, :] = high
    scales, carries, tildes = chebyshev_coefficients(SECTIONS)
    stage = 0
    current, other = one, two
    for repeat in range(FINE_STEPS):
        for degree in range(1, SECTIONS + 1):
            stage += 1
            first, last = box.span(margin + FINE_REACH - stage)

            def plane_body(plane, current=current, other=other, degree=degree):
                for at, size in chunks(first, last):
                    values = operator(current, coeff, plane, at, size, 1)
                    for i, (spread, drift, centre) in enumerate(values):
                        change = tildes[degree] * FINE_STEP * (spread - 0.5 * drift)
                        where = (i, plane + 2, pl.ds(PAD + at, size), slice(None))
                        if degree == 1:
                            other[where] = centre + change
                        else:
                            other[where] = (
                                scales[degree] * centre + carries[degree] * other[where] + change
                            )

            each_plane(box.depth, plane_body)
            current, other = other, current
    first, last = box.span(margin)
    end[...] = current[:, 2 : 2 + box.depth, PAD + first : PAD + last, :]


def pair_columns(value):
    lane = lane_index(value.shape[0])
    other = jnp.where(
        lane % 2 == 0, pltpu.roll(value, LANES - 1, 1), pltpu.roll(value, 1, 1)
    )
    return value + other


def pair_rows(field, i, plane, at, size):
    row = row_index(size)
    other = jnp.where(
        row % 2 == 0,
        field[i, plane + 2, pl.ds(PAD + at + 1, size), :],
        field[i, plane + 2, pl.ds(PAD + at - 1, size), :],
    )
    return field[i, plane + 2, pl.ds(PAD + at, size), :] + other


def prepare_body(box, coeff, coarse, weight, coarse_weight, work):
    clear(work)
    for k in range(4):

        def columns_body(plane, k=k):
            for at, size in chunks(0, box.height):
                for i in range(box.tiles):
                    low = coeff[k, i, 2 * plane, pl.ds(at, size), :]
                    high = coeff[k, i, 2 * plane + 1, pl.ds(at, size), :]
                    work[i, plane + 2, pl.ds(PAD + at, size), :] = pair_columns(low + high)
                    if k == 0:
                        weight[i, 2 * plane, pl.ds(at, size), :] = RELAX / (
                            1.0 + 6.0 * INTERVAL * low
                        )
                        weight[i, 2 * plane + 1, pl.ds(at, size), :] = RELAX / (
                            1.0 + 6.0 * INTERVAL * high
                        )

        each_plane(box.depth // 2, columns_body)

        def rows_body(plane, k=k):
            for at, size in chunks(0, box.height):
                for i in range(box.tiles):
                    mean = 0.125 * pair_rows(work, i, plane, at, size)
                    coarse[k, i, plane, pl.ds(at, size), :] = mean
                    if k == 0:
                        coarse_weight[i, plane, pl.ds(at, size), :] = RELAX / (
                            1.0 + 6.0 * INTERVAL * mean / 4.0
                        )

        each_plane(box.depth // 2, rows_body)


def coarse_step_body(box, margin, source, trial, pairs, guess, residual, params, finish):
    coeff, coarse, weight, coarse_weight = params
    half = box.depth // 2

    first, last = box.span(margin + 5)

    def smooth(plane):
        for at, size in chunks(first, last):
            values = operator(source, coeff, plane, at, size, 1)
            for i, (spread, drift, centre) in enumerate(values):
                change = INTERVAL * spread - (INTERVAL * 0.5) * drift
                trial[i, plane + 2, pl.ds(PAD + at, size), :] = (
                    centre + weight[i, plane, pl.ds(at, size), :] * change
                )

    each_plane(box.depth, smooth)

    first, last = box.span(margin + 4)

    def restrict(plane):
        for at, size in chunks(first, last):
            sums = [None] * box.tiles
            for half_plane in range(2):
                fine_plane = 2 * plane + half_plane
                values = operator(trial, coeff, fine_plane, at, size, 1)
                for i, (spread, drift, centre) in enumerate(values):
                    misfit = (
                        source[i, fine_plane + 2, pl.ds(PAD + at, size), :]
                        - centre
                        + (INTERVAL * spread - (INTERVAL * 0.5) * drift)
                    )
                    sums[i] = misfit if sums[i] is None else sums[i] + misfit
            for i in range(box.tiles):
                pairs[i, plane + 2, pl.ds(PAD + at, size), :] = pair_columns(sums[i])

    each_plane(half, restrict)

    def first_guess(plane):
        for at, size in chunks(first, last):
            for i in range(box.tiles):
                mean = 0.125 * pair_rows(pairs, i, plane, at, size)
                residual[i, plane + 2, pl.ds(PAD + at, size), :] = mean
                guess[i, plane + 2, pl.ds(PAD + at, size), :] = (
                    coarse_weight[i, plane, pl.ds(at, size), :] * mean
                )

    each_plane(half, first_guess)

    first, last = box.span(margin + 2)

    def correct(plane):
        for at, size in chunks(first, last):
            values = operator(guess, coarse, plane, at, size, 2)
            for i, (spread, drift, centre) in enumerate(values):
                change = (INTERVAL / 4.0) * (spread - drift)
                rest = residual[i, plane + 2, pl.ds(PAD + at, size), :] - centre + change
                fix = centre + coarse_weight[i, plane, pl.ds(at, size), :] * rest
                for half_plane in range(2):
                    where = (i, 2 * plane + half_plane + 2, pl.ds(PAD + at, size), slice(None))
                    trial[where] = trial[where] + fix

    each_plane(half, correct)

    first, last = box.span(margin)

    def smooth_again(plane):
        for at, size in chunks(first, last):
            values = operator(trial, coeff, plane, at, size, 1)
            for i, (spread, drift, centre) in enumerate(values):
                misfit = (
                    source[i, plane + 2, pl.ds(PAD + at, size), :]
                    - centre
                    + (INTERVAL * spread - (INTERVAL * 0.5) * drift)
                )
                finish(
                    plane, i, at, size, centre + weight[i, plane, pl.ds(at, size), :] * misfit
                )

    each_plane(box.depth, smooth_again)


def coarse_scratch(box):
    half = box.depth // 2
    return [box.scratch(), box.scratch(half), box.scratch(half), box.scratch(half)]


def pair_body(box, own_end, other_end, starts, *rest):
    params, out, first_out = rest[:4], rest[4], rest[5]
    source, trial, pairs, guess, residual = rest[6:]
    core = lax.axis_index("tm") % 2
    clear(source)
    clear(trial)
    clear(pairs)
    clear(guess)
    first, last = box.span(COARSE_REACH)

    def put(first_end, second_end):
        source[:, 2 : 2 + box.depth, PAD + first : PAD + last, :] = (
            first_end[...] - starts[1, :, :, first:last, :]
        )
        inner = slice(box.side - first, box.side - first + box.rows)
        out[...] = second_end[:, :, inner, :]
        first_out[...] = first_end[:, :, inner, :]

    @pl.when(core == 0)
    def _():
        put(own_end, other_end)

    @pl.when(core == 1)
    def _():
        put(other_end, own_end)

    def finish(plane, i, at, size, value):
        where = (i, plane, pl.ds(at - box.side, size), slice(None))
        out[where] = value + out[where]

    coarse_step_body(box, 0, source, trial, pairs, guess, residual, params, finish)


def last_body(box, own_depth, turn, first_end, joined, centre, low, high, starts, *rest):
    params, result, leaving = rest[:4], rest[4], rest[5]
    source, second, trial, pairs, guess, residual = rest[6:]
    place = lax.axis_index("tm")
    core = place % 2
    active = place // 2 == turn
    clear(source)
    clear(second)
    clear(trial)
    clear(pairs)
    clear(guess)
    side, rows = box.side, box.rows
    width = low.shape[-2]

    @pl.when(active)
    def _():
        for value, at, size in (
            (low, side - width, width),
            (centre, side, rows),
            (high, side + rows, width),
        ):
            source[:, 2 : 2 + box.depth, PAD + at : PAD + at + size, :] = (
                value[...] - starts[0, :, :, at : at + size, :]
            )

    def finish_once(plane, i, at, size, value):
        second[i, plane + 2, pl.ds(PAD + at, size), :] = value

    coarse_step_body(
        box, COARSE_REACH, source, trial, pairs, guess, residual, params, finish_once
    )

    def finish_twice(plane, i, at, size, value):
        where = (i, plane, pl.ds(at - box.side, size), slice(None))
        leaving[where] = value + joined[where]

    coarse_step_body(box, 0, second, trial, pairs, guess, residual, params, finish_twice)
    base = lax.axis_index("slab") * own_depth

    @pl.when(core == 0)
    def _():
        for i in range(box.tiles):
            result[0, :, :, i * LANES : (i + 1) * LANES] = (
                first_end[i, pl.ds(base, own_depth)]
                + second[i, pl.ds(base + 2, own_depth), PAD + side : PAD + side + rows, :]
            )

    @pl.when(core == 1)
    def _():
        for i in range(box.tiles):
            result[0, :, :, i * LANES : (i + 1) * LANES] = leaving[i, pl.ds(base, own_depth)]


def run(body, outs, scratch, *args):
    whole = pl.BlockSpec(memory_space=pltpu.VMEM)
    single = not isinstance(outs, list)
    shapes = [outs] if single else outs
    result = pl.pallas_call(
        body,
        out_shape=[jax.ShapeDtypeStruct(shape, jnp.float32) for shape in shapes],
        in_specs=[whole] * len(args),
        out_specs=[whole] * len(shapes),
        scratch_shapes=scratch,
    )(*args)
    return result[0] if single else result


def slab_blocks(block):
    count = lax.axis_size("slab")
    if count == 1:
        return [block]
    if count == 2:
        return [block, lax.ppermute(block, "slab", [(0, 1), (1, 0)])]
    gathered = lax.all_gather(block, "slab", axis=0)
    return [gathered[i] for i in range(count)]


def row_slice(block, first, last):
    return lax.slice_in_dim(block, first, last, axis=block.ndim - 2)


def row_pairs(count):
    one = [(i, i ^ 1) for i in range(count) if i ^ 1 < count]
    two = [(i, i + 1 if i % 2 else i - 1) for i in range(count)]
    return one, [(i, j) for i, j in two if 0 <= j < count]


def row_halo(blocks, width):
    rows = blocks[0].shape[-2]
    odd = lax.axis_index("coarse") % 2 == 1
    one, two = row_pairs(lax.axis_size("coarse"))
    low, high = [], []
    from_low, from_high = blocks, blocks
    left = width
    while left > 0:
        size = min(rows, left)
        up = jnp.stack([row_slice(b, b.shape[-2] - size, b.shape[-2]) for b in from_low])
        down = jnp.stack([row_slice(b, 0, size) for b in from_high])
        got_one = lax.ppermute(jnp.where(odd, down, up), "coarse", one)
        got_two = lax.ppermute(jnp.where(odd, up, down), "coarse", two)
        low.insert(0, jnp.where(odd, got_one, got_two))
        high.append(jnp.where(odd, got_two, got_one))
        from_low, from_high = list(low[0]), list(high[-1])
        left -= size
    low, high = (
        x[0] if len(x) == 1 else jnp.concatenate(x, axis=x[0].ndim - 2) for x in (low, high)
    )
    return jnp.stack([low, high])


def core_swapped(block):
    count = lax.axis_size("tm")
    assert count % 2 == 0
    return lax.ppermute(block, "tm", [(i, i ^ 1) for i in range(count)])


def next_pair(block, width):
    windows, count = lax.axis_size("tm"), lax.axis_size("coarse")
    rows = block.shape[-2]
    hop = [(t, (t + 2) % windows) for t in range(windows)]
    if width > rows:
        centre = lax.ppermute(block, "tm", hop)
        halo = row_halo([centre], width)
        return centre, halo[0, 0], halo[1, 0]
    odd = lax.axis_index("coarse") % 2 == 1
    both = ("tm", "coarse")
    one, two = (
        [(t * count + i, u * count + j) for t, u in hop for i, j in pairs]
        for pairs in row_pairs(count)
    )
    up, down = row_slice(block, rows - width, rows), row_slice(block, 0, width)
    centre = lax.ppermute(block, "tm", hop)
    got_one = lax.ppermute(jnp.where(odd, down, up), both, one)
    got_two = lax.ppermute(jnp.where(odd, up, down), both, two)
    return centre, jnp.where(odd, got_one, got_two), jnp.where(odd, got_two, got_one)


def per_device(states, diffusivity, velocity):
    windows = lax.axis_size("tm")
    place = lax.axis_index("tm")
    second = place % 2 == 1
    own_depth, rows, columns = diffusivity.shape
    reach = FINE_REACH + COARSE_REACH
    side = round_up(max(reach, 2 * COARSE_REACH), 8)
    depth = own_depth * lax.axis_size("slab")
    box = Box(depth, rows, side, columns)
    tiles, height, half = box.tiles, box.height, depth // 2

    parcel = jnp.stack(
        [
            states[0],
            jnp.where(second, velocity[1], diffusivity),
            jnp.where(second, velocity[2], velocity[0]),
        ]
    )
    blocks = slab_blocks(parcel)
    other_blocks = [core_swapped(block) for block in blocks]
    halo = row_halo(blocks, reach)
    other_halo = core_swapped(halo)

    first, last = box.span(COARSE_REACH)
    end, starts, coeff = run(
        functools.partial(fine_body, box, COARSE_REACH, own_depth, len(blocks)),
        [
            (tiles, depth, last - first, LANES),
            (2, tiles, depth, height, LANES),
            (4, tiles, depth, height, LANES),
        ],
        [box.scratch(), box.scratch()],
        *blocks,
        halo,
        *other_blocks,
        other_halo,
    )
    params = run(
        functools.partial(prepare_body, box),
        [
            (4, tiles, half, height, LANES),
            (tiles, depth, height, LANES),
            (tiles, half, height, LANES),
        ],
        [box.scratch(half)],
        coeff,
    )
    params = [coeff, *params]
    joined, first_end = run(
        functools.partial(pair_body, box),
        [(tiles, depth, rows, LANES)] * 2,
        [box.scratch()] + coarse_scratch(box),
        end,
        core_swapped(end),
        starts,
        *params,
    )
    ends = jnp.where(second, joined, first_end)
    ends = jnp.concatenate([ends[i] for i in range(tiles)], axis=-1)
    base = lax.axis_index("slab") * own_depth
    result, leaving = lax.dynamic_slice_in_dim(ends, base, own_depth, 0)[None], joined
    for turn in range(1, windows // 2):
        arrived = next_pair(leaving, 2 * COARSE_REACH)
        out, leaving = run(
            functools.partial(last_body, box, own_depth, turn),
            [(1, own_depth, rows, columns), (tiles, depth, rows, LANES)],
            [box.scratch()] * 2 + coarse_scratch(box),
            first_end,
            joined,
            *arrived,
            starts,
            *params,
        )
        result = out if turn == 1 else jnp.where(place // 2 >= turn, out, result)
    return result


def solution(mesh):
    return jax.shard_map(
        per_device,
        mesh=mesh,
        in_specs=(
            P("tm", "slab", "coarse", None),
            P("slab", "coarse", None),
            P(None, "slab", "coarse", None),
        ),
        out_specs=P("tm", "slab", "coarse", None),
        check_vma=False,
    )
```

```python
import functools

import jax
import jax.numpy as jnp
from jax import lax
from jax.experimental import pallas as pl
from jax.experimental.pallas import tpu as pltpu
from jax.sharding import PartitionSpec as P

SECTIONS = 4
FINE_STEPS = 2
FINE_STEP = 1.0
RELAX = 0.8
INTERVAL = FINE_STEPS * FINE_STEP
LANES = 128
PAD = 8
COARSE_REACH = 6
FINE_REACH = SECTIONS * FINE_STEPS


def chebyshev_coefficients(sections):
    damping = 0.05
    centre_point = 1.0 + damping / (sections * sections)
    chebyshev = [1.0, centre_point]
    slopes = [0.0, 1.0]
    for degree in range(2, sections + 1):
        chebyshev.append(2.0 * centre_point * chebyshev[degree - 1] - chebyshev[degree - 2])
        slopes.append(
            2.0 * chebyshev[degree - 1]
            + 2.0 * centre_point * slopes[degree - 1]
            - slopes[degree - 2]
        )
    slope_ratio = chebyshev[sections] / slopes[sections]
    weights = [1.0 / entry for entry in chebyshev]
    scales = [0.0, 0.0]
    carries = [0.0, 0.0]
    tildes = [0.0, slope_ratio / centre_point]
    for degree in range(2, sections + 1):
        scales.append(2.0 * weights[degree] * centre_point / weights[degree - 1])
        carries.append(-weights[degree] / weights[degree - 2])
        tildes.append(2.0 * weights[degree] * slope_ratio / weights[degree - 1])
    return (scales, carries, tildes)


def round_up(value, unit):
    return -(-value // unit) * unit


class Box:
    def __init__(self, depth, rows, side, columns):
        self.depth, self.rows, self.side, self.columns = depth, rows, side, columns
        self.height = rows + 2 * side
        self.tiles = columns // LANES

    def scratch(self, depth=None):
        depth = self.depth if depth is None else depth
        return pltpu.VMEM(
            (self.tiles, depth + 4, self.height + 2 * PAD, LANES), jnp.float32
        )

    def span(self, margin):
        first = (self.side - margin) // 8 * 8
        last = round_up(self.side + self.rows + margin, 8)
        assert first >= 0 and last <= self.height
        return first, last


CHUNK = 16


def chunks(first, last):
    at = first
    while at < last:
        size = min(CHUNK, last - at)
        yield at, size
        at += size


def each_plane(count, body):
    if count <= 8:
        for plane in range(count):
            body(plane)
    else:
        lax.fori_loop(0, count, lambda plane, _: (body(plane), 0)[1], 0)


def lane_index(size):
    return lax.broadcasted_iota(jnp.int32, (size, LANES), 1)


def row_index(size):
    return lax.broadcasted_iota(jnp.int32, (size, LANES), 0)


def sideways(values, step):
    size = values[0].shape[0]
    lane = lane_index(size)
    back = [pltpu.roll(entry, LANES - step, 1) for entry in values]
    forth = [pltpu.roll(entry, step, 1) for entry in values]
    zero = jnp.zeros_like(values[0])
    count = len(values)
    after = [
        jnp.where(lane >= LANES - step, back[i + 1] if i + 1 < count else zero, back[i])
        for i in range(count)
    ]
    before = [
        jnp.where(lane < step, forth[i - 1] if i else zero, forth[i]) for i in range(count)
    ]
    return after, before


def operator(field, coeff, plane, at, size, step):
    tiles = field.shape[0]
    centre = [field[i, plane + 2, pl.ds(PAD + at, size), :] for i in range(tiles)]
    after, before = sideways(centre, step)
    result = []
    for i in range(tiles):
        deep_after = field[i, plane + 3, pl.ds(PAD + at, size), :]
        deep_before = field[i, plane + 1, pl.ds(PAD + at, size), :]
        row_after = field[i, plane + 2, pl.ds(PAD + at + step, size), :]
        row_before = field[i, plane + 2, pl.ds(PAD + at - step, size), :]
        c = [coeff[k, i, plane, pl.ds(at, size), :] for k in range(4)]
        total = (deep_after + deep_before) + (row_after + row_before) + (after[i] + before[i])
        spread = c[0] * (total - 6.0 * centre[i])
        drift = (
            c[1] * (deep_after - deep_before)
            + c[2] * (row_after - row_before)
            + c[3] * (after[i] - before[i])
        )
        result.append((spread, drift, centre[i]))
    return result


def clear(field):
    field[...] = jnp.zeros_like(field)


def gather_body(states, diffusivity, velocity, parcel, sem):
    core = lax.axis_index("tm") % 2
    start = pltpu.make_async_copy(states, parcel.at[pl.ds(0, 1)], sem.at[0])
    start.start()

    @pl.when(core == 0)
    def _():
        one = pltpu.make_async_copy(diffusivity, parcel.at[1], sem.at[1])
        two = pltpu.make_async_copy(velocity.at[0], parcel.at[2], sem.at[2])
        one.start()
        two.start()
        one.wait()
        two.wait()

    @pl.when(core == 1)
    def _():
        both = pltpu.make_async_copy(
            velocity.at[pl.ds(1, 2)], parcel.at[pl.ds(1, 2)], sem.at[1]
        )
        both.start()
        both.wait()

    start.wait()


def row_places(box, sizes):
    place, count = lax.axis_index("coarse"), lax.axis_size("coarse")
    odd = place % 2
    result = []
    gone = 0
    for step, size in enumerate(sizes, 1):
        below = pl.multiple_of(box.side - gone - size, 8)
        above = pl.multiple_of(box.side + box.rows + gone, 8)
        gone += size
        one = pl.multiple_of(jnp.where(odd == 1, below, above), 8)
        two = pl.multiple_of(jnp.where(odd == 1, above, below), 8)
        below_valid, above_valid = place >= step, place + step < count
        one_valid = jnp.where(odd == 1, below_valid, above_valid)
        two_valid = jnp.where(odd == 1, above_valid, below_valid)
        result.append(((one, one_valid), (two, two_valid)))
    return result


def fine_body(box, margin, own_depth, blocks, *refs):
    end, starts, coeff, one, two = refs[-5:]
    half = (len(refs) - 5) // 2
    each = half // blocks
    core = lax.axis_index("tm") % 2
    shift = lax.axis_index("slab") if blocks == 2 else 0
    places = row_places(box, [refs[at].shape[-2] for at in range(1, each, 2)])
    clear(one)
    clear(two)
    for side, rank in ((0, core), (1, 1 - core)):
        for block in range(blocks):
            pieces = refs[side * half + block * each : side * half + (block + 1) * each]
            base = (block + shift) % blocks * own_depth
            moves = [(pieces[0], box.side, None)]
            for step, pair in enumerate(places):
                for ref, (at, valid) in zip(pieces[1 + 2 * step : 3 + 2 * step], pair):
                    moves.append((ref, at, valid))
            for ref, at, valid in moves:
                size = ref.shape[-2]
                for plane in range(own_depth):
                    for i in range(box.tiles):
                        cols = slice(i * LANES, (i + 1) * LANES)
                        for array in range(3):
                            value = ref[array, plane, :, cols]
                            if valid is not None:
                                value = jnp.where(valid, value, 0.0)
                            if array == 0:
                                starts[rank, i, base + plane, pl.ds(at, size), :] = value
                                if side == 0:
                                    one[i, base + plane + 2, pl.ds(PAD + at, size), :] = value
                            else:
                                coeff[
                                    2 * rank + array - 1, i, base + plane, pl.ds(at, size), :
                                ] = value
    scales, carries, tildes = chebyshev_coefficients(SECTIONS)
    stage = 0
    current, other = one, two
    for repeat in range(FINE_STEPS):
        for degree in range(1, SECTIONS + 1):
            stage += 1
            first, last = box.span(margin + FINE_REACH - stage)

            def plane_body(plane, current=current, other=other, degree=degree):
                for at, size in chunks(first, last):
                    values = operator(current, coeff, plane, at, size, 1)
                    for i, (spread, drift, centre) in enumerate(values):
                        change = tildes[degree] * FINE_STEP * (spread - 0.5 * drift)
                        where = (i, plane + 2, pl.ds(PAD + at, size), slice(None))
                        if degree == 1:
                            other[where] = centre + change
                        else:
                            other[where] = (
                                scales[degree] * centre + carries[degree] * other[where] + change
                            )

            each_plane(box.depth, plane_body)
            current, other = other, current
    first, last = box.span(margin)
    end[...] = current[:, 2 : 2 + box.depth, PAD + first : PAD + last, :]


def pair_columns(value):
    lane = lane_index(value.shape[0])
    other = jnp.where(
        lane % 2 == 0, pltpu.roll(value, LANES - 1, 1), pltpu.roll(value, 1, 1)
    )
    return value + other


def pair_rows(field, i, plane, at, size):
    row = row_index(size)
    other = jnp.where(
        row % 2 == 0,
        field[i, plane + 2, pl.ds(PAD + at + 1, size), :],
        field[i, plane + 2, pl.ds(PAD + at - 1, size), :],
    )
    return field[i, plane + 2, pl.ds(PAD + at, size), :] + other


def prepare_body(box, coeff, coarse, weight, coarse_weight, work):
    clear(work)
    for k in range(4):

        def columns_body(plane, k=k):
            for at, size in chunks(0, box.height):
                for i in range(box.tiles):
                    low = coeff[k, i, 2 * plane, pl.ds(at, size), :]
                    high = coeff[k, i, 2 * plane + 1, pl.ds(at, size), :]
                    work[i, plane + 2, pl.ds(PAD + at, size), :] = pair_columns(low + high)
                    if k == 0:
                        weight[i, 2 * plane, pl.ds(at, size), :] = RELAX / (
                            1.0 + 6.0 * INTERVAL * low
                        )
                        weight[i, 2 * plane + 1, pl.ds(at, size), :] = RELAX / (
                            1.0 + 6.0 * INTERVAL * high
                        )

        each_plane(box.depth // 2, columns_body)

        def rows_body(plane, k=k):
            for at, size in chunks(0, box.height):
                for i in range(box.tiles):
                    mean = 0.125 * pair_rows(work, i, plane, at, size)
                    coarse[k, i, plane, pl.ds(at, size), :] = mean
                    if k == 0:
                        coarse_weight[i, plane, pl.ds(at, size), :] = RELAX / (
                            1.0 + 6.0 * INTERVAL * mean / 4.0
                        )

        each_plane(box.depth // 2, rows_body)


def coarse_step_body(box, margin, source, trial, pairs, guess, residual, params, finish):
    coeff, coarse, weight, coarse_weight = params
    half = box.depth // 2

    first, last = box.span(margin + 5)

    def smooth(plane):
        for at, size in chunks(first, last):
            values = operator(source, coeff, plane, at, size, 1)
            for i, (spread, drift, centre) in enumerate(values):
                change = INTERVAL * spread - (INTERVAL * 0.5) * drift
                trial[i, plane + 2, pl.ds(PAD + at, size), :] = (
                    centre + weight[i, plane, pl.ds(at, size), :] * change
                )

    each_plane(box.depth, smooth)

    first, last = box.span(margin + 4)

    def restrict(plane):
        for at, size in chunks(first, last):
            sums = [None] * box.tiles
            for half_plane in range(2):
                fine_plane = 2 * plane + half_plane
                values = operator(trial, coeff, fine_plane, at, size, 1)
                for i, (spread, drift, centre) in enumerate(values):
                    misfit = (
                        source[i, fine_plane + 2, pl.ds(PAD + at, size), :]
                        - centre
                        + (INTERVAL * spread - (INTERVAL * 0.5) * drift)
                    )
                    sums[i] = misfit if sums[i] is None else sums[i] + misfit
            for i in range(box.tiles):
                pairs[i, plane + 2, pl.ds(PAD + at, size), :] = pair_columns(sums[i])

    each_plane(half, restrict)

    def first_guess(plane):
        for at, size in chunks(first, last):
            for i in range(box.tiles):
                mean = 0.125 * pair_rows(pairs, i, plane, at, size)
                residual[i, plane + 2, pl.ds(PAD + at, size), :] = mean
                guess[i, plane + 2, pl.ds(PAD + at, size), :] = (
                    coarse_weight[i, plane, pl.ds(at, size), :] * mean
                )

    each_plane(half, first_guess)

    first, last = box.span(margin + 2)

    def correct(plane):
        for at, size in chunks(first, last):
            values = operator(guess, coarse, plane, at, size, 2)
            for i, (spread, drift, centre) in enumerate(values):
                change = (INTERVAL / 4.0) * (spread - drift)
                rest = residual[i, plane + 2, pl.ds(PAD + at, size), :] - centre + change
                fix = centre + coarse_weight[i, plane, pl.ds(at, size), :] * rest
                for half_plane in range(2):
                    where = (i, 2 * plane + half_plane + 2, pl.ds(PAD + at, size), slice(None))
                    trial[where] = trial[where] + fix

    each_plane(half, correct)

    first, last = box.span(margin)

    def smooth_again(plane):
        for at, size in chunks(first, last):
            values = operator(trial, coeff, plane, at, size, 1)
            for i, (spread, drift, centre) in enumerate(values):
                misfit = (
                    source[i, plane + 2, pl.ds(PAD + at, size), :]
                    - centre
                    + (INTERVAL * spread - (INTERVAL * 0.5) * drift)
                )
                finish(
                    plane, i, at, size, centre + weight[i, plane, pl.ds(at, size), :] * misfit
                )

    each_plane(box.depth, smooth_again)


def coarse_scratch(box):
    half = box.depth // 2
    return [box.scratch(), box.scratch(half), box.scratch(half), box.scratch(half)]


def pair_body(box, own_end, other_end, starts, *rest):
    params, out, first_out, leaving = rest[:4], rest[4], rest[5], rest[6]
    source, trial, pairs, guess, residual = rest[7:]
    core = lax.axis_index("tm") % 2
    clear(source)
    clear(trial)
    clear(pairs)
    clear(guess)
    first, last = box.span(COARSE_REACH)

    def put(first_end, second_end):
        source[:, 2 : 2 + box.depth, PAD + first : PAD + last, :] = (
            first_end[...] - starts[1, :, :, first:last, :]
        )
        inner = slice(box.side - first, box.side - first + box.rows)
        out[...] = second_end[:, :, inner, :]
        first_out[...] = first_end[:, :, inner, :]

    @pl.when(core == 0)
    def _():
        put(own_end, other_end)

    @pl.when(core == 1)
    def _():
        put(other_end, own_end)

    def finish(plane, i, at, size, value):
        where = (i, plane, pl.ds(at - box.side, size), slice(None))
        out[where] = value + out[where]

    coarse_step_body(box, 0, source, trial, pairs, guess, residual, params, finish)
    half = box.depth // 2
    leaving[...] = out[:, pl.ds(core * half, half)]


def last_body(box, own_depth, turn, pieces, first_end, joined, *rest):
    arrived, rest = rest[:pieces], rest[pieces:]
    starts, params, result, leaving = rest[0], rest[1:5], rest[5], rest[6]
    source, second, trial, pairs, guess, residual, total = rest[7:]
    place = lax.axis_index("tm")
    core = place % 2
    active = place // 2 == turn
    clear(source)
    clear(second)
    clear(trial)
    clear(pairs)
    clear(guess)
    side, rows = box.side, box.rows
    half = box.depth // 2
    each = pieces // 2
    places = row_places(box, [arrived[at].shape[-2] for at in range(1, each, 2)])

    @pl.when(active)
    def _():
        for part, rank in ((0, core), (1, 1 - core)):
            moves = [(arrived[part * each], side, None)]
            for step, pair in enumerate(places):
                at = part * each + 1 + 2 * step
                for ref, (where, valid) in zip(arrived[at : at + 2], pair):
                    moves.append((ref, where, valid))
            base = rank * half
            for ref, at, valid in moves:
                size = ref.shape[-2]
                for plane in range(half):
                    for i in range(box.tiles):
                        value = ref[i, plane]
                        if valid is not None:
                            value = jnp.where(valid, value, 0.0)
                        source[i, base + plane + 2, pl.ds(PAD + at, size), :] = (
                            value - starts[0, i, base + plane, pl.ds(at, size), :]
                        )

    def finish_once(plane, i, at, size, value):
        second[i, plane + 2, pl.ds(PAD + at, size), :] = value

    coarse_step_body(
        box, COARSE_REACH, source, trial, pairs, guess, residual, params, finish_once
    )

    def finish_twice(plane, i, at, size, value):
        where = (i, plane, pl.ds(at - box.side, size), slice(None))
        total[where] = value + joined[where]

    coarse_step_body(box, 0, second, trial, pairs, guess, residual, params, finish_twice)
    base = lax.axis_index("slab") * own_depth

    @pl.when(core == 0)
    def _():
        for i in range(box.tiles):
            result[0, :, :, i * LANES : (i + 1) * LANES] = (
                first_end[i, pl.ds(base, own_depth)]
                + second[i, pl.ds(base + 2, own_depth), PAD + side : PAD + side + rows, :]
            )

    @pl.when(core == 1)
    def _():
        for i in range(box.tiles):
            result[0, :, :, i * LANES : (i + 1) * LANES] = total[i, pl.ds(base, own_depth)]

    leaving[...] = total[:, pl.ds(core * half, half)]


def run(body, outs, scratch, *args, space=pltpu.VMEM):
    return pl.pallas_call(
        body,
        out_shape=[jax.ShapeDtypeStruct(shape, jnp.float32) for shape in outs],
        in_specs=[pl.BlockSpec(memory_space=space)] * len(args),
        out_specs=[pl.BlockSpec(memory_space=pltpu.VMEM)] * len(outs),
        scratch_shapes=scratch,
        compiler_params=pltpu.CompilerParams(vmem_limit_bytes=20 * 1024 * 1024),
    )(*args)


def slab_blocks(block):
    count = lax.axis_size("slab")
    if count == 1:
        return [block]
    if count == 2:
        return [block, lax.ppermute(block, "slab", [(0, 1), (1, 0)])]
    gathered = lax.all_gather(block, "slab", axis=0)
    return [gathered[i] for i in range(count)]


def row_swaps(hop, away):
    windows, count = lax.axis_size("tm"), lax.axis_size("coarse")
    rounds = []
    for first in (0, 1):
        pairs = []
        for place in range(count):
            other = place + 1 if place % 2 == first else place - 1
            for t in range(windows):
                inside = 0 <= other < count
                target = (hop(t), other) if inside else (away(t), place)
                pairs.append((t * count + place, target[0] * count + target[1]))
        rounds.append(pairs)
    return rounds


def row_pieces(block, width, rounds):
    rows = block.shape[-2]
    axis = block.ndim - 2
    both = ("tm", "coarse")
    odd = lax.axis_index("coarse") % 2 == 1
    pieces = []
    up, down = block, block
    left = width
    while left > 0:
        size = min(rows, left)
        if size == rows and up is down:
            send_one = send_two = block
        else:
            high = lax.slice_in_dim(up, up.shape[axis] - size, None, axis=axis)
            low = lax.slice_in_dim(down, 0, size, axis=axis)
            send_one, send_two = jnp.where(odd, low, high), jnp.where(odd, high, low)
        got_one = lax.ppermute(send_one, both, rounds[0])
        got_two = lax.ppermute(send_two, both, rounds[1])
        pieces += [got_one, got_two]
        left -= size
        if left > 0:
            up, down = jnp.where(odd, got_one, got_two), jnp.where(odd, got_two, got_one)
    return pieces


def core_swapped(block):
    count = lax.axis_size("tm")
    assert count % 2 == 0
    return lax.ppermute(block, "tm", [(i, i ^ 1) for i in range(count)])


def per_device(states, diffusivity, velocity):
    windows = lax.axis_size("tm")
    place = lax.axis_index("tm")
    own_depth, rows, columns = diffusivity.shape
    side = round_up(FINE_REACH + COARSE_REACH, 8)
    depth = own_depth * lax.axis_size("slab")
    box = Box(depth, rows, side, columns)
    tiles, height, half = box.tiles, box.height, depth // 2

    (parcel,) = run(
        gather_body,
        [(3, own_depth, rows, columns)],
        [pltpu.SemaphoreType.DMA((3,))],
        states,
        diffusivity,
        velocity,
        space=pl.ANY,
    )
    rounds = row_swaps(lambda t: t, lambda t: t ^ 1)
    blocks = slab_blocks(parcel)
    own_pieces = []
    for block in blocks:
        own_pieces += [block, *row_pieces(block, side, rounds)]
    other_pieces = [core_swapped(piece) for piece in own_pieces]

    first, last = box.span(COARSE_REACH)
    end, starts, coeff = run(
        functools.partial(fine_body, box, COARSE_REACH, own_depth, len(blocks)),
        [
            (tiles, depth, last - first, LANES),
            (2, tiles, depth, height, LANES),
            (4, tiles, depth, height, LANES),
        ],
        [box.scratch(), box.scratch()],
        *own_pieces,
        *other_pieces,
    )
    params = run(
        functools.partial(prepare_body, box),
        [
            (4, tiles, half, height, LANES),
            (tiles, depth, height, LANES),
            (tiles, half, height, LANES),
        ],
        [box.scratch(half)],
        coeff,
    )
    params = [coeff, *params]
    joined, first_end, leaving = run(
        functools.partial(pair_body, box),
        [(tiles, depth, rows, LANES)] * 2 + [(tiles, half, rows, LANES)],
        [box.scratch()] + coarse_scratch(box),
        end,
        core_swapped(end),
        starts,
        *params,
    )
    ends = jnp.where(place % 2 == 1, joined, first_end)
    ends = jnp.concatenate([ends[i] for i in range(tiles)], axis=-1)
    base = lax.axis_index("slab") * own_depth
    result = lax.dynamic_slice_in_dim(ends, base, own_depth, 0)[None]
    hop = lambda t: (t + 2) % windows
    rounds = row_swaps(hop, hop)
    for turn in range(1, windows // 2):
        centre = lax.ppermute(leaving, "tm", [(t, hop(t)) for t in range(windows)])
        if rows >= 2 * COARSE_REACH:
            arrived = [centre, *row_pieces(leaving, min(rows, side), rounds)]
        else:
            near = row_swaps(lambda t: t, lambda t: t ^ 1)
            arrived = [centre, *row_pieces(centre, side, near)]
        arrived += [core_swapped(piece) for piece in arrived]
        out, leaving = run(
            functools.partial(last_body, box, own_depth, turn, len(arrived)),
            [(1, own_depth, rows, columns), (tiles, half, rows, LANES)],
            [box.scratch()] * 2
            + coarse_scratch(box)
            + [pltpu.VMEM((tiles, depth, rows, LANES), jnp.float32)],
            first_end,
            joined,
            *arrived,
            starts,
            *params,
        )
        result = out if turn == 1 else jnp.where(place // 2 >= turn, out, result)
    return result


def solution(mesh):
    return jax.shard_map(
        per_device,
        mesh=mesh,
        in_specs=(
            P("tm", "slab", "coarse", None),
            P("slab", "coarse", None),
            P(None, "slab", "coarse", None),
        ),
        out_specs=P("tm", "slab", "coarse", None),
        check_vma=False,
    )
```

```python
import functools

import jax
import jax.numpy as jnp
from jax import lax
from jax.experimental import pallas as pl
from jax.experimental.pallas import tpu as pltpu
from jax.sharding import PartitionSpec as P

SECTIONS = 4
FINE_STEPS = 2
FINE_STEP = 1.0
RELAX = 0.8
INTERVAL = FINE_STEPS * FINE_STEP
LANES = 128
PAD = 8
COARSE_REACH = 6
FINE_REACH = SECTIONS * FINE_STEPS


def chebyshev_coefficients(sections):
    damping = 0.05
    centre_point = 1.0 + damping / (sections * sections)
    chebyshev = [1.0, centre_point]
    slopes = [0.0, 1.0]
    for degree in range(2, sections + 1):
        chebyshev.append(2.0 * centre_point * chebyshev[degree - 1] - chebyshev[degree - 2])
        slopes.append(
            2.0 * chebyshev[degree - 1]
            + 2.0 * centre_point * slopes[degree - 1]
            - slopes[degree - 2]
        )
    slope_ratio = chebyshev[sections] / slopes[sections]
    weights = [1.0 / entry for entry in chebyshev]
    scales = [0.0, 0.0]
    carries = [0.0, 0.0]
    tildes = [0.0, slope_ratio / centre_point]
    for degree in range(2, sections + 1):
        scales.append(2.0 * weights[degree] * centre_point / weights[degree - 1])
        carries.append(-weights[degree] / weights[degree - 2])
        tildes.append(2.0 * weights[degree] * slope_ratio / weights[degree - 1])
    return (scales, carries, tildes)


def round_up(value, unit):
    return -(-value // unit) * unit


class Box:
    def __init__(self, depth, rows, side, columns):
        self.depth, self.rows, self.side, self.columns = depth, rows, side, columns
        self.height = rows + 2 * side
        self.tiles = columns // LANES

    def scratch(self, depth=None):
        depth = self.depth if depth is None else depth
        return pltpu.VMEM(
            (self.tiles, depth + 4, self.height + 2 * PAD, LANES), jnp.float32
        )

    def span(self, margin):
        first = (self.side - margin) // 8 * 8
        last = round_up(self.side + self.rows + margin, 8)
        assert first >= 0 and last <= self.height
        return first, last


CHUNK = 16


def chunks(first, last):
    at = first
    while at < last:
        size = min(CHUNK, last - at)
        yield at, size
        at += size


def each_plane(count, body):
    if count <= 8:
        for plane in range(count):
            body(plane)
    else:
        lax.fori_loop(0, count, lambda plane, _: (body(plane), 0)[1], 0)


def lane_index(size):
    return lax.broadcasted_iota(jnp.int32, (size, LANES), 1)


def row_index(size):
    return lax.broadcasted_iota(jnp.int32, (size, LANES), 0)


def sideways(values, step):
    size = values[0].shape[0]
    lane = lane_index(size)
    back = [pltpu.roll(entry, LANES - step, 1) for entry in values]
    forth = [pltpu.roll(entry, step, 1) for entry in values]
    zero = jnp.zeros_like(values[0])
    count = len(values)
    after = [
        jnp.where(lane >= LANES - step, back[i + 1] if i + 1 < count else zero, back[i])
        for i in range(count)
    ]
    before = [
        jnp.where(lane < step, forth[i - 1] if i else zero, forth[i]) for i in range(count)
    ]
    return after, before


def operator(field, coeff, plane, at, size, step):
    tiles = field.shape[0]
    centre = [field[i, plane + 2, pl.ds(PAD + at, size), :] for i in range(tiles)]
    after, before = sideways(centre, step)
    result = []
    for i in range(tiles):
        deep_after = field[i, plane + 3, pl.ds(PAD + at, size), :]
        deep_before = field[i, plane + 1, pl.ds(PAD + at, size), :]
        row_after = field[i, plane + 2, pl.ds(PAD + at + step, size), :]
        row_before = field[i, plane + 2, pl.ds(PAD + at - step, size), :]
        c = [coeff[k, i, plane, pl.ds(at, size), :] for k in range(4)]
        total = (deep_after + deep_before) + (row_after + row_before) + (after[i] + before[i])
        spread = c[0] * (total - 6.0 * centre[i])
        drift = (
            c[1] * (deep_after - deep_before)
            + c[2] * (row_after - row_before)
            + c[3] * (after[i] - before[i])
        )
        result.append((spread, drift, centre[i]))
    return result


def clear(field):
    field[...] = jnp.zeros_like(field)


def row_places(box, sizes):
    place, count = lax.axis_index("coarse"), lax.axis_size("coarse")
    odd = place % 2
    result = []
    gone = 0
    for step, size in enumerate(sizes, 1):
        below = pl.multiple_of(box.side - gone - size, 8)
        above = pl.multiple_of(box.side + box.rows + gone, 8)
        gone += size
        one = pl.multiple_of(jnp.where(odd == 1, below, above), 8)
        two = pl.multiple_of(jnp.where(odd == 1, above, below), 8)
        below_valid, above_valid = place >= step, place + step < count
        one_valid = jnp.where(odd == 1, below_valid, above_valid)
        two_valid = jnp.where(odd == 1, above_valid, below_valid)
        result.append(((one, one_valid), (two, two_valid)))
    return result


def fine_body(box, margin, own_depth, blocks, *refs):
    end, starts, coeff, one, two = refs[-5:]
    half = (len(refs) - 5) // 2
    each = half // blocks
    core = lax.axis_index("tm") % 2
    shift = lax.axis_index("slab") if blocks == 2 else 0
    places = row_places(box, [refs[at].shape[-2] for at in range(1, each, 2)])
    clear(one)
    clear(two)
    for side, rank in ((0, core), (1, 1 - core)):
        slots = ((2 - 2 * rank, None), (rank, 1 + rank), (1 + rank, 3 * rank))
        for block in range(blocks):
            pieces = refs[side * half + block * each : side * half + (block + 1) * each]
            base = (block + shift) % blocks * own_depth
            moves = [(pieces[0], box.side, None)]
            for step, pair in enumerate(places):
                for ref, (at, valid) in zip(pieces[1 + 2 * step : 3 + 2 * step], pair):
                    moves.append((ref, at, valid))
            for ref, at, valid in moves:
                size = ref.shape[-2]
                for plane in range(own_depth):
                    for i in range(box.tiles):
                        cols = slice(i * LANES, (i + 1) * LANES)
                        for array, (slot, kind) in enumerate(slots):
                            value = ref[slot, plane, :, cols]
                            if valid is not None:
                                value = jnp.where(valid, value, 0.0)
                            if array == 0:
                                starts[rank, i, base + plane, pl.ds(at, size), :] = value
                                if side == 0:
                                    one[i, base + plane + 2, pl.ds(PAD + at, size), :] = value
                            else:
                                coeff[kind, i, base + plane, pl.ds(at, size), :] = value
    scales, carries, tildes = chebyshev_coefficients(SECTIONS)
    stage = 0
    current, other = one, two
    for repeat in range(FINE_STEPS):
        for degree in range(1, SECTIONS + 1):
            stage += 1
            first, last = box.span(margin + FINE_REACH - stage)

            def plane_body(plane, current=current, other=other, degree=degree):
                for at, size in chunks(first, last):
                    values = operator(current, coeff, plane, at, size, 1)
                    for i, (spread, drift, centre) in enumerate(values):
                        change = tildes[degree] * FINE_STEP * (spread - 0.5 * drift)
                        where = (i, plane + 2, pl.ds(PAD + at, size), slice(None))
                        if degree == 1:
                            other[where] = centre + change
                        else:
                            other[where] = (
                                scales[degree] * centre + carries[degree] * other[where] + change
                            )

            each_plane(box.depth, plane_body)
            current, other = other, current
    first, last = box.span(margin)
    end[...] = current[:, 2 : 2 + box.depth, PAD + first : PAD + last, :]


def pair_columns(value):
    lane = lane_index(value.shape[0])
    other = jnp.where(
        lane % 2 == 0, pltpu.roll(value, LANES - 1, 1), pltpu.roll(value, 1, 1)
    )
    return value + other


def pair_rows(field, i, plane, at, size):
    row = row_index(size)
    other = jnp.where(
        row % 2 == 0,
        field[i, plane + 2, pl.ds(PAD + at + 1, size), :],
        field[i, plane + 2, pl.ds(PAD + at - 1, size), :],
    )
    return field[i, plane + 2, pl.ds(PAD + at, size), :] + other


def prepare_body(box, coeff, coarse, weight, coarse_weight, work):
    clear(work)
    for k in range(4):

        def columns_body(plane, k=k):
            for at, size in chunks(0, box.height):
                for i in range(box.tiles):
                    low = coeff[k, i, 2 * plane, pl.ds(at, size), :]
                    high = coeff[k, i, 2 * plane + 1, pl.ds(at, size), :]
                    work[i, plane + 2, pl.ds(PAD + at, size), :] = pair_columns(low + high)
                    if k == 0:
                        weight[i, 2 * plane, pl.ds(at, size), :] = RELAX / (
                            1.0 + 6.0 * INTERVAL * low
                        )
                        weight[i, 2 * plane + 1, pl.ds(at, size), :] = RELAX / (
                            1.0 + 6.0 * INTERVAL * high
                        )

        each_plane(box.depth // 2, columns_body)

        def rows_body(plane, k=k):
            for at, size in chunks(0, box.height):
                for i in range(box.tiles):
                    mean = 0.125 * pair_rows(work, i, plane, at, size)
                    coarse[k, i, plane, pl.ds(at, size), :] = mean
                    if k == 0:
                        coarse_weight[i, plane, pl.ds(at, size), :] = RELAX / (
                            1.0 + 6.0 * INTERVAL * mean / 4.0
                        )

        each_plane(box.depth // 2, rows_body)


def coarse_step_body(box, margin, source, trial, pairs, guess, residual, params, finish):
    coeff, coarse, weight, coarse_weight = params
    half = box.depth // 2

    first, last = box.span(margin + 5)

    def smooth(plane):
        for at, size in chunks(first, last):
            values = operator(source, coeff, plane, at, size, 1)
            for i, (spread, drift, centre) in enumerate(values):
                change = INTERVAL * spread - (INTERVAL * 0.5) * drift
                trial[i, plane + 2, pl.ds(PAD + at, size), :] = (
                    centre + weight[i, plane, pl.ds(at, size), :] * change
                )

    each_plane(box.depth, smooth)

    first, last = box.span(margin + 4)

    def restrict(plane):
        for at, size in chunks(first, last):
            sums = [None] * box.tiles
            for half_plane in range(2):
                fine_plane = 2 * plane + half_plane
                values = operator(trial, coeff, fine_plane, at, size, 1)
                for i, (spread, drift, centre) in enumerate(values):
                    misfit = (
                        source[i, fine_plane + 2, pl.ds(PAD + at, size), :]
                        - centre
                        + (INTERVAL * spread - (INTERVAL * 0.5) * drift)
                    )
                    sums[i] = misfit if sums[i] is None else sums[i] + misfit
            for i in range(box.tiles):
                pairs[i, plane + 2, pl.ds(PAD + at, size), :] = pair_columns(sums[i])

    each_plane(half, restrict)

    def first_guess(plane):
        for at, size in chunks(first, last):
            for i in range(box.tiles):
                mean = 0.125 * pair_rows(pairs, i, plane, at, size)
                residual[i, plane + 2, pl.ds(PAD + at, size), :] = mean
                guess[i, plane + 2, pl.ds(PAD + at, size), :] = (
                    coarse_weight[i, plane, pl.ds(at, size), :] * mean
                )

    each_plane(half, first_guess)

    first, last = box.span(margin + 2)

    def correct(plane):
        for at, size in chunks(first, last):
            values = operator(guess, coarse, plane, at, size, 2)
            for i, (spread, drift, centre) in enumerate(values):
                change = (INTERVAL / 4.0) * (spread - drift)
                rest = residual[i, plane + 2, pl.ds(PAD + at, size), :] - centre + change
                fix = centre + coarse_weight[i, plane, pl.ds(at, size), :] * rest
                for half_plane in range(2):
                    where = (i, 2 * plane + half_plane + 2, pl.ds(PAD + at, size), slice(None))
                    trial[where] = trial[where] + fix

    each_plane(half, correct)

    first, last = box.span(margin)

    def smooth_again(plane):
        for at, size in chunks(first, last):
            values = operator(trial, coeff, plane, at, size, 1)
            for i, (spread, drift, centre) in enumerate(values):
                misfit = (
                    source[i, plane + 2, pl.ds(PAD + at, size), :]
                    - centre
                    + (INTERVAL * spread - (INTERVAL * 0.5) * drift)
                )
                finish(
                    plane, i, at, size, centre + weight[i, plane, pl.ds(at, size), :] * misfit
                )

    each_plane(box.depth, smooth_again)


def coarse_scratch(box):
    half = box.depth // 2
    return [box.scratch(), box.scratch(half), box.scratch(half), box.scratch(half)]


def pair_body(box, own_end, other_end, starts, *rest):
    params, out, first_out, leaving = rest[:4], rest[4], rest[5], rest[6]
    source, trial, pairs, guess, residual = rest[7:]
    core = lax.axis_index("tm") % 2
    clear(source)
    clear(trial)
    clear(pairs)
    clear(guess)
    first, last = box.span(COARSE_REACH)

    def put(first_end, second_end):
        source[:, 2 : 2 + box.depth, PAD + first : PAD + last, :] = (
            first_end[...] - starts[1, :, :, first:last, :]
        )
        inner = slice(box.side - first, box.side - first + box.rows)
        out[...] = second_end[:, :, inner, :]
        first_out[...] = first_end[:, :, inner, :]

    @pl.when(core == 0)
    def _():
        put(own_end, other_end)

    @pl.when(core == 1)
    def _():
        put(other_end, own_end)

    def finish(plane, i, at, size, value):
        where = (i, plane, pl.ds(at - box.side, size), slice(None))
        out[where] = value + out[where]

    coarse_step_body(box, 0, source, trial, pairs, guess, residual, params, finish)
    half = box.depth // 2
    leaving[...] = out[:, pl.ds(core * half, half)]


def last_body(box, own_depth, turn, pieces, first_end, joined, *rest):
    arrived, rest = rest[:pieces], rest[pieces:]
    starts, params, result, leaving = rest[0], rest[1:5], rest[5], rest[6]
    source, second, trial, pairs, guess, residual, total = rest[7:]
    place = lax.axis_index("tm")
    core = place % 2
    active = place // 2 == turn
    clear(source)
    clear(second)
    clear(trial)
    clear(pairs)
    clear(guess)
    side, rows = box.side, box.rows
    half = box.depth // 2
    each = pieces // 2
    places = row_places(box, [arrived[at].shape[-2] for at in range(1, each, 2)])

    @pl.when(active)
    def _():
        for part, rank in ((0, core), (1, 1 - core)):
            moves = [(arrived[part * each], side, None)]
            for step, pair in enumerate(places):
                at = part * each + 1 + 2 * step
                for ref, (where, valid) in zip(arrived[at : at + 2], pair):
                    moves.append((ref, where, valid))
            base = rank * half
            for ref, at, valid in moves:
                size = ref.shape[-2]
                for plane in range(half):
                    for i in range(box.tiles):
                        value = ref[i, plane]
                        if valid is not None:
                            value = jnp.where(valid, value, 0.0)
                        source[i, base + plane + 2, pl.ds(PAD + at, size), :] = (
                            value - starts[0, i, base + plane, pl.ds(at, size), :]
                        )

    def finish_once(plane, i, at, size, value):
        second[i, plane + 2, pl.ds(PAD + at, size), :] = value

    coarse_step_body(
        box, COARSE_REACH, source, trial, pairs, guess, residual, params, finish_once
    )

    def finish_twice(plane, i, at, size, value):
        where = (i, plane, pl.ds(at - box.side, size), slice(None))
        total[where] = value + joined[where]

    coarse_step_body(box, 0, second, trial, pairs, guess, residual, params, finish_twice)
    base = lax.axis_index("slab") * own_depth

    @pl.when(core == 0)
    def _():
        for i in range(box.tiles):
            result[0, :, :, i * LANES : (i + 1) * LANES] = (
                first_end[i, pl.ds(base, own_depth)]
                + second[i, pl.ds(base + 2, own_depth), PAD + side : PAD + side + rows, :]
            )

    @pl.when(core == 1)
    def _():
        for i in range(box.tiles):
            result[0, :, :, i * LANES : (i + 1) * LANES] = total[i, pl.ds(base, own_depth)]

    leaving[...] = total[:, pl.ds(core * half, half)]


def run(body, outs, scratch, *args):
    return pl.pallas_call(
        body,
        out_shape=[jax.ShapeDtypeStruct(shape, jnp.float32) for shape in outs],
        in_specs=[pl.BlockSpec(memory_space=pltpu.VMEM)] * len(args),
        out_specs=[pl.BlockSpec(memory_space=pltpu.VMEM)] * len(outs),
        scratch_shapes=scratch,
        compiler_params=pltpu.CompilerParams(vmem_limit_bytes=20 * 1024 * 1024),
    )(*args)


def slab_blocks(block):
    count = lax.axis_size("slab")
    if count == 1:
        return [block]
    if count == 2:
        return [block, lax.ppermute(block, "slab", [(0, 1), (1, 0)])]
    gathered = lax.all_gather(block, "slab", axis=0)
    return [gathered[i] for i in range(count)]


def row_swaps(hop, away):
    windows, count = lax.axis_size("tm"), lax.axis_size("coarse")
    rounds = []
    for first in (0, 1):
        pairs = []
        for place in range(count):
            other = place + 1 if place % 2 == first else place - 1
            for t in range(windows):
                inside = 0 <= other < count
                target = (hop(t), other) if inside else (away(t), place)
                pairs.append((t * count + place, target[0] * count + target[1]))
        rounds.append(pairs)
    return rounds


def row_pieces(block, width, rounds):
    rows = block.shape[-2]
    axis = block.ndim - 2
    both = ("tm", "coarse")
    odd = lax.axis_index("coarse") % 2 == 1
    pieces = []
    up, down = block, block
    left = width
    while left > 0:
        size = min(rows, left)
        if size == rows and up is down:
            send_one = send_two = block
        else:
            high = lax.slice_in_dim(up, up.shape[axis] - size, None, axis=axis)
            low = lax.slice_in_dim(down, 0, size, axis=axis)
            send_one, send_two = jnp.where(odd, low, high), jnp.where(odd, high, low)
        got_one = lax.ppermute(send_one, both, rounds[0])
        got_two = lax.ppermute(send_two, both, rounds[1])
        pieces += [got_one, got_two]
        left -= size
        if left > 0:
            up, down = jnp.where(odd, got_one, got_two), jnp.where(odd, got_two, got_one)
    return pieces


def core_swapped(block):
    count = lax.axis_size("tm")
    assert count % 2 == 0
    return lax.ppermute(block, "tm", [(i, i ^ 1) for i in range(count)])


def per_device(states, diffusivity, velocity):
    windows = lax.axis_size("tm")
    place = lax.axis_index("tm")
    own_depth, rows, columns = diffusivity.shape
    side = round_up(FINE_REACH + COARSE_REACH, 8)
    depth = own_depth * lax.axis_size("slab")
    box = Box(depth, rows, side, columns)
    tiles, height, half = box.tiles, box.height, depth // 2

    second = place % 2 == 1
    slot = lax.broadcasted_iota(jnp.int32, (3, 1, 1, 1), 0)
    parcel = jnp.where(
        (slot == 0) != second, velocity, jnp.where(slot == 1, diffusivity[None], states)
    )
    rounds = row_swaps(lambda t: t, lambda t: t ^ 1)
    blocks = slab_blocks(parcel)
    own_pieces = []
    for block in blocks:
        own_pieces += [block, *row_pieces(block, side, rounds)]
    other_pieces = [core_swapped(piece) for piece in own_pieces]

    first, last = box.span(COARSE_REACH)
    end, starts, coeff = run(
        functools.partial(fine_body, box, COARSE_REACH, own_depth, len(blocks)),
        [
            (tiles, depth, last - first, LANES),
            (2, tiles, depth, height, LANES),
            (4, tiles, depth, height, LANES),
        ],
        [box.scratch(), box.scratch()],
        *own_pieces,
        *other_pieces,
    )
    params = run(
        functools.partial(prepare_body, box),
        [
            (4, tiles, half, height, LANES),
            (tiles, depth, height, LANES),
            (tiles, half, height, LANES),
        ],
        [box.scratch(half)],
        coeff,
    )
    params = [coeff, *params]
    joined, first_end, leaving = run(
        functools.partial(pair_body, box),
        [(tiles, depth, rows, LANES)] * 2 + [(tiles, half, rows, LANES)],
        [box.scratch()] + coarse_scratch(box),
        end,
        core_swapped(end),
        starts,
        *params,
    )
    ends = jnp.where(place % 2 == 1, joined, first_end)
    ends = jnp.concatenate([ends[i] for i in range(tiles)], axis=-1)
    base = lax.axis_index("slab") * own_depth
    result = lax.dynamic_slice_in_dim(ends, base, own_depth, 0)[None]
    hop = lambda t: (t + 2) % windows
    rounds = row_swaps(hop, hop)
    for turn in range(1, windows // 2):
        centre = lax.ppermute(leaving, "tm", [(t, hop(t)) for t in range(windows)])
        if rows >= 2 * COARSE_REACH:
            arrived = [centre, *row_pieces(leaving, min(rows, side), rounds)]
        else:
            near = row_swaps(lambda t: t, lambda t: t ^ 1)
            arrived = [centre, *row_pieces(centre, side, near)]
        arrived += [core_swapped(piece) for piece in arrived]
        out, leaving = run(
            functools.partial(last_body, box, own_depth, turn, len(arrived)),
            [(1, own_depth, rows, columns), (tiles, half, rows, LANES)],
            [box.scratch()] * 2
            + coarse_scratch(box)
            + [pltpu.VMEM((tiles, depth, rows, LANES), jnp.float32)],
            first_end,
            joined,
            *arrived,
            starts,
            *params,
        )
        result = out if turn == 1 else jnp.where(place // 2 >= turn, out, result)
    return result


def solution(mesh):
    return jax.shard_map(
        per_device,
        mesh=mesh,
        in_specs=(
            P("tm", "slab", "coarse", None),
            P("slab", "coarse", None),
            P(None, "slab", "coarse", None),
        ),
        out_specs=P("tm", "slab", "coarse", None),
        check_vma=False,
    )
```

```python
import functools

import jax
import jax.numpy as jnp
from jax import lax
from jax.experimental import pallas as pl
from jax.experimental.pallas import tpu as pltpu
from jax.sharding import PartitionSpec as P

SECTIONS = 4
FINE_STEPS = 2
FINE_STEP = 1.0
RELAX = 0.8
INTERVAL = FINE_STEPS * FINE_STEP
LANES = 128
PAD = 8
COARSE_REACH = 6
FINE_REACH = SECTIONS * FINE_STEPS


def chebyshev_coefficients(sections):
    damping = 0.05
    centre_point = 1.0 + damping / (sections * sections)
    chebyshev = [1.0, centre_point]
    slopes = [0.0, 1.0]
    for degree in range(2, sections + 1):
        chebyshev.append(2.0 * centre_point * chebyshev[degree - 1] - chebyshev[degree - 2])
        slopes.append(
            2.0 * chebyshev[degree - 1]
            + 2.0 * centre_point * slopes[degree - 1]
            - slopes[degree - 2]
        )
    slope_ratio = chebyshev[sections] / slopes[sections]
    weights = [1.0 / entry for entry in chebyshev]
    scales = [0.0, 0.0]
    carries = [0.0, 0.0]
    tildes = [0.0, slope_ratio / centre_point]
    for degree in range(2, sections + 1):
        scales.append(2.0 * weights[degree] * centre_point / weights[degree - 1])
        carries.append(-weights[degree] / weights[degree - 2])
        tildes.append(2.0 * weights[degree] * slope_ratio / weights[degree - 1])
    return (scales, carries, tildes)


def round_up(value, unit):
    return -(-value // unit) * unit


class Box:
    def __init__(self, depth, rows, side, columns):
        self.depth, self.rows, self.side, self.columns = depth, rows, side, columns
        self.height = rows + 2 * side
        self.tiles = columns // LANES

    def scratch(self, depth=None):
        depth = self.depth if depth is None else depth
        return pltpu.VMEM(
            (self.tiles, depth + 4, self.height + 2 * PAD, LANES), jnp.float32
        )

    def span(self, margin):
        first = (self.side - margin) // 8 * 8
        last = round_up(self.side + self.rows + margin, 8)
        assert first >= 0 and last <= self.height
        return first, last


CHUNK = 16
AFTER_DEPTH, BEFORE_DEPTH, AFTER_ROW, BEFORE_ROW, AFTER_COLUMN, BEFORE_COLUMN, CENTRE = range(7)


def chunks(first, last):
    at = first
    while at < last:
        size = min(CHUNK, last - at)
        yield at, size
        at += size


def sweep(count, first, last, body):
    if count <= 8:
        for at, size in chunks(first, last):
            cache = {}
            for plane in range(count):
                body(plane, at, size, cache)
    else:

        def step(plane, carry):
            for at, size in chunks(first, last):
                body(plane, at, size, None)
            return carry

        lax.fori_loop(0, count, step, 0)


def lane_index(size):
    return lax.broadcasted_iota(jnp.int32, (size, LANES), 1)


def row_index(size):
    return lax.broadcasted_iota(jnp.int32, (size, LANES), 0)


def sideways(values, step):
    lane = lane_index(values[0].shape[0])
    back = [pltpu.roll(entry, LANES - step, 1) for entry in values]
    forth = [pltpu.roll(entry, step, 1) for entry in values]
    count = len(values)
    after = [
        jnp.where(lane >= LANES - step, back[i + 1], back[i]) if i + 1 < count else back[i]
        for i in range(count)
    ]
    before = [jnp.where(lane < step, forth[i - 1], forth[i]) if i else forth[i] for i in range(count)]
    return after, before


def neighbours(field, weights, plane, at, size, step, cache):
    tiles = field.shape[0]

    def level(i, index):
        if cache is None:
            return field[i, index, pl.ds(PAD + at, size), :]
        if (i, index) not in cache:
            cache[i, index] = field[i, index, pl.ds(PAD + at, size), :]
        return cache[i, index]

    def weight(kind, i):
        return weights[kind, i, plane, pl.ds(at, size), :]

    centre = [level(i, plane + 2) for i in range(tiles)]
    after, before = sideways(centre, step)
    result = []
    for i in range(tiles):
        row_after = field[i, plane + 2, pl.ds(PAD + at + step, size), :]
        row_before = field[i, plane + 2, pl.ds(PAD + at - step, size), :]
        deep = weight(AFTER_DEPTH, i) * level(i, plane + 3) + weight(BEFORE_DEPTH, i) * level(
            i, plane + 1
        )
        down = weight(AFTER_ROW, i) * row_after + weight(BEFORE_ROW, i) * row_before
        along = weight(AFTER_COLUMN, i) * after[i] + weight(BEFORE_COLUMN, i) * before[i]
        result.append(((deep + down) + along, centre[i]))
    return result


def set_weights(weights, where, c, scale, drift_scale, tile, tiles, step):
    size = c[0].shape[-2]
    base = scale * c[0]
    for axis in range(3):
        drift = drift_scale * c[axis + 1]
        after, before = base - drift, base + drift
        if axis == 2 and tile == tiles - 1:
            after = jnp.where(lane_index(size) >= LANES - step, 0.0, after)
        if axis == 2 and tile == 0:
            before = jnp.where(lane_index(size) < step, 0.0, before)
        weights[(2 * axis,) + where] = after
        weights[(2 * axis + 1,) + where] = before


def clear_edges(field, first, last):
    tiles, planes = field.shape[:2]
    size = field.shape[2]
    plane = jnp.zeros((tiles, 1, size, LANES), jnp.float32)
    field[:, 1:2] = plane
    field[:, planes - 2 : planes - 1] = plane
    rows = jnp.zeros((tiles, planes - 4, PAD, LANES), jnp.float32)
    field[:, 2 : planes - 2, first : first + PAD, :] = rows
    field[:, 2 : planes - 2, PAD + last : PAD + last + PAD, :] = rows


def fine_scheme():
    scales, carries, tildes = chebyshev_coefficients(SECTIONS)
    centre = INTERVAL / (tildes[1] * FINE_STEP)
    factors = [1.0]
    for degree in range(1, SECTIONS + 1):
        factors.append(factors[-1] * tildes[degree] * FINE_STEP / INTERVAL)
    back = [0.0, 0.0]
    for degree in range(2, SECTIONS + 1):
        back.append(carries[degree] * factors[degree - 2] / factors[degree])
    return centre, back, factors[SECTIONS]


def row_places(box, sizes):
    place, count = lax.axis_index("coarse"), lax.axis_size("coarse")
    odd = place % 2
    result = []
    gone = 0
    for step, size in enumerate(sizes, 1):
        below = pl.multiple_of(box.side - gone - size, 8)
        above = pl.multiple_of(box.side + box.rows + gone, 8)
        gone += size
        one = pl.multiple_of(jnp.where(odd == 1, below, above), 8)
        two = pl.multiple_of(jnp.where(odd == 1, above, below), 8)
        below_valid, above_valid = place >= step, place + step < count
        one_valid = jnp.where(odd == 1, below_valid, above_valid)
        two_valid = jnp.where(odd == 1, above_valid, below_valid)
        result.append(((one, one_valid), (two, two_valid)))
    return result


def place_pieces(box, own_depth, pieces, starts, coeff, weights):
    core = lax.axis_index("tm") % 2
    centre_constant = fine_scheme()[0]
    for own, other, block, blocks, at, valid in pieces:
        shift = lax.axis_index("slab") if blocks == 2 else 0
        base = (block + shift) % blocks * own_depth
        size = own.shape[-2]
        for plane in range(own_depth):
            for i in range(box.tiles):
                cols = slice(i * LANES, (i + 1) * LANES)
                where = (i, base + plane, pl.ds(at, size), slice(None))
                for ref, rank in ((own, core), (other, 1 - core)):
                    for slot, kind in ((2 - 2 * rank, None), (rank, 1 + rank), (1 + rank, 3 * rank)):
                        value = ref[slot, plane, :, cols]
                        if valid is not None:
                            value = jnp.where(valid, value, 0.0)
                        if kind is None:
                            starts[(rank,) + where] = value
                        else:
                            coeff[(kind,) + where] = value
                c = [coeff[(k,) + where] for k in range(4)]
                set_weights(weights, where, c, INTERVAL, 0.5 * INTERVAL, i, box.tiles, 1)
                weights[(CENTRE,) + where] = centre_constant - 6.0 * INTERVAL * c[0]


def early_body(box, own_depth, blocks, *refs):
    starts, coeff, weights = refs[-3:]
    half = (len(refs) - 3) // 2
    own, other = refs[:half], refs[half : 2 * half]
    places = row_places(box, [ref.shape[-2] for ref in own[blocks::2]])
    moves = [(own[block], other[block], block, blocks, box.side, None) for block in range(blocks)]
    for step, pair in enumerate(places):
        for which, (at, valid) in enumerate(pair):
            index = blocks + 2 * step + which
            moves.append((own[index], other[index], 0, blocks, at, valid))
    place_pieces(box, own_depth, moves, starts, coeff, weights)


def fine_body(box, margin, own_depth, blocks, *refs):
    end, starts, coeff, weights, one, two = refs[-6:]
    half = (len(refs) - 9) // 2
    own, other = refs[:half], refs[half : 2 * half]
    core = lax.axis_index("tm") % 2
    moves = []
    if blocks > 1:
        each = half // (blocks - 1)
        places = row_places(box, [ref.shape[-2] for ref in own[0:each:2]])
        for block in range(1, blocks):
            for step, pair in enumerate(places):
                for which, (at, valid) in enumerate(pair):
                    index = (block - 1) * each + 2 * step + which
                    moves.append((own[index], other[index], block, blocks, at, valid))
    place_pieces(box, own_depth, moves, starts, coeff, weights)
    clear_edges(one, 0, box.height)
    clear_edges(two, 0, box.height)
    one[:, 2 : 2 + box.depth, PAD : PAD + box.height, :] = starts[core]
    _, back, factor = fine_scheme()
    stage = 0
    current, other_field = one, two
    first, last = box.span(margin)
    for repeat in range(FINE_STEPS):
        for degree in range(1, SECTIONS + 1):
            stage += 1
            final = stage == FINE_REACH

            def body(plane, at, size, cache, current=current, old=other_field, degree=degree, final=final):
                values = neighbours(current, weights, plane, at, size, 1, cache)
                for i, (total, centre) in enumerate(values):
                    value = total + weights[CENTRE, i, plane, pl.ds(at, size), :] * centre
                    where = (i, plane + 2, pl.ds(PAD + at, size), slice(None))
                    if degree > 1:
                        value = value + back[degree] * old[where]
                    if final:
                        end[i, plane, pl.ds(at - first, size), :] = factor**FINE_STEPS * value
                    else:
                        old[where] = value

            sweep(box.depth, *box.span(margin + FINE_REACH - stage), body)
            current, other_field = other_field, current


def pair_columns(value):
    lane = lane_index(value.shape[0])
    other = jnp.where(
        lane % 2 == 0, pltpu.roll(value, LANES - 1, 1), pltpu.roll(value, 1, 1)
    )
    return value + other


def pair_rows(field, i, plane, at, size):
    row = row_index(size)
    other = jnp.where(
        row % 2 == 0,
        field[i, plane + 2, pl.ds(PAD + at + 1, size), :],
        field[i, plane + 2, pl.ds(PAD + at - 1, size), :],
    )
    return field[i, plane + 2, pl.ds(PAD + at, size), :] + other


def prepare_body(box, coeff, coarse, weight, work):
    half = box.depth // 2
    for k in range(4):
        clear_edges(work.at[k], 0, box.height)

        def columns(plane, at, size, cache, k=k):
            for i in range(box.tiles):
                low = coeff[k, i, 2 * plane, pl.ds(at, size), :]
                high = coeff[k, i, 2 * plane + 1, pl.ds(at, size), :]
                work[k, i, plane + 2, pl.ds(PAD + at, size), :] = pair_columns(low + high)
                if k == 0:
                    for offset, value in ((0, low), (1, high)):
                        weight[i, 2 * plane + offset, pl.ds(at, size), :] = RELAX / (
                            1.0 + 6.0 * INTERVAL * value
                        )

        sweep(half, 0, box.height, columns)

    def rows(plane, at, size, cache):
        for i in range(box.tiles):
            where = (i, plane, pl.ds(at, size), slice(None))
            c = [0.125 * pair_rows(work.at[k], i, plane, at, size) for k in range(4)]
            set_weights(coarse, where, c, INTERVAL / 4.0, INTERVAL / 4.0, i, box.tiles, 2)
            coarse[(CENTRE,) + where] = RELAX / (1.0 + 6.0 * INTERVAL / 4.0 * c[0])

    sweep(half, 0, box.height, rows)


def coarse_step_body(box, margin, source, trial, pairs, guess, residual, params, finish):
    weights, coarse, weight = params
    half = box.depth // 2
    centre_constant = fine_scheme()[0]

    def smooth(plane, at, size, cache):
        values = neighbours(source, weights, plane, at, size, 1, cache)
        for i, (total, centre) in enumerate(values):
            trial[i, plane + 2, pl.ds(PAD + at, size), :] = (1.0 - RELAX) * centre + weight[
                i, plane, pl.ds(at, size), :
            ] * (centre + total)

    first, last = box.span(margin + 5)
    clear_edges(trial, first, last)
    sweep(box.depth, first, last, smooth)

    def restrict(plane, at, size, cache):
        sums = [None] * box.tiles
        for half_plane in range(2):
            fine_plane = 2 * plane + half_plane
            values = neighbours(trial, weights, fine_plane, at, size, 1, cache)
            for i, (total, centre) in enumerate(values):
                given = source[i, fine_plane + 2, pl.ds(PAD + at, size), :]
                inner = weights[CENTRE, i, fine_plane, pl.ds(at, size), :] - (1.0 + centre_constant)
                misfit = (given + total) + inner * centre
                sums[i] = misfit if sums[i] is None else sums[i] + misfit
        for i in range(box.tiles):
            pairs[i, plane + 2, pl.ds(PAD + at, size), :] = pair_columns(sums[i])

    first, last = box.span(margin + 4)
    clear_edges(pairs, first, last)
    sweep(half, first, last, restrict)

    def first_guess(plane, at, size, cache):
        for i in range(box.tiles):
            mean = 0.125 * pair_rows(pairs, i, plane, at, size)
            residual[i, plane + 2, pl.ds(PAD + at, size), :] = mean
            guess[i, plane + 2, pl.ds(PAD + at, size), :] = (
                coarse[CENTRE, i, plane, pl.ds(at, size), :] * mean
            )

    clear_edges(guess, first, last)
    sweep(half, first, last, first_guess)

    def correct(plane, at, size, cache):
        values = neighbours(guess, coarse, plane, at, size, 2, cache)
        for i, (total, centre) in enumerate(values):
            rest = residual[i, plane + 2, pl.ds(PAD + at, size), :] + total
            fix = (1.0 - RELAX) * centre + coarse[CENTRE, i, plane, pl.ds(at, size), :] * rest
            for half_plane in range(2):
                where = (i, 2 * plane + half_plane + 2, pl.ds(PAD + at, size), slice(None))
                trial[where] = trial[where] + fix

    sweep(half, *box.span(margin + 2), correct)

    def smooth_again(plane, at, size, cache):
        values = neighbours(trial, weights, plane, at, size, 1, cache)
        for i, (total, centre) in enumerate(values):
            given = source[i, plane + 2, pl.ds(PAD + at, size), :]
            value = (1.0 - RELAX) * centre + weight[i, plane, pl.ds(at, size), :] * (given + total)
            finish(plane, i, at, size, value)

    sweep(box.depth, *box.span(margin), smooth_again)


def coarse_scratch(box):
    half = box.depth // 2
    return [box.scratch(), box.scratch(half), box.scratch(half), box.scratch(half)]


def pair_body(box, own_end, other_end, starts, *rest):
    params, out, first_out, leaving = rest[:3], rest[3], rest[4], rest[5]
    source, trial, pairs, guess, residual = rest[6:]
    core = lax.axis_index("tm") % 2
    first, last = box.span(COARSE_REACH)
    clear_edges(source, first, last)

    def put(first_end, second_end):
        source[:, 2 : 2 + box.depth, PAD + first : PAD + last, :] = (
            first_end[...] - starts[1, :, :, first:last, :]
        )
        inner = slice(box.side - first, box.side - first + box.rows)
        out[...] = second_end[:, :, inner, :]
        first_out[...] = first_end[:, :, inner, :]

    @pl.when(core == 0)
    def _():
        put(own_end, other_end)

    @pl.when(core == 1)
    def _():
        put(other_end, own_end)

    def finish(plane, i, at, size, value):
        where = (i, plane, pl.ds(at - box.side, size), slice(None))
        out[where] = value + out[where]

    coarse_step_body(box, 0, source, trial, pairs, guess, residual, params, finish)
    half = box.depth // 2
    leaving[...] = out[:, pl.ds(core * half, half)]


def last_body(box, own_depth, turn, pieces, first_end, joined, *rest):
    arrived, rest = rest[:pieces], rest[pieces:]
    starts, params, result, leaving = rest[0], rest[1:4], rest[4], rest[5]
    source, second, trial, pairs, guess, residual, total = rest[6:]
    place = lax.axis_index("tm")
    core = place % 2
    active = place // 2 == turn
    side, rows = box.side, box.rows
    half = box.depth // 2
    clear_edges(source, 0, box.height)
    clear_edges(second, *box.span(COARSE_REACH))
    each = pieces // 2
    places = row_places(box, [arrived[at].shape[-2] for at in range(1, each, 2)])

    @pl.when(jnp.logical_not(active))
    def _():
        source[:, 2 : 2 + box.depth, PAD : PAD + box.height, :] = jnp.zeros(
            (box.tiles, box.depth, box.height, LANES), jnp.float32
        )

    @pl.when(active)
    def _():
        for part, rank in ((0, core), (1, 1 - core)):
            moves = [(arrived[part * each], side, None)]
            for step, pair in enumerate(places):
                at = part * each + 1 + 2 * step
                for ref, (where, valid) in zip(arrived[at : at + 2], pair):
                    moves.append((ref, where, valid))
            base = rank * half
            for ref, at, valid in moves:
                size = ref.shape[-2]
                for plane in range(half):
                    for i in range(box.tiles):
                        value = ref[i, plane]
                        if valid is not None:
                            value = jnp.where(valid, value, 0.0)
                        source[i, base + plane + 2, pl.ds(PAD + at, size), :] = (
                            value - starts[0, i, base + plane, pl.ds(at, size), :]
                        )

    def finish_once(plane, i, at, size, value):
        second[i, plane + 2, pl.ds(PAD + at, size), :] = value

    coarse_step_body(
        box, COARSE_REACH, source, trial, pairs, guess, residual, params, finish_once
    )

    def finish_twice(plane, i, at, size, value):
        where = (i, plane, pl.ds(at - box.side, size), slice(None))
        total[where] = value + joined[where]

    coarse_step_body(box, 0, second, trial, pairs, guess, residual, params, finish_twice)
    base = lax.axis_index("slab") * own_depth

    @pl.when(core == 0)
    def _():
        for i in range(box.tiles):
            result[0, :, :, i * LANES : (i + 1) * LANES] = (
                first_end[i, pl.ds(base, own_depth)]
                + second[i, pl.ds(base + 2, own_depth), PAD + side : PAD + side + rows, :]
            )

    @pl.when(core == 1)
    def _():
        for i in range(box.tiles):
            result[0, :, :, i * LANES : (i + 1) * LANES] = total[i, pl.ds(base, own_depth)]

    leaving[...] = total[:, pl.ds(core * half, half)]


def run(body, outs, scratch, *args, aliases={}):
    return pl.pallas_call(
        body,
        out_shape=[jax.ShapeDtypeStruct(shape, jnp.float32) for shape in outs],
        in_specs=[pl.BlockSpec(memory_space=pltpu.VMEM)] * len(args),
        out_specs=[pl.BlockSpec(memory_space=pltpu.VMEM)] * len(outs),
        scratch_shapes=scratch,
        input_output_aliases=aliases,
        compiler_params=pltpu.CompilerParams(vmem_limit_bytes=20 * 1024 * 1024),
    )(*args)


def slab_blocks(block):
    count = lax.axis_size("slab")
    if count == 1:
        return [block]
    if count == 2:
        return [block, lax.ppermute(block, "slab", [(0, 1), (1, 0)])]
    gathered = lax.all_gather(block, "slab", axis=0)
    return [gathered[i] for i in range(count)]


def row_swaps(hop, away):
    windows, count = lax.axis_size("tm"), lax.axis_size("coarse")
    rounds = []
    for first in (0, 1):
        pairs = []
        for place in range(count):
            other = place + 1 if place % 2 == first else place - 1
            for t in range(windows):
                inside = 0 <= other < count
                target = (hop(t), other) if inside else (away(t), place)
                pairs.append((t * count + place, target[0] * count + target[1]))
        rounds.append(pairs)
    return rounds


def row_pieces(block, width, rounds):
    rows = block.shape[-2]
    axis = block.ndim - 2
    both = ("tm", "coarse")
    odd = lax.axis_index("coarse") % 2 == 1
    pieces = []
    up, down = block, block
    left = width
    while left > 0:
        size = min(rows, left)
        if size == rows and up is down:
            send_one = send_two = block
        else:
            high = lax.slice_in_dim(up, up.shape[axis] - size, None, axis=axis)
            low = lax.slice_in_dim(down, 0, size, axis=axis)
            send_one, send_two = jnp.where(odd, low, high), jnp.where(odd, high, low)
        got_one = lax.ppermute(send_one, both, rounds[0])
        got_two = lax.ppermute(send_two, both, rounds[1])
        pieces += [got_one, got_two]
        left -= size
        if left > 0:
            up, down = jnp.where(odd, got_one, got_two), jnp.where(odd, got_two, got_one)
    return pieces


def core_swapped(block):
    count = lax.axis_size("tm")
    assert count % 2 == 0
    return lax.ppermute(block, "tm", [(i, i ^ 1) for i in range(count)])


def per_device(states, diffusivity, velocity):
    windows = lax.axis_size("tm")
    place = lax.axis_index("tm")
    own_depth, rows, columns = diffusivity.shape
    side = round_up(FINE_REACH + COARSE_REACH, 8)
    depth = own_depth * lax.axis_size("slab")
    box = Box(depth, rows, side, columns)
    tiles, height, half = box.tiles, box.height, depth // 2

    second = place % 2 == 1
    slot = lax.broadcasted_iota(jnp.int32, (3, 1, 1, 1), 0)
    parcel = jnp.where(
        (slot == 0) != second, velocity, jnp.where(slot == 1, diffusivity[None], states)
    )
    rounds = row_swaps(lambda t: t, lambda t: t ^ 1)
    blocks = slab_blocks(parcel)
    swapped = [core_swapped(block) for block in blocks]
    near = row_pieces(blocks[0], side, rounds)
    near_swapped = [core_swapped(piece) for piece in near]
    count = len(blocks)
    shapes = [(n, tiles, depth, height, LANES) for n in (2, 4, 7)]
    placed = run(
        functools.partial(early_body, box, own_depth, count),
        shapes,
        [],
        *blocks,
        *near,
        *swapped,
        *near_swapped,
    )
    far = []
    for block in blocks[1:]:
        far += row_pieces(block, side, rounds)
    far += [core_swapped(piece) for piece in far]
    first, last = box.span(COARSE_REACH)
    end, starts, coeff, weights = run(
        functools.partial(fine_body, box, COARSE_REACH, own_depth, count),
        [(tiles, depth, last - first, LANES)] + shapes,
        [box.scratch(), box.scratch()],
        *far,
        *placed,
        aliases={len(far) + n: 1 + n for n in range(3)},
    )
    params = run(
        functools.partial(prepare_body, box),
        [(7, tiles, half, height, LANES), (tiles, depth, height, LANES)],
        [pltpu.VMEM((4, *box.scratch(half).shape), jnp.float32)],
        coeff,
    )
    params = [weights, *params]
    joined, first_end, leaving = run(
        functools.partial(pair_body, box),
        [(tiles, depth, rows, LANES)] * 2 + [(tiles, half, rows, LANES)],
        [box.scratch()] + coarse_scratch(box),
        end,
        core_swapped(end),
        starts,
        *params,
    )
    ends = jnp.where(place % 2 == 1, joined, first_end)
    ends = jnp.concatenate([ends[i] for i in range(tiles)], axis=-1)
    base = lax.axis_index("slab") * own_depth
    result = lax.dynamic_slice_in_dim(ends, base, own_depth, 0)[None]
    hop = lambda t: (t + 2) % windows
    rounds = row_swaps(hop, hop)
    for turn in range(1, windows // 2):
        centre = lax.ppermute(leaving, "tm", [(t, hop(t)) for t in range(windows)])
        if rows >= 2 * COARSE_REACH:
            arrived = [centre, *row_pieces(leaving, min(rows, side), rounds)]
        else:
            near = row_swaps(lambda t: t, lambda t: t ^ 1)
            arrived = [centre, *row_pieces(centre, side, near)]
        arrived += [core_swapped(piece) for piece in arrived]
        out, leaving = run(
            functools.partial(last_body, box, own_depth, turn, len(arrived)),
            [(1, own_depth, rows, columns), (tiles, half, rows, LANES)],
            [box.scratch()] * 2
            + coarse_scratch(box)
            + [pltpu.VMEM((tiles, depth, rows, LANES), jnp.float32)],
            first_end,
            joined,
            *arrived,
            starts,
            *params,
        )
        result = out if turn == 1 else jnp.where(place // 2 >= turn, out, result)
    return result


def solution(mesh):
    return jax.shard_map(
        per_device,
        mesh=mesh,
        in_specs=(
            P("tm", "slab", "coarse", None),
            P("slab", "coarse", None),
            P(None, "slab", "coarse", None),
        ),
        out_specs=P("tm", "slab", "coarse", None),
        check_vma=False,
    )
```

```python
import functools

import jax
import jax.numpy as jnp
from jax import lax
from jax.experimental import pallas as pl
from jax.experimental.pallas import tpu as pltpu
from jax.sharding import PartitionSpec as P

SECTIONS = 4
FINE_STEPS = 2
FINE_STEP = 1.0
RELAX = 0.8
INTERVAL = FINE_STEPS * FINE_STEP
LANES = 128
PAD = 8
COARSE_REACH = 6
FINE_REACH = SECTIONS * FINE_STEPS


def chebyshev_coefficients(sections):
    damping = 0.05
    centre_point = 1.0 + damping / (sections * sections)
    chebyshev = [1.0, centre_point]
    slopes = [0.0, 1.0]
    for degree in range(2, sections + 1):
        chebyshev.append(2.0 * centre_point * chebyshev[degree - 1] - chebyshev[degree - 2])
        slopes.append(
            2.0 * chebyshev[degree - 1]
            + 2.0 * centre_point * slopes[degree - 1]
            - slopes[degree - 2]
        )
    slope_ratio = chebyshev[sections] / slopes[sections]
    weights = [1.0 / entry for entry in chebyshev]
    scales = [0.0, 0.0]
    carries = [0.0, 0.0]
    tildes = [0.0, slope_ratio / centre_point]
    for degree in range(2, sections + 1):
        scales.append(2.0 * weights[degree] * centre_point / weights[degree - 1])
        carries.append(-weights[degree] / weights[degree - 2])
        tildes.append(2.0 * weights[degree] * slope_ratio / weights[degree - 1])
    return (scales, carries, tildes)


def round_up(value, unit):
    return -(-value // unit) * unit


class Box:
    def __init__(self, depth, rows, side, columns):
        self.depth, self.rows, self.side, self.columns = depth, rows, side, columns
        self.height = rows + 2 * side
        self.tiles = columns // LANES

    def scratch(self, depth=None):
        depth = self.depth if depth is None else depth
        return pltpu.VMEM(
            (self.tiles, depth + 4, self.height + 2 * PAD, LANES), jnp.float32
        )

    def span(self, margin):
        size = round_up(self.rows + 2 * margin, 8)
        first = self.side - (size - self.rows) // 2
        assert first >= 0 and first % 2 == 0
        return first, first + size


CHUNK = 16
AFTER_DEPTH, BEFORE_DEPTH, AFTER_ROW, BEFORE_ROW, AFTER_COLUMN, BEFORE_COLUMN, CENTRE = range(7)


def chunks(first, last):
    at = first
    while at < last:
        size = min(CHUNK, last - at)
        yield at, size
        at += size


def sweep(count, first, last, body):
    if count <= 8:
        for at, size in chunks(first, last):
            cache = {}
            for plane in range(count):
                body(plane, at, size, cache)
    else:

        def step(plane, carry):
            for at, size in chunks(first, last):
                body(plane, at, size, None)
            return carry

        lax.fori_loop(0, count, step, 0)


def lane_index(size):
    return lax.broadcasted_iota(jnp.int32, (size, LANES), 1)


def row_index(size):
    return lax.broadcasted_iota(jnp.int32, (size, LANES), 0)


def sideways(values, step):
    lane = lane_index(values[0].shape[0])
    back = [pltpu.roll(entry, LANES - step, 1) for entry in values]
    forth = [pltpu.roll(entry, step, 1) for entry in values]
    count = len(values)
    after = [
        jnp.where(lane >= LANES - step, back[i + 1], back[i]) if i + 1 < count else back[i]
        for i in range(count)
    ]
    before = [jnp.where(lane < step, forth[i - 1], forth[i]) if i else forth[i] for i in range(count)]
    return after, before


def neighbours(field, weights, plane, at, size, step, cache):
    tiles = field.shape[0]

    def level(i, index):
        if cache is None:
            return field[i, index, pl.ds(PAD + at, size), :]
        if (i, index) not in cache:
            cache[i, index] = field[i, index, pl.ds(PAD + at, size), :]
        return cache[i, index]

    def weight(kind, i):
        return weights[kind, i, plane, pl.ds(at, size), :]

    centre = [level(i, plane + 2) for i in range(tiles)]
    after, before = sideways(centre, step)
    result = []
    for i in range(tiles):
        row_after = field[i, plane + 2, pl.ds(PAD + at + step, size), :]
        row_before = field[i, plane + 2, pl.ds(PAD + at - step, size), :]
        deep = weight(AFTER_DEPTH, i) * level(i, plane + 3) + weight(BEFORE_DEPTH, i) * level(
            i, plane + 1
        )
        down = weight(AFTER_ROW, i) * row_after + weight(BEFORE_ROW, i) * row_before
        along = weight(AFTER_COLUMN, i) * after[i] + weight(BEFORE_COLUMN, i) * before[i]
        result.append(((deep + down) + along, centre[i]))
    return result


def set_weights(weights, where, c, scale, drift_scale, tile, tiles, step):
    size = c[0].shape[-2]
    base = scale * c[0]
    for axis in range(3):
        drift = drift_scale * c[axis + 1]
        after, before = base - drift, base + drift
        if axis == 2 and tile == tiles - 1:
            after = jnp.where(lane_index(size) >= LANES - step, 0.0, after)
        if axis == 2 and tile == 0:
            before = jnp.where(lane_index(size) < step, 0.0, before)
        weights[(2 * axis,) + where] = after
        weights[(2 * axis + 1,) + where] = before


def clear_edges(field, first, last):
    tiles, planes = field.shape[:2]
    size = field.shape[2]
    plane = jnp.zeros((tiles, 1, size, LANES), jnp.float32)
    field[:, 1:2] = plane
    field[:, planes - 2 : planes - 1] = plane
    rows = jnp.zeros((tiles, planes - 4, PAD, LANES), jnp.float32)
    field[:, 2 : planes - 2, first : first + PAD, :] = rows
    field[:, 2 : planes - 2, PAD + last : PAD + last + PAD, :] = rows


def fine_scheme():
    scales, carries, tildes = chebyshev_coefficients(SECTIONS)
    centre = INTERVAL / (tildes[1] * FINE_STEP)
    factors = [1.0]
    for degree in range(1, SECTIONS + 1):
        factors.append(factors[-1] * tildes[degree] * FINE_STEP / INTERVAL)
    back = [0.0, 0.0]
    for degree in range(2, SECTIONS + 1):
        back.append(carries[degree] * factors[degree - 2] / factors[degree])
    return centre, back, factors[SECTIONS]


def row_places(box, sizes):
    place, count = lax.axis_index("coarse"), lax.axis_size("coarse")
    odd = place % 2
    result = []
    gone = 0
    for step, size in enumerate(sizes, 1):
        below = pl.multiple_of(box.side - gone - size, 8)
        above = pl.multiple_of(box.side + box.rows + gone, 8)
        gone += size
        one = pl.multiple_of(jnp.where(odd == 1, below, above), 8)
        two = pl.multiple_of(jnp.where(odd == 1, above, below), 8)
        below_valid, above_valid = place >= step, place + step < count
        one_valid = jnp.where(odd == 1, below_valid, above_valid)
        two_valid = jnp.where(odd == 1, above_valid, below_valid)
        result.append(((one, one_valid), (two, two_valid)))
    return result


def place_pieces(box, own_depth, pieces, starts, coeff, weights):
    core = lax.axis_index("tm") % 2
    centre_constant = fine_scheme()[0]
    for own, other, block, blocks, at, valid in pieces:
        shift = lax.axis_index("slab") if blocks == 2 else 0
        base = (block + shift) % blocks * own_depth
        size = own.shape[-2]
        for plane in range(own_depth):
            for i in range(box.tiles):
                cols = slice(i * LANES, (i + 1) * LANES)
                where = (i, base + plane, pl.ds(at, size), slice(None))
                for ref, rank in ((own, core), (other, 1 - core)):
                    for slot, kind in ((2 - 2 * rank, None), (rank, 1 + rank), (1 + rank, 3 * rank)):
                        value = ref[slot, plane, :, cols]
                        if valid is not None:
                            value = jnp.where(valid, value, 0.0)
                        if kind is None:
                            starts[(rank,) + where] = value
                        else:
                            coeff[(kind,) + where] = value
                c = [coeff[(k,) + where] for k in range(4)]
                set_weights(weights, where, c, INTERVAL, 0.5 * INTERVAL, i, box.tiles, 1)
                weights[(CENTRE,) + where] = centre_constant - 6.0 * INTERVAL * c[0]


def early_body(box, own_depth, blocks, *refs):
    starts, coeff, weights = refs[-3:]
    half = (len(refs) - 3) // 2
    own, other = refs[:half], refs[half : 2 * half]
    places = row_places(box, [ref.shape[-2] for ref in own[blocks::2]])
    moves = [(own[block], other[block], block, blocks, box.side, None) for block in range(blocks)]
    for step, pair in enumerate(places):
        for which, (at, valid) in enumerate(pair):
            index = blocks + 2 * step + which
            moves.append((own[index], other[index], 0, blocks, at, valid))
    place_pieces(box, own_depth, moves, starts, coeff, weights)


def fine_body(box, margin, own_depth, blocks, *refs):
    end, starts, coeff, weights, one, two = refs[-6:]
    half = (len(refs) - 9) // 2
    own, other = refs[:half], refs[half : 2 * half]
    core = lax.axis_index("tm") % 2
    moves = []
    if blocks > 1:
        each = half // (blocks - 1)
        places = row_places(box, [ref.shape[-2] for ref in own[0:each:2]])
        for block in range(1, blocks):
            for step, pair in enumerate(places):
                for which, (at, valid) in enumerate(pair):
                    index = (block - 1) * each + 2 * step + which
                    moves.append((own[index], other[index], block, blocks, at, valid))
    place_pieces(box, own_depth, moves, starts, coeff, weights)
    clear_edges(one, 0, box.height)
    clear_edges(two, 0, box.height)
    one[:, 2 : 2 + box.depth, PAD : PAD + box.height, :] = starts[core]
    _, back, factor = fine_scheme()
    stage = 0
    current, other_field = one, two
    first, last = box.span(margin)
    for repeat in range(FINE_STEPS):
        for degree in range(1, SECTIONS + 1):
            stage += 1
            final = stage == FINE_REACH

            def body(plane, at, size, cache, current=current, old=other_field, degree=degree, final=final):
                values = neighbours(current, weights, plane, at, size, 1, cache)
                for i, (total, centre) in enumerate(values):
                    value = total + weights[CENTRE, i, plane, pl.ds(at, size), :] * centre
                    where = (i, plane + 2, pl.ds(PAD + at, size), slice(None))
                    if degree > 1:
                        value = value + back[degree] * old[where]
                    if final:
                        end[i, plane, pl.ds(at - first, size), :] = factor**FINE_STEPS * value
                    else:
                        old[where] = value

            sweep(box.depth, *box.span(margin + FINE_REACH - stage), body)
            current, other_field = other_field, current


def pair_columns(value):
    lane = lane_index(value.shape[0])
    other = jnp.where(
        lane % 2 == 0, pltpu.roll(value, LANES - 1, 1), pltpu.roll(value, 1, 1)
    )
    return value + other


def pair_rows(field, i, plane, at, size):
    row = row_index(size)
    other = jnp.where(
        row % 2 == 0,
        field[i, plane + 2, pl.ds(PAD + at + 1, size), :],
        field[i, plane + 2, pl.ds(PAD + at - 1, size), :],
    )
    return field[i, plane + 2, pl.ds(PAD + at, size), :] + other


def prepare_body(box, coeff, coarse, weight, work):
    half = box.depth // 2
    for k in range(4):
        clear_edges(work.at[k], 0, box.height)

        def columns(plane, at, size, cache, k=k):
            for i in range(box.tiles):
                low = coeff[k, i, 2 * plane, pl.ds(at, size), :]
                high = coeff[k, i, 2 * plane + 1, pl.ds(at, size), :]
                work[k, i, plane + 2, pl.ds(PAD + at, size), :] = pair_columns(low + high)
                if k == 0:
                    for offset, value in ((0, low), (1, high)):
                        weight[i, 2 * plane + offset, pl.ds(at, size), :] = RELAX / (
                            1.0 + 6.0 * INTERVAL * value
                        )

        sweep(half, 0, box.height, columns)

    def rows(plane, at, size, cache):
        for i in range(box.tiles):
            where = (i, plane, pl.ds(at, size), slice(None))
            c = [0.125 * pair_rows(work.at[k], i, plane, at, size) for k in range(4)]
            set_weights(coarse, where, c, INTERVAL / 4.0, INTERVAL / 4.0, i, box.tiles, 2)
            coarse[(CENTRE,) + where] = RELAX / (1.0 + 6.0 * INTERVAL / 4.0 * c[0])

    sweep(half, 0, box.height, rows)


def coarse_step_body(box, margin, source, trial, pairs, guess, residual, params, finish):
    weights, coarse, weight = params
    half = box.depth // 2
    centre_constant = fine_scheme()[0]

    def smooth(plane, at, size, cache):
        values = neighbours(source, weights, plane, at, size, 1, cache)
        for i, (total, centre) in enumerate(values):
            trial[i, plane + 2, pl.ds(PAD + at, size), :] = (1.0 - RELAX) * centre + weight[
                i, plane, pl.ds(at, size), :
            ] * (centre + total)

    first, last = box.span(margin + 5)
    clear_edges(trial, first, last)
    sweep(box.depth, first, last, smooth)

    def restrict(plane, at, size, cache):
        sums = [None] * box.tiles
        for half_plane in range(2):
            fine_plane = 2 * plane + half_plane
            values = neighbours(trial, weights, fine_plane, at, size, 1, cache)
            for i, (total, centre) in enumerate(values):
                given = source[i, fine_plane + 2, pl.ds(PAD + at, size), :]
                inner = weights[CENTRE, i, fine_plane, pl.ds(at, size), :] - (1.0 + centre_constant)
                misfit = (given + total) + inner * centre
                sums[i] = misfit if sums[i] is None else sums[i] + misfit
        for i in range(box.tiles):
            pairs[i, plane + 2, pl.ds(PAD + at, size), :] = sums[i]

    first, last = box.span(margin + 4)
    clear_edges(pairs, first, last)
    sweep(half, first, last, restrict)

    def first_guess(plane, at, size, cache):
        for i in range(box.tiles):
            mean = 0.125 * pair_columns(pair_rows(pairs, i, plane, at, size))
            residual[i, plane + 2, pl.ds(PAD + at, size), :] = mean
            guess[i, plane + 2, pl.ds(PAD + at, size), :] = (
                coarse[CENTRE, i, plane, pl.ds(at, size), :] * mean
            )

    clear_edges(guess, first, last)
    sweep(half, first, last, first_guess)

    def correct(plane, at, size, cache):
        values = neighbours(guess, coarse, plane, at, size, 2, cache)
        for i, (total, centre) in enumerate(values):
            rest = residual[i, plane + 2, pl.ds(PAD + at, size), :] + total
            fix = (1.0 - RELAX) * centre + coarse[CENTRE, i, plane, pl.ds(at, size), :] * rest
            for half_plane in range(2):
                where = (i, 2 * plane + half_plane + 2, pl.ds(PAD + at, size), slice(None))
                trial[where] = trial[where] + fix

    sweep(half, *box.span(margin + 2), correct)

    def smooth_again(plane, at, size, cache):
        values = neighbours(trial, weights, plane, at, size, 1, cache)
        for i, (total, centre) in enumerate(values):
            given = source[i, plane + 2, pl.ds(PAD + at, size), :]
            value = (1.0 - RELAX) * centre + weight[i, plane, pl.ds(at, size), :] * (given + total)
            finish(plane, i, at, size, value)

    sweep(box.depth, *box.span(margin), smooth_again)


def coarse_scratch(box):
    half = box.depth // 2
    return [box.scratch(), box.scratch(half), box.scratch(half), box.scratch(half)]


def pair_body(box, own_end, other_end, starts, *rest):
    params, out, first_out, leaving = rest[:3], rest[3], rest[4], rest[5]
    source, trial, pairs, guess, residual = rest[6:]
    core = lax.axis_index("tm") % 2
    first, last = box.span(COARSE_REACH)
    clear_edges(source, first, last)

    def put(first_end, second_end):
        source[:, 2 : 2 + box.depth, PAD + first : PAD + last, :] = (
            first_end[...] - starts[1, :, :, first:last, :]
        )
        inner = slice(box.side - first, box.side - first + box.rows)
        out[...] = second_end[:, :, inner, :]
        first_out[...] = first_end[:, :, inner, :]

    @pl.when(core == 0)
    def _():
        put(own_end, other_end)

    @pl.when(core == 1)
    def _():
        put(other_end, own_end)

    def finish(plane, i, at, size, value):
        where = (i, plane, pl.ds(at - box.side, size), slice(None))
        out[where] = value + out[where]

    coarse_step_body(box, 0, source, trial, pairs, guess, residual, params, finish)
    half = box.depth // 2
    leaving[...] = out[:, pl.ds(core * half, half)]


def last_body(box, own_depth, turn, pieces, first_end, joined, *rest):
    arrived, rest = rest[:pieces], rest[pieces:]
    starts, params, result, leaving = rest[0], rest[1:4], rest[4], rest[5]
    source, second, trial, pairs, guess, residual, total = rest[6:]
    place = lax.axis_index("tm")
    core = place % 2
    active = place // 2 == turn
    side, rows = box.side, box.rows
    half = box.depth // 2
    clear_edges(source, 0, box.height)
    clear_edges(second, *box.span(COARSE_REACH))
    each = pieces // 2
    places = row_places(box, [arrived[at].shape[-2] for at in range(1, each, 2)])

    @pl.when(jnp.logical_not(active))
    def _():
        source[:, 2 : 2 + box.depth, PAD : PAD + box.height, :] = jnp.zeros(
            (box.tiles, box.depth, box.height, LANES), jnp.float32
        )

    @pl.when(active)
    def _():
        for part, rank in ((0, core), (1, 1 - core)):
            moves = [(arrived[part * each], side, None)]
            for step, pair in enumerate(places):
                at = part * each + 1 + 2 * step
                for ref, (where, valid) in zip(arrived[at : at + 2], pair):
                    moves.append((ref, where, valid))
            base = rank * half
            for ref, at, valid in moves:
                size = ref.shape[-2]
                for plane in range(half):
                    for i in range(box.tiles):
                        value = ref[i, plane]
                        if valid is not None:
                            value = jnp.where(valid, value, 0.0)
                        source[i, base + plane + 2, pl.ds(PAD + at, size), :] = (
                            value - starts[0, i, base + plane, pl.ds(at, size), :]
                        )

    def finish_once(plane, i, at, size, value):
        second[i, plane + 2, pl.ds(PAD + at, size), :] = value

    coarse_step_body(
        box, COARSE_REACH, source, trial, pairs, guess, residual, params, finish_once
    )

    def finish_twice(plane, i, at, size, value):
        where = (i, plane, pl.ds(at - box.side, size), slice(None))
        total[where] = value + joined[where]

    coarse_step_body(box, 0, second, trial, pairs, guess, residual, params, finish_twice)
    base = lax.axis_index("slab") * own_depth

    @pl.when(core == 0)
    def _():
        for i in range(box.tiles):
            result[0, :, :, i * LANES : (i + 1) * LANES] = (
                first_end[i, pl.ds(base, own_depth)]
                + second[i, pl.ds(base + 2, own_depth), PAD + side : PAD + side + rows, :]
            )

    @pl.when(core == 1)
    def _():
        for i in range(box.tiles):
            result[0, :, :, i * LANES : (i + 1) * LANES] = total[i, pl.ds(base, own_depth)]

    leaving[...] = total[:, pl.ds(core * half, half)]


def run(body, outs, scratch, *args, aliases={}):
    return pl.pallas_call(
        body,
        out_shape=[jax.ShapeDtypeStruct(shape, jnp.float32) for shape in outs],
        in_specs=[pl.BlockSpec(memory_space=pltpu.VMEM)] * len(args),
        out_specs=[pl.BlockSpec(memory_space=pltpu.VMEM)] * len(outs),
        scratch_shapes=scratch,
        input_output_aliases=aliases,
        compiler_params=pltpu.CompilerParams(vmem_limit_bytes=20 * 1024 * 1024),
    )(*args)


def slab_blocks(block):
    count = lax.axis_size("slab")
    if count == 1:
        return [block]
    if count == 2:
        return [block, lax.ppermute(block, "slab", [(0, 1), (1, 0)])]
    gathered = lax.all_gather(block, "slab", axis=0)
    return [gathered[i] for i in range(count)]


def row_swaps(hop, away):
    windows, count = lax.axis_size("tm"), lax.axis_size("coarse")
    rounds = []
    for first in (0, 1):
        pairs = []
        for place in range(count):
            other = place + 1 if place % 2 == first else place - 1
            for t in range(windows):
                inside = 0 <= other < count
                target = (hop(t), other) if inside else (away(t), place)
                pairs.append((t * count + place, target[0] * count + target[1]))
        rounds.append(pairs)
    return rounds


def row_pieces(block, width, rounds):
    rows = block.shape[-2]
    axis = block.ndim - 2
    both = ("tm", "coarse")
    odd = lax.axis_index("coarse") % 2 == 1
    pieces = []
    up, down = block, block
    left = width
    while left > 0:
        size = min(rows, left)
        if size == rows and up is down:
            send_one = send_two = block
        else:
            high = lax.slice_in_dim(up, up.shape[axis] - size, None, axis=axis)
            low = lax.slice_in_dim(down, 0, size, axis=axis)
            send_one, send_two = jnp.where(odd, low, high), jnp.where(odd, high, low)
        got_one = lax.ppermute(send_one, both, rounds[0])
        got_two = lax.ppermute(send_two, both, rounds[1])
        pieces += [got_one, got_two]
        left -= size
        if left > 0:
            up, down = jnp.where(odd, got_one, got_two), jnp.where(odd, got_two, got_one)
    return pieces


def core_swapped(block):
    count = lax.axis_size("tm")
    assert count % 2 == 0
    return lax.ppermute(block, "tm", [(i, i ^ 1) for i in range(count)])


def per_device(states, diffusivity, velocity):
    windows = lax.axis_size("tm")
    place = lax.axis_index("tm")
    own_depth, rows, columns = diffusivity.shape
    side = round_up(FINE_REACH + COARSE_REACH, 8)
    depth = own_depth * lax.axis_size("slab")
    box = Box(depth, rows, side, columns)
    tiles, height, half = box.tiles, box.height, depth // 2

    second = place % 2 == 1
    slot = lax.broadcasted_iota(jnp.int32, (3, 1, 1, 1), 0)
    parcel = jnp.where(
        (slot == 0) != second, velocity, jnp.where(slot == 1, diffusivity[None], states)
    )
    rounds = row_swaps(lambda t: t, lambda t: t ^ 1)
    blocks = slab_blocks(parcel)
    swapped = [core_swapped(block) for block in blocks]
    near = row_pieces(blocks[0], side, rounds)
    near_swapped = [core_swapped(piece) for piece in near]
    count = len(blocks)
    shapes = [(n, tiles, depth, height, LANES) for n in (2, 4, 7)]
    placed = run(
        functools.partial(early_body, box, own_depth, count),
        shapes,
        [],
        *blocks,
        *near,
        *swapped,
        *near_swapped,
    )
    far = []
    for block in blocks[1:]:
        far += row_pieces(block, side, rounds)
    far += [core_swapped(piece) for piece in far]
    first, last = box.span(COARSE_REACH)
    end, starts, coeff, weights = run(
        functools.partial(fine_body, box, COARSE_REACH, own_depth, count),
        [(tiles, depth, last - first, LANES)] + shapes,
        [box.scratch(), box.scratch()],
        *far,
        *placed,
        aliases={len(far) + n: 1 + n for n in range(3)},
    )
    params = run(
        functools.partial(prepare_body, box),
        [(7, tiles, half, height, LANES), (tiles, depth, height, LANES)],
        [pltpu.VMEM((4, *box.scratch(half).shape), jnp.float32)],
        coeff,
    )
    params = [weights, *params]
    joined, first_end, leaving = run(
        functools.partial(pair_body, box),
        [(tiles, depth, rows, LANES)] * 2 + [(tiles, half, rows, LANES)],
        [box.scratch()] + coarse_scratch(box),
        end,
        core_swapped(end),
        starts,
        *params,
    )
    ends = jnp.where(place % 2 == 1, joined, first_end)
    ends = jnp.concatenate([ends[i] for i in range(tiles)], axis=-1)
    base = lax.axis_index("slab") * own_depth
    result = lax.dynamic_slice_in_dim(ends, base, own_depth, 0)[None]
    hop = lambda t: (t + 2) % windows
    rounds = row_swaps(hop, hop)
    for turn in range(1, windows // 2):
        centre = lax.ppermute(leaving, "tm", [(t, hop(t)) for t in range(windows)])
        if rows >= 2 * COARSE_REACH:
            arrived = [centre, *row_pieces(leaving, min(rows, side), rounds)]
        else:
            near = row_swaps(lambda t: t, lambda t: t ^ 1)
            arrived = [centre, *row_pieces(centre, side, near)]
        arrived += [core_swapped(piece) for piece in arrived]
        out, leaving = run(
            functools.partial(last_body, box, own_depth, turn, len(arrived)),
            [(1, own_depth, rows, columns), (tiles, half, rows, LANES)],
            [box.scratch()] * 2
            + coarse_scratch(box)
            + [pltpu.VMEM((tiles, depth, rows, LANES), jnp.float32)],
            first_end,
            joined,
            *arrived,
            starts,
            *params,
        )
        result = out if turn == 1 else jnp.where(place // 2 >= turn, out, result)
    return result


def solution(mesh):
    return jax.shard_map(
        per_device,
        mesh=mesh,
        in_specs=(
            P("tm", "slab", "coarse", None),
            P("slab", "coarse", None),
            P(None, "slab", "coarse", None),
        ),
        out_specs=P("tm", "slab", "coarse", None),
        check_vma=False,
    )
```

```python
import functools

import jax
import jax.numpy as jnp
from jax import lax
from jax.experimental import pallas as pl
from jax.experimental.pallas import tpu as pltpu
from jax.sharding import PartitionSpec as P

SECTIONS = 4
FINE_STEPS = 2
FINE_STEP = 1.0
RELAX = 0.8
INTERVAL = FINE_STEPS * FINE_STEP
LANES = 128
PAD = 8
COARSE_REACH = 6
FINE_REACH = SECTIONS * FINE_STEPS


def chebyshev_coefficients(sections):
    damping = 0.05
    centre_point = 1.0 + damping / (sections * sections)
    chebyshev = [1.0, centre_point]
    slopes = [0.0, 1.0]
    for degree in range(2, sections + 1):
        chebyshev.append(2.0 * centre_point * chebyshev[degree - 1] - chebyshev[degree - 2])
        slopes.append(
            2.0 * chebyshev[degree - 1]
            + 2.0 * centre_point * slopes[degree - 1]
            - slopes[degree - 2]
        )
    slope_ratio = chebyshev[sections] / slopes[sections]
    weights = [1.0 / entry for entry in chebyshev]
    scales = [0.0, 0.0]
    carries = [0.0, 0.0]
    tildes = [0.0, slope_ratio / centre_point]
    for degree in range(2, sections + 1):
        scales.append(2.0 * weights[degree] * centre_point / weights[degree - 1])
        carries.append(-weights[degree] / weights[degree - 2])
        tildes.append(2.0 * weights[degree] * slope_ratio / weights[degree - 1])
    return (scales, carries, tildes)


def round_up(value, unit):
    return -(-value // unit) * unit


class Box:
    def __init__(self, depth, rows, side, columns):
        self.depth, self.rows, self.side, self.columns = depth, rows, side, columns
        self.height = rows + 2 * side
        self.tiles = columns // LANES

    def scratch(self, depth=None):
        depth = self.depth if depth is None else depth
        return pltpu.VMEM(
            (self.tiles, depth + 4, self.height + 2 * PAD, LANES), jnp.float32
        )

    def span(self, margin):
        size = round_up(self.rows + 2 * margin, 8)
        first = self.side - (size - self.rows) // 2
        assert first >= 0 and first % 2 == 0
        return first, first + size


CHUNK = 16
AFTER_DEPTH, BEFORE_DEPTH, AFTER_ROW, BEFORE_ROW, AFTER_COLUMN, BEFORE_COLUMN, CENTRE = range(7)


def chunks(first, last):
    at = first
    while at < last:
        size = min(CHUNK, last - at)
        yield at, size
        at += size


def sweep(count, first, last, body):
    if count <= 8:
        for at, size in chunks(first, last):
            cache = {}
            for plane in range(count):
                body(plane, at, size, cache)
    else:

        def step(plane, carry):
            for at, size in chunks(first, last):
                body(plane, at, size, None)
            return carry

        lax.fori_loop(0, count, step, 0)


def lane_index(size):
    return lax.broadcasted_iota(jnp.int32, (size, LANES), 1)


def row_index(size):
    return lax.broadcasted_iota(jnp.int32, (size, LANES), 0)


def sideways(values, step):
    lane = lane_index(values[0].shape[0])
    back = [pltpu.roll(entry, LANES - step, 1) for entry in values]
    forth = [pltpu.roll(entry, step, 1) for entry in values]
    count = len(values)
    after = [
        jnp.where(lane >= LANES - step, back[i + 1], back[i]) if i + 1 < count else back[i]
        for i in range(count)
    ]
    before = [jnp.where(lane < step, forth[i - 1], forth[i]) if i else forth[i] for i in range(count)]
    return after, before


def neighbours(field, weights, plane, at, size, step, cache):
    tiles = field.shape[0]

    def level(i, index):
        if cache is None:
            return field[i, index, pl.ds(PAD + at, size), :]
        if (i, index) not in cache:
            cache[i, index] = field[i, index, pl.ds(PAD + at, size), :]
        return cache[i, index]

    def weight(kind, i):
        return weights[kind, i, plane, pl.ds(at, size), :]

    centre = [level(i, plane + 2) for i in range(tiles)]
    after, before = sideways(centre, step)
    result = []
    for i in range(tiles):
        row_after = field[i, plane + 2, pl.ds(PAD + at + step, size), :]
        row_before = field[i, plane + 2, pl.ds(PAD + at - step, size), :]
        deep = weight(AFTER_DEPTH, i) * level(i, plane + 3) + weight(BEFORE_DEPTH, i) * level(
            i, plane + 1
        )
        down = weight(AFTER_ROW, i) * row_after + weight(BEFORE_ROW, i) * row_before
        along = weight(AFTER_COLUMN, i) * after[i] + weight(BEFORE_COLUMN, i) * before[i]
        result.append(((deep + down) + along, centre[i]))
    return result


def set_weights(weights, where, c, scale, drift_scale, tile, tiles, step):
    size = c[0].shape[-2]
    base = scale * c[0]
    for axis in range(3):
        drift = drift_scale * c[axis + 1]
        after, before = base - drift, base + drift
        if axis == 2 and tile == tiles - 1:
            after = jnp.where(lane_index(size) >= LANES - step, 0.0, after)
        if axis == 2 and tile == 0:
            before = jnp.where(lane_index(size) < step, 0.0, before)
        weights[(2 * axis,) + where] = after
        weights[(2 * axis + 1,) + where] = before


def clear_edges(field, first, last):
    tiles, planes = field.shape[:2]
    size = field.shape[2]
    plane = jnp.zeros((tiles, 1, size, LANES), jnp.float32)
    field[:, 1:2] = plane
    field[:, planes - 2 : planes - 1] = plane
    rows = jnp.zeros((tiles, planes - 4, PAD, LANES), jnp.float32)
    field[:, 2 : planes - 2, first : first + PAD, :] = rows
    field[:, 2 : planes - 2, PAD + last : PAD + last + PAD, :] = rows


def fine_scheme():
    scales, carries, tildes = chebyshev_coefficients(SECTIONS)
    centre = INTERVAL / (tildes[1] * FINE_STEP)
    factors = [1.0]
    for degree in range(1, SECTIONS + 1):
        factors.append(factors[-1] * tildes[degree] * FINE_STEP / INTERVAL)
    back = [0.0, 0.0]
    for degree in range(2, SECTIONS + 1):
        back.append(carries[degree] * factors[degree - 2] / factors[degree])
    return centre, back, factors[SECTIONS]


def row_places(box, sizes):
    place, count = lax.axis_index("coarse"), lax.axis_size("coarse")
    odd = place % 2
    result = []
    gone = 0
    for step, size in enumerate(sizes, 1):
        below = pl.multiple_of(box.side - gone - size, 8)
        above = pl.multiple_of(box.side + box.rows + gone, 8)
        gone += size
        one = pl.multiple_of(jnp.where(odd == 1, below, above), 8)
        two = pl.multiple_of(jnp.where(odd == 1, above, below), 8)
        below_valid, above_valid = place >= step, place + step < count
        one_valid = jnp.where(odd == 1, below_valid, above_valid)
        two_valid = jnp.where(odd == 1, above_valid, below_valid)
        result.append(((one, one_valid), (two, two_valid)))
    return result


def place_pieces(box, own_depth, pieces, starts, coeff, weights):
    core = lax.axis_index("tm") % 2
    centre_constant = fine_scheme()[0]
    for own, other, block, blocks, at, valid in pieces:
        shift = lax.axis_index("slab") if blocks == 2 else 0
        base = (block + shift) % blocks * own_depth
        size = own.shape[-2]
        for plane in range(own_depth):
            for i in range(box.tiles):
                cols = slice(i * LANES, (i + 1) * LANES)
                where = (i, base + plane, pl.ds(at, size), slice(None))
                for ref, rank in ((own, core), (other, 1 - core)):
                    for slot, kind in ((2 - 2 * rank, None), (rank, 1 + rank), (1 + rank, 3 * rank)):
                        value = ref[slot, plane, :, cols]
                        if valid is not None:
                            value = jnp.where(valid, value, 0.0)
                        if kind is None:
                            starts[(rank,) + where] = value
                        else:
                            coeff[(kind,) + where] = value
                c = [coeff[(k,) + where] for k in range(4)]
                set_weights(weights, where, c, INTERVAL, 0.5 * INTERVAL, i, box.tiles, 1)
                weights[(CENTRE,) + where] = centre_constant - 6.0 * INTERVAL * c[0]


def early_body(box, own_depth, blocks, *refs):
    starts, coeff, weights = refs[-3:]
    half = (len(refs) - 3) // 2
    own, other = refs[:half], refs[half : 2 * half]
    places = row_places(box, [ref.shape[-2] for ref in own[blocks::2]])
    moves = [(own[block], other[block], block, blocks, box.side, None) for block in range(blocks)]
    for step, pair in enumerate(places):
        for which, (at, valid) in enumerate(pair):
            index = blocks + 2 * step + which
            moves.append((own[index], other[index], 0, blocks, at, valid))
    place_pieces(box, own_depth, moves, starts, coeff, weights)


def fine_body(box, margin, own_depth, blocks, *refs):
    end, starts, coeff, weights, one, two = refs[-6:]
    half = (len(refs) - 9) // 2
    own, other = refs[:half], refs[half : 2 * half]
    core = lax.axis_index("tm") % 2
    moves = []
    if blocks > 1:
        each = half // (blocks - 1)
        places = row_places(box, [ref.shape[-2] for ref in own[0:each:2]])
        for block in range(1, blocks):
            for step, pair in enumerate(places):
                for which, (at, valid) in enumerate(pair):
                    index = (block - 1) * each + 2 * step + which
                    moves.append((own[index], other[index], block, blocks, at, valid))
    place_pieces(box, own_depth, moves, starts, coeff, weights)
    clear_edges(one, 0, box.height)
    clear_edges(two, 0, box.height)
    one[:, 2 : 2 + box.depth, PAD : PAD + box.height, :] = starts[core]
    _, back, factor = fine_scheme()
    stage = 0
    current, other_field = one, two
    first, last = box.span(margin)
    for repeat in range(FINE_STEPS):
        for degree in range(1, SECTIONS + 1):
            stage += 1
            final = stage == FINE_REACH

            def body(plane, at, size, cache, current=current, old=other_field, degree=degree, final=final):
                values = neighbours(current, weights, plane, at, size, 1, cache)
                for i, (total, centre) in enumerate(values):
                    value = total + weights[CENTRE, i, plane, pl.ds(at, size), :] * centre
                    where = (i, plane + 2, pl.ds(PAD + at, size), slice(None))
                    if degree > 1:
                        value = value + back[degree] * old[where]
                    if final:
                        end[i, plane, pl.ds(at - first, size), :] = factor**FINE_STEPS * value
                    else:
                        old[where] = value

            sweep(box.depth, *box.span(margin + FINE_REACH - stage), body)
            current, other_field = other_field, current


def pair_columns(value):
    lane = lane_index(value.shape[0])
    other = jnp.where(
        lane % 2 == 0, pltpu.roll(value, LANES - 1, 1), pltpu.roll(value, 1, 1)
    )
    return value + other


def pair_rows(field, i, plane, at, size):
    row = row_index(size)
    other = jnp.where(
        row % 2 == 0,
        field[i, plane + 2, pl.ds(PAD + at + 1, size), :],
        field[i, plane + 2, pl.ds(PAD + at - 1, size), :],
    )
    return field[i, plane + 2, pl.ds(PAD + at, size), :] + other


def prepare_body(box, coeff, coarse, weight, work):
    half = box.depth // 2
    for k in range(4):
        clear_edges(work.at[k], 0, box.height)

        def columns(plane, at, size, cache, k=k):
            for i in range(box.tiles):
                low = coeff[k, i, 2 * plane, pl.ds(at, size), :]
                high = coeff[k, i, 2 * plane + 1, pl.ds(at, size), :]
                work[k, i, plane + 2, pl.ds(PAD + at, size), :] = pair_columns(low + high)
                if k == 0:
                    for offset, value in ((0, low), (1, high)):
                        weight[i, 2 * plane + offset, pl.ds(at, size), :] = RELAX / (
                            1.0 + 6.0 * INTERVAL * value
                        )

        sweep(half, 0, box.height, columns)

    def rows(plane, at, size, cache):
        for i in range(box.tiles):
            where = (i, plane, pl.ds(at, size), slice(None))
            c = [0.125 * pair_rows(work.at[k], i, plane, at, size) for k in range(4)]
            set_weights(coarse, where, c, INTERVAL / 4.0, INTERVAL / 4.0, i, box.tiles, 2)
            coarse[(CENTRE,) + where] = RELAX / (1.0 + 6.0 * INTERVAL / 4.0 * c[0])

    sweep(half, 0, box.height, rows)


def coarse_step_body(box, margin, source, trial, pairs, guess, residual, params, finish):
    weights, coarse, weight = params
    half = box.depth // 2
    centre_constant = fine_scheme()[0]

    def smooth(plane, at, size, cache):
        values = neighbours(source, weights, plane, at, size, 1, cache)
        for i, (total, centre) in enumerate(values):
            trial[i, plane + 2, pl.ds(PAD + at, size), :] = (1.0 - RELAX) * centre + weight[
                i, plane, pl.ds(at, size), :
            ] * (centre + total)

    first, last = box.span(margin + 5)
    clear_edges(trial, first, last)
    sweep(box.depth, first, last, smooth)

    def restrict(plane, at, size, cache):
        sums = [None] * box.tiles
        for half_plane in range(2):
            fine_plane = 2 * plane + half_plane
            values = neighbours(trial, weights, fine_plane, at, size, 1, cache)
            for i, (total, centre) in enumerate(values):
                given = source[i, fine_plane + 2, pl.ds(PAD + at, size), :]
                inner = weights[CENTRE, i, fine_plane, pl.ds(at, size), :] - (1.0 + centre_constant)
                misfit = (given + total) + inner * centre
                sums[i] = misfit if sums[i] is None else sums[i] + misfit
        for i in range(box.tiles):
            pairs[i, plane + 2, pl.ds(PAD + at, size), :] = sums[i]

    first, last = box.span(margin + 4)
    clear_edges(pairs, first, last)
    sweep(half, first, last, restrict)

    def first_guess(plane, at, size, cache):
        for i in range(box.tiles):
            mean = 0.125 * pair_columns(pair_rows(pairs, i, plane, at, size))
            residual[i, plane + 2, pl.ds(PAD + at, size), :] = mean
            guess[i, plane + 2, pl.ds(PAD + at, size), :] = (
                coarse[CENTRE, i, plane, pl.ds(at, size), :] * mean
            )

    clear_edges(guess, first, last)
    sweep(half, first, last, first_guess)

    def correct(plane, at, size, cache):
        values = neighbours(guess, coarse, plane, at, size, 2, cache)
        for i, (total, centre) in enumerate(values):
            rest = residual[i, plane + 2, pl.ds(PAD + at, size), :] + total
            fix = (1.0 - RELAX) * centre + coarse[CENTRE, i, plane, pl.ds(at, size), :] * rest
            for half_plane in range(2):
                where = (i, 2 * plane + half_plane + 2, pl.ds(PAD + at, size), slice(None))
                trial[where] = trial[where] + fix

    sweep(half, *box.span(margin + 2), correct)

    def smooth_again(plane, at, size, cache):
        values = neighbours(trial, weights, plane, at, size, 1, cache)
        for i, (total, centre) in enumerate(values):
            given = source[i, plane + 2, pl.ds(PAD + at, size), :]
            value = (1.0 - RELAX) * centre + weight[i, plane, pl.ds(at, size), :] * (given + total)
            finish(plane, i, at, size, value)

    sweep(box.depth, *box.span(margin), smooth_again)


def coarse_scratch(box):
    half = box.depth // 2
    return [box.scratch(), box.scratch(half), box.scratch(half), box.scratch(half)]


def pair_body(box, own_end, other_end, starts, *rest):
    params, out, first_out, leaving = rest[:3], rest[3], rest[4], rest[5:7]
    source, trial, pairs, guess, residual = rest[7:]
    core = lax.axis_index("tm") % 2
    first, last = box.span(COARSE_REACH)
    clear_edges(source, first, last)

    def put(first_end, second_end):
        source[:, 2 : 2 + box.depth, PAD + first : PAD + last, :] = (
            first_end[...] - starts[1, :, :, first:last, :]
        )
        inner = slice(box.side - first, box.side - first + box.rows)
        out[...] = second_end[:, :, inner, :]
        first_out[...] = first_end[:, :, inner, :]

    @pl.when(core == 0)
    def _():
        put(own_end, other_end)

    @pl.when(core == 1)
    def _():
        put(other_end, own_end)

    def finish(plane, i, at, size, value):
        where = (i, plane, pl.ds(at - box.side, size), slice(None))
        out[where] = value + out[where]

    coarse_step_body(box, 0, source, trial, pairs, guess, residual, params, finish)
    pack(box, out, *leaving)


def pack(box, field, centre, edge):
    core, place = lax.axis_index("tm") % 2, lax.axis_index("coarse")
    half = box.depth // 2
    centre[...] = field[:, pl.ds(core * half, half)]
    width = edge.shape[1] // box.depth
    up = place % 2 == core
    for i in range(box.tiles):
        for plane in range(box.depth):
            edge[i, plane * width : (plane + 1) * width, :] = jnp.where(
                up, field[i, plane, box.rows - width :, :], field[i, plane, :width, :]
            )


def last_body(box, own_depth, turn, first_end, joined, *rest):
    arrived, rest = rest[:4], rest[4:]
    starts, params, result, leaving = rest[0], rest[1:4], rest[4], rest[5:7]
    source, second, trial, pairs, guess, residual, total = rest[7:]
    place = lax.axis_index("tm")
    core = place % 2
    active = place // 2 == turn
    side, rows = box.side, box.rows
    half = box.depth // 2
    reach = 2 * COARSE_REACH
    clear_edges(source, side - reach, side + rows + reach)
    clear_edges(second, *box.span(COARSE_REACH))

    @pl.when(jnp.logical_not(active))
    def _():
        source[:, 2 : 2 + box.depth, PAD : PAD + box.height, :] = jnp.zeros(
            (box.tiles, box.depth, box.height, LANES), jnp.float32
        )

    @pl.when(active)
    def _():
        centre, edge, other_centre, other_edge = arrived
        for piece, rank in ((centre, core), (other_centre, 1 - core)):
            base = rank * half
            for i in range(box.tiles):
                for plane in range(half):
                    source[i, base + plane + 2, PAD + side : PAD + side + rows, :] = (
                        piece[i, plane] - starts[0, i, base + plane, side : side + rows, :]
                    )
        width = edge.shape[1] // box.depth
        row_place, count = lax.axis_index("coarse"), lax.axis_size("coarse")
        below = row_place % 2 != core

        def edges(low, high):
            for ref, at, valid in (
                (low, side - width, row_place > 0),
                (high, side + rows, row_place < count - 1),
            ):
                for i in range(box.tiles):
                    for plane in range(box.depth):
                        value = ref[i, plane * width : (plane + 1) * width, :]
                        source[i, plane + 2, PAD + at : PAD + at + width, :] = (
                            jnp.where(valid, value, 0.0) - starts[0, i, plane, at : at + width, :]
                        )

        @pl.when(below)
        def _():
            edges(edge, other_edge)

        @pl.when(jnp.logical_not(below))
        def _():
            edges(other_edge, edge)

    def finish_once(plane, i, at, size, value):
        second[i, plane + 2, pl.ds(PAD + at, size), :] = value

    coarse_step_body(
        box, COARSE_REACH, source, trial, pairs, guess, residual, params, finish_once
    )

    def finish_twice(plane, i, at, size, value):
        where = (i, plane, pl.ds(at - box.side, size), slice(None))
        total[where] = value + joined[where]

    coarse_step_body(box, 0, second, trial, pairs, guess, residual, params, finish_twice)
    base = lax.axis_index("slab") * own_depth

    @pl.when(core == 0)
    def _():
        for i in range(box.tiles):
            result[0, :, :, i * LANES : (i + 1) * LANES] = (
                first_end[i, pl.ds(base, own_depth)]
                + second[i, pl.ds(base + 2, own_depth), PAD + side : PAD + side + rows, :]
            )

    @pl.when(core == 1)
    def _():
        for i in range(box.tiles):
            result[0, :, :, i * LANES : (i + 1) * LANES] = total[i, pl.ds(base, own_depth)]

    pack(box, total, *leaving)


def run(body, outs, scratch, *args, aliases={}):
    return pl.pallas_call(
        body,
        out_shape=[jax.ShapeDtypeStruct(shape, jnp.float32) for shape in outs],
        in_specs=[pl.BlockSpec(memory_space=pltpu.VMEM)] * len(args),
        out_specs=[pl.BlockSpec(memory_space=pltpu.VMEM)] * len(outs),
        scratch_shapes=scratch,
        input_output_aliases=aliases,
        compiler_params=pltpu.CompilerParams(vmem_limit_bytes=20 * 1024 * 1024),
    )(*args)


def slab_blocks(block):
    count = lax.axis_size("slab")
    if count == 1:
        return [block]
    if count == 2:
        return [block, lax.ppermute(block, "slab", [(0, 1), (1, 0)])]
    gathered = lax.all_gather(block, "slab", axis=0)
    return [gathered[i] for i in range(count)]


def row_swaps(hop, away):
    windows, count = lax.axis_size("tm"), lax.axis_size("coarse")
    rounds = []
    for first in (0, 1):
        pairs = []
        for place in range(count):
            other = place + 1 if place % 2 == first else place - 1
            for t in range(windows):
                inside = 0 <= other < count
                target = (hop(t), other) if inside else (away(t), place)
                pairs.append((t * count + place, target[0] * count + target[1]))
        rounds.append(pairs)
    return rounds


def row_pieces(block, width, rounds):
    rows = block.shape[-2]
    axis = block.ndim - 2
    both = ("tm", "coarse")
    odd = lax.axis_index("coarse") % 2 == 1
    pieces = []
    up, down = block, block
    left = width
    while left > 0:
        size = min(rows, left)
        if size == rows and up is down:
            send_one = send_two = block
        else:
            high = lax.slice_in_dim(up, up.shape[axis] - size, None, axis=axis)
            low = lax.slice_in_dim(down, 0, size, axis=axis)
            send_one, send_two = jnp.where(odd, low, high), jnp.where(odd, high, low)
        got_one = lax.ppermute(send_one, both, rounds[0])
        got_two = lax.ppermute(send_two, both, rounds[1])
        pieces += [got_one, got_two]
        left -= size
        if left > 0:
            up, down = jnp.where(odd, got_one, got_two), jnp.where(odd, got_two, got_one)
    return pieces


def core_swapped(block):
    count = lax.axis_size("tm")
    assert count % 2 == 0
    return lax.ppermute(block, "tm", [(i, i ^ 1) for i in range(count)])


def per_device(states, diffusivity, velocity):
    windows = lax.axis_size("tm")
    place = lax.axis_index("tm")
    own_depth, rows, columns = diffusivity.shape
    side = round_up(FINE_REACH + COARSE_REACH, 8)
    depth = own_depth * lax.axis_size("slab")
    box = Box(depth, rows, side, columns)
    tiles, height, half = box.tiles, box.height, depth // 2

    second = place % 2 == 1
    slot = lax.broadcasted_iota(jnp.int32, (3, 1, 1, 1), 0)
    parcel = jnp.where(
        (slot == 0) != second, velocity, jnp.where(slot == 1, diffusivity[None], states)
    )
    rounds = row_swaps(lambda t: t, lambda t: t ^ 1)
    blocks = slab_blocks(parcel)
    swapped = [core_swapped(block) for block in blocks]
    near = row_pieces(blocks[0], side, rounds)
    near_swapped = [core_swapped(piece) for piece in near]
    count = len(blocks)
    shapes = [(n, tiles, depth, height, LANES) for n in (2, 4, 7)]
    placed = run(
        functools.partial(early_body, box, own_depth, count),
        shapes,
        [],
        *blocks,
        *near,
        *swapped,
        *near_swapped,
    )
    far = []
    for block in blocks[1:]:
        far += row_pieces(block, side, rounds)
    far += [core_swapped(piece) for piece in far]
    first, last = box.span(COARSE_REACH)
    end, starts, coeff, weights = run(
        functools.partial(fine_body, box, COARSE_REACH, own_depth, count),
        [(tiles, depth, last - first, LANES)] + shapes,
        [box.scratch(), box.scratch()],
        *far,
        *placed,
        aliases={len(far) + n: 1 + n for n in range(3)},
    )
    params = run(
        functools.partial(prepare_body, box),
        [(7, tiles, half, height, LANES), (tiles, depth, height, LANES)],
        [pltpu.VMEM((4, *box.scratch(half).shape), jnp.float32)],
        coeff,
    )
    params = [weights, *params]
    width = 2 * COARSE_REACH
    assert rows >= width
    leaving_shapes = [(tiles, half, rows, LANES), (tiles, depth * width, LANES)]
    joined, first_end, *leaving = run(
        functools.partial(pair_body, box),
        [(tiles, depth, rows, LANES)] * 2 + leaving_shapes,
        [box.scratch()] + coarse_scratch(box),
        end,
        core_swapped(end),
        starts,
        *params,
    )
    ends = jnp.where(place % 2 == 1, joined, first_end)
    ends = jnp.concatenate([ends[i] for i in range(tiles)], axis=-1)
    base = lax.axis_index("slab") * own_depth
    result = lax.dynamic_slice_in_dim(ends, base, own_depth, 0)[None]
    hop = lambda t: (t + 2) % windows
    one, two = row_swaps(hop, hop)
    across = [(t, hop(t)) for t in range(windows)]
    count = lax.axis_size("coarse")
    aside = [
        pair for pairs, core in ((one, 0), (two, 1)) for pair in pairs if pair[0] // count % 2 == core
    ]
    for turn in range(1, windows // 2):
        arrived = [
            lax.ppermute(leaving[0], "tm", across),
            lax.ppermute(leaving[1], ("tm", "coarse"), aside),
        ]
        arrived += [core_swapped(piece) for piece in arrived]
        out, *leaving = run(
            functools.partial(last_body, box, own_depth, turn),
            [(1, own_depth, rows, columns)] + leaving_shapes,
            [box.scratch()] * 2
            + coarse_scratch(box)
            + [pltpu.VMEM((tiles, depth, rows, LANES), jnp.float32)],
            first_end,
            joined,
            *arrived,
            starts,
            *params,
        )
        result = out if turn == 1 else jnp.where(place // 2 >= turn, out, result)
    return result


def solution(mesh):
    return jax.shard_map(
        per_device,
        mesh=mesh,
        in_specs=(
            P("tm", "slab", "coarse", None),
            P("slab", "coarse", None),
            P(None, "slab", "coarse", None),
        ),
        out_specs=P("tm", "slab", "coarse", None),
        check_vma=False,
    )
```

```python
import functools

import jax
import jax.numpy as jnp
from jax import lax
from jax.experimental import pallas as pl
from jax.experimental.pallas import tpu as pltpu
from jax.sharding import PartitionSpec as P

SECTIONS = 4
FINE_STEPS = 2
FINE_STEP = 1.0
RELAX = 0.8
INTERVAL = FINE_STEPS * FINE_STEP
LANES = 128
PAD = 8
COARSE_REACH = 6
FINE_REACH = SECTIONS * FINE_STEPS


def chebyshev_coefficients(sections):
    damping = 0.05
    centre_point = 1.0 + damping / (sections * sections)
    chebyshev = [1.0, centre_point]
    slopes = [0.0, 1.0]
    for degree in range(2, sections + 1):
        chebyshev.append(2.0 * centre_point * chebyshev[degree - 1] - chebyshev[degree - 2])
        slopes.append(
            2.0 * chebyshev[degree - 1]
            + 2.0 * centre_point * slopes[degree - 1]
            - slopes[degree - 2]
        )
    slope_ratio = chebyshev[sections] / slopes[sections]
    weights = [1.0 / entry for entry in chebyshev]
    scales = [0.0, 0.0]
    carries = [0.0, 0.0]
    tildes = [0.0, slope_ratio / centre_point]
    for degree in range(2, sections + 1):
        scales.append(2.0 * weights[degree] * centre_point / weights[degree - 1])
        carries.append(-weights[degree] / weights[degree - 2])
        tildes.append(2.0 * weights[degree] * slope_ratio / weights[degree - 1])
    return (scales, carries, tildes)


def round_up(value, unit):
    return -(-value // unit) * unit


class Box:
    def __init__(self, depth, rows, side, columns):
        self.depth, self.rows, self.side, self.columns = depth, rows, side, columns
        self.height = rows + 2 * side
        self.tiles = columns // LANES

    def scratch(self, depth=None):
        depth = self.depth if depth is None else depth
        return pltpu.VMEM(
            (self.tiles, depth + 4, self.height + 2 * PAD, LANES), jnp.float32
        )

    def span(self, margin):
        size = round_up(self.rows + 2 * margin, 8)
        first = self.side - (size - self.rows) // 2
        assert first >= 0 and first % 2 == 0
        return first, first + size


CHUNK = 16
AFTER_DEPTH, BEFORE_DEPTH, AFTER_ROW, BEFORE_ROW, AFTER_COLUMN, BEFORE_COLUMN, CENTRE = range(7)


def chunks(first, last):
    at = first
    while at < last:
        size = min(CHUNK, last - at)
        yield at, size
        at += size


def sweep(count, first, last, body):
    if count <= 8:
        for at, size in chunks(first, last):
            cache = {}
            for plane in range(count):
                body(plane, at, size, cache)
    else:

        def step(plane, carry):
            for at, size in chunks(first, last):
                body(plane, at, size, None)
            return carry

        lax.fori_loop(0, count, step, 0)


def lane_index(size):
    return lax.broadcasted_iota(jnp.int32, (size, LANES), 1)


def row_index(size):
    return lax.broadcasted_iota(jnp.int32, (size, LANES), 0)


def sideways(values, step):
    lane = lane_index(values[0].shape[0])
    back = [pltpu.roll(entry, LANES - step, 1) for entry in values]
    forth = [pltpu.roll(entry, step, 1) for entry in values]
    count = len(values)
    after = [
        jnp.where(lane >= LANES - step, back[i + 1], back[i]) if i + 1 < count else back[i]
        for i in range(count)
    ]
    before = [jnp.where(lane < step, forth[i - 1], forth[i]) if i else forth[i] for i in range(count)]
    return after, before


def neighbours(field, weights, plane, at, size, step, cache):
    tiles = field.shape[0]

    def level(i, index):
        if cache is None:
            return field[i, index, pl.ds(PAD + at, size), :]
        if (i, index) not in cache:
            cache[i, index] = field[i, index, pl.ds(PAD + at, size), :]
        return cache[i, index]

    def weight(kind, i):
        return weights[kind, i, plane, pl.ds(at, size), :]

    centre = [level(i, plane + 2) for i in range(tiles)]
    after, before = sideways(centre, step)
    result = []
    for i in range(tiles):
        row_after = field[i, plane + 2, pl.ds(PAD + at + step, size), :]
        row_before = field[i, plane + 2, pl.ds(PAD + at - step, size), :]
        deep = weight(AFTER_DEPTH, i) * level(i, plane + 3) + weight(BEFORE_DEPTH, i) * level(
            i, plane + 1
        )
        down = weight(AFTER_ROW, i) * row_after + weight(BEFORE_ROW, i) * row_before
        along = weight(AFTER_COLUMN, i) * after[i] + weight(BEFORE_COLUMN, i) * before[i]
        result.append(((deep + down) + along, centre[i]))
    return result


def set_weights(weights, where, c, scale, drift_scale, tile, tiles, step):
    size = c[0].shape[-2]
    base = scale * c[0]
    for axis in range(3):
        drift = drift_scale * c[axis + 1]
        after, before = base - drift, base + drift
        if axis == 2 and tile == tiles - 1:
            after = jnp.where(lane_index(size) >= LANES - step, 0.0, after)
        if axis == 2 and tile == 0:
            before = jnp.where(lane_index(size) < step, 0.0, before)
        weights[(2 * axis,) + where] = after
        weights[(2 * axis + 1,) + where] = before


def clear_edges(field, first, last):
    tiles, planes = field.shape[:2]
    size = field.shape[2]
    plane = jnp.zeros((tiles, 1, size, LANES), jnp.float32)
    field[:, 1:2] = plane
    field[:, planes - 2 : planes - 1] = plane
    rows = jnp.zeros((tiles, planes - 4, PAD, LANES), jnp.float32)
    field[:, 2 : planes - 2, first : first + PAD, :] = rows
    field[:, 2 : planes - 2, PAD + last : PAD + last + PAD, :] = rows


def fine_scheme():
    scales, carries, tildes = chebyshev_coefficients(SECTIONS)
    centre = INTERVAL / (tildes[1] * FINE_STEP)
    factors = [1.0]
    for degree in range(1, SECTIONS + 1):
        factors.append(factors[-1] * tildes[degree] * FINE_STEP / INTERVAL)
    back = [0.0, 0.0]
    for degree in range(2, SECTIONS + 1):
        back.append(carries[degree] * factors[degree - 2] / factors[degree])
    return centre, back, factors[SECTIONS]


def row_places(box, sizes):
    place, count = lax.axis_index("coarse"), lax.axis_size("coarse")
    odd = place % 2
    result = []
    gone = 0
    for step, size in enumerate(sizes, 1):
        below = pl.multiple_of(box.side - gone - size, 8)
        above = pl.multiple_of(box.side + box.rows + gone, 8)
        gone += size
        one = pl.multiple_of(jnp.where(odd == 1, below, above), 8)
        two = pl.multiple_of(jnp.where(odd == 1, above, below), 8)
        below_valid, above_valid = place >= step, place + step < count
        one_valid = jnp.where(odd == 1, below_valid, above_valid)
        two_valid = jnp.where(odd == 1, above_valid, below_valid)
        result.append(((one, one_valid), (two, two_valid)))
    return result


def place_pieces(box, own_depth, pieces, starts, coeff, weights):
    core = lax.axis_index("tm") % 2
    centre_constant = fine_scheme()[0]
    for own, other, block, blocks, at, valid in pieces:
        shift = lax.axis_index("slab") if blocks == 2 else 0
        base = (block + shift) % blocks * own_depth
        size = own.shape[-2]
        for plane in range(own_depth):
            for i in range(box.tiles):
                cols = slice(i * LANES, (i + 1) * LANES)
                where = (i, base + plane, pl.ds(at, size), slice(None))
                for ref, rank in ((own, core), (other, 1 - core)):
                    for slot, kind in ((2 - 2 * rank, None), (rank, 1 + rank), (1 + rank, 3 * rank)):
                        value = ref[slot, plane, :, cols]
                        if valid is not None:
                            value = jnp.where(valid, value, 0.0)
                        if kind is None:
                            starts[(rank,) + where] = value
                        else:
                            coeff[(kind,) + where] = value
                c = [coeff[(k,) + where] for k in range(4)]
                set_weights(weights, where, c, INTERVAL, 0.5 * INTERVAL, i, box.tiles, 1)
                weights[(CENTRE,) + where] = centre_constant - 6.0 * INTERVAL * c[0]


def early_body(box, own_depth, blocks, *refs):
    starts, coeff, weights = refs[-3:]
    half = (len(refs) - 3) // 2
    own, other = refs[:half], refs[half : 2 * half]
    places = row_places(box, [ref.shape[-2] for ref in own[blocks::2]])
    moves = [(own[block], other[block], block, blocks, box.side, None) for block in range(blocks)]
    for step, pair in enumerate(places):
        for which, (at, valid) in enumerate(pair):
            index = blocks + 2 * step + which
            moves.append((own[index], other[index], 0, blocks, at, valid))
    place_pieces(box, own_depth, moves, starts, coeff, weights)


def late_moves(box, blocks, own, other, which):
    if blocks == 1:
        return []
    steps = len(own) // (blocks - 1)
    places = row_places(box, [ref.shape[-2] for ref in own[:steps]])
    return [
        (own[n], other[n], 1 + n // steps, blocks, *places[n % steps][which]) for n in range(len(own))
    ]


def late_body(box, own_depth, blocks, *refs):
    half = (len(refs) - 6) // 2
    moves = late_moves(box, blocks, refs[:half], refs[half : 2 * half], 1)
    place_pieces(box, own_depth, moves, *refs[-3:])


def fine_body(box, margin, own_depth, blocks, *refs):
    end, starts, coeff, weights, one, two = refs[-6:]
    half = (len(refs) - 9) // 2
    core = lax.axis_index("tm") % 2
    moves = late_moves(box, blocks, refs[:half], refs[half : 2 * half], 0)
    place_pieces(box, own_depth, moves, starts, coeff, weights)
    clear_edges(one, 0, box.height)
    clear_edges(two, 0, box.height)
    one[:, 2 : 2 + box.depth, PAD : PAD + box.height, :] = starts[core]
    _, back, factor = fine_scheme()
    stage = 0
    current, other_field = one, two
    first, last = box.span(margin)
    for repeat in range(FINE_STEPS):
        for degree in range(1, SECTIONS + 1):
            stage += 1
            final = stage == FINE_REACH

            def body(plane, at, size, cache, current=current, old=other_field, degree=degree, final=final):
                values = neighbours(current, weights, plane, at, size, 1, cache)
                for i, (total, centre) in enumerate(values):
                    value = total + weights[CENTRE, i, plane, pl.ds(at, size), :] * centre
                    where = (i, plane + 2, pl.ds(PAD + at, size), slice(None))
                    if degree > 1:
                        value = value + back[degree] * old[where]
                    if final:
                        end[i, plane, pl.ds(at - first, size), :] = factor**FINE_STEPS * value
                    else:
                        old[where] = value

            sweep(box.depth, *box.span(margin + FINE_REACH - stage), body)
            current, other_field = other_field, current


def pair_columns(value):
    lane = lane_index(value.shape[0])
    other = jnp.where(
        lane % 2 == 0, pltpu.roll(value, LANES - 1, 1), pltpu.roll(value, 1, 1)
    )
    return value + other


def pair_rows(field, i, plane, at, size):
    row = row_index(size)
    other = jnp.where(
        row % 2 == 0,
        field[i, plane + 2, pl.ds(PAD + at + 1, size), :],
        field[i, plane + 2, pl.ds(PAD + at - 1, size), :],
    )
    return field[i, plane + 2, pl.ds(PAD + at, size), :] + other


def prepare_body(box, coeff, coarse, weight, work):
    half = box.depth // 2
    for k in range(4):
        clear_edges(work.at[k], 0, box.height)

        def columns(plane, at, size, cache, k=k):
            for i in range(box.tiles):
                low = coeff[k, i, 2 * plane, pl.ds(at, size), :]
                high = coeff[k, i, 2 * plane + 1, pl.ds(at, size), :]
                work[k, i, plane + 2, pl.ds(PAD + at, size), :] = pair_columns(low + high)
                if k == 0:
                    for offset, value in ((0, low), (1, high)):
                        weight[i, 2 * plane + offset, pl.ds(at, size), :] = RELAX / (
                            1.0 + 6.0 * INTERVAL * value
                        )

        sweep(half, 0, box.height, columns)

    def rows(plane, at, size, cache):
        for i in range(box.tiles):
            where = (i, plane, pl.ds(at, size), slice(None))
            c = [0.125 * pair_rows(work.at[k], i, plane, at, size) for k in range(4)]
            set_weights(coarse, where, c, INTERVAL / 4.0, INTERVAL / 4.0, i, box.tiles, 2)
            coarse[(CENTRE,) + where] = RELAX / (1.0 + 6.0 * INTERVAL / 4.0 * c[0])

    sweep(half, 0, box.height, rows)


def coarse_step_body(
    box, margin, source, trial, pairs, guess, residual, params, finish, base=0, planes=None
):
    weights, coarse, weight = params
    half = box.depth // 2
    centre_constant = fine_scheme()[0]

    def smooth(plane, at, size, cache):
        values = neighbours(source, weights, plane, at, size, 1, cache)
        for i, (total, centre) in enumerate(values):
            trial[i, plane + 2, pl.ds(PAD + at, size), :] = (1.0 - RELAX) * centre + weight[
                i, plane, pl.ds(at, size), :
            ] * (centre + total)

    first, last = box.span(margin + 5)
    clear_edges(trial, first, last)
    sweep(box.depth, first, last, smooth)

    def restrict(plane, at, size, cache):
        sums = [None] * box.tiles
        for half_plane in range(2):
            fine_plane = 2 * plane + half_plane
            values = neighbours(trial, weights, fine_plane, at, size, 1, cache)
            for i, (total, centre) in enumerate(values):
                given = source[i, fine_plane + 2, pl.ds(PAD + at, size), :]
                inner = weights[CENTRE, i, fine_plane, pl.ds(at, size), :] - (1.0 + centre_constant)
                misfit = (given + total) + inner * centre
                sums[i] = misfit if sums[i] is None else sums[i] + misfit
        for i in range(box.tiles):
            pairs[i, plane + 2, pl.ds(PAD + at, size), :] = sums[i]

    first, last = box.span(margin + 4)
    clear_edges(pairs, first, last)
    sweep(half, first, last, restrict)

    def first_guess(plane, at, size, cache):
        for i in range(box.tiles):
            mean = 0.125 * pair_columns(pair_rows(pairs, i, plane, at, size))
            residual[i, plane + 2, pl.ds(PAD + at, size), :] = mean
            guess[i, plane + 2, pl.ds(PAD + at, size), :] = (
                coarse[CENTRE, i, plane, pl.ds(at, size), :] * mean
            )

    clear_edges(guess, first, last)
    sweep(half, first, last, first_guess)

    def correct(plane, at, size, cache):
        values = neighbours(guess, coarse, plane, at, size, 2, cache)
        for i, (total, centre) in enumerate(values):
            rest = residual[i, plane + 2, pl.ds(PAD + at, size), :] + total
            fix = (1.0 - RELAX) * centre + coarse[CENTRE, i, plane, pl.ds(at, size), :] * rest
            for half_plane in range(2):
                where = (i, 2 * plane + half_plane + 2, pl.ds(PAD + at, size), slice(None))
                trial[where] = trial[where] + fix

    sweep(half, *box.span(margin + 2), correct)

    def smooth_again(plane, at, size, cache):
        values = neighbours(trial, weights, plane, at, size, 1, cache)
        for i, (total, centre) in enumerate(values):
            given = source[i, plane + 2, pl.ds(PAD + at, size), :]
            value = (1.0 - RELAX) * centre + weight[i, plane, pl.ds(at, size), :] * (given + total)
            finish(plane, i, at, size, value)

    if planes is None:
        sweep(box.depth, *box.span(margin), smooth_again)
    else:
        sweep(
            planes,
            *box.span(margin),
            lambda plane, at, size, cache: smooth_again(base + plane, at, size, None),
        )


def coarse_scratch(box):
    half = box.depth // 2
    return [box.scratch(), box.scratch(half), box.scratch(half), box.scratch(half)]


def pair_body(box, own_end, other_end, starts, *rest):
    params, out, first_out, leaving = rest[:3], rest[3], rest[4], rest[5:7]
    source, trial, pairs, guess, residual = rest[7:]
    core = lax.axis_index("tm") % 2
    first, last = box.span(COARSE_REACH)
    clear_edges(source, first, last)

    def put(first_end, second_end):
        source[:, 2 : 2 + box.depth, PAD + first : PAD + last, :] = (
            first_end[...] - starts[1, :, :, first:last, :]
        )
        inner = slice(box.side - first, box.side - first + box.rows)
        out[...] = second_end[:, :, inner, :]
        first_out[...] = first_end[:, :, inner, :]

    @pl.when(core == 0)
    def _():
        put(own_end, other_end)

    @pl.when(core == 1)
    def _():
        put(other_end, own_end)

    def finish(plane, i, at, size, value):
        where = (i, plane, pl.ds(at - box.side, size), slice(None))
        out[where] = value + out[where]

    coarse_step_body(box, 0, source, trial, pairs, guess, residual, params, finish)
    pack(box, out, *leaving)


def pack(box, field, centre, edge):
    core, place = lax.axis_index("tm") % 2, lax.axis_index("coarse")
    half = box.depth // 2
    centre[...] = field[:, pl.ds(core * half, half)]
    width = edge.shape[1] // box.depth
    up = place % 2 == core
    for i in range(box.tiles):
        for plane in range(box.depth):
            edge[i, plane * width : (plane + 1) * width, :] = jnp.where(
                up, field[i, plane, box.rows - width :, :], field[i, plane, :width, :]
            )


def last_body(box, own_depth, turn, final, first_end, joined, *rest):
    arrived, rest = rest[:4], rest[4:]
    starts, params, result, leaving = rest[0], rest[1:4], rest[4], rest[5:-7]
    source, second, trial, pairs, guess, residual, total = rest[-7:]
    place = lax.axis_index("tm")
    core = place % 2
    active = place // 2 == turn
    side, rows = box.side, box.rows
    half = box.depth // 2
    reach = 2 * COARSE_REACH
    clear_edges(source, side - reach, side + rows + reach)
    clear_edges(second, *box.span(COARSE_REACH))

    @pl.when(jnp.logical_not(active))
    def _():
        source[:, 2 : 2 + box.depth, PAD : PAD + box.height, :] = jnp.zeros(
            (box.tiles, box.depth, box.height, LANES), jnp.float32
        )

    @pl.when(active)
    def _():
        centre, edge, other_centre, other_edge = arrived
        for piece, rank in ((centre, core), (other_centre, 1 - core)):
            base = rank * half
            for i in range(box.tiles):
                for plane in range(half):
                    source[i, base + plane + 2, PAD + side : PAD + side + rows, :] = (
                        piece[i, plane] - starts[0, i, base + plane, side : side + rows, :]
                    )
        width = edge.shape[1] // box.depth
        row_place, count = lax.axis_index("coarse"), lax.axis_size("coarse")
        below = row_place % 2 != core

        def edges(low, high):
            for ref, at, valid in (
                (low, side - width, row_place > 0),
                (high, side + rows, row_place < count - 1),
            ):
                for i in range(box.tiles):
                    for plane in range(box.depth):
                        value = ref[i, plane * width : (plane + 1) * width, :]
                        source[i, plane + 2, PAD + at : PAD + at + width, :] = (
                            jnp.where(valid, value, 0.0) - starts[0, i, plane, at : at + width, :]
                        )

        @pl.when(below)
        def _():
            edges(edge, other_edge)

        @pl.when(jnp.logical_not(below))
        def _():
            edges(other_edge, edge)

    def finish_once(plane, i, at, size, value):
        second[i, plane + 2, pl.ds(PAD + at, size), :] = value

    coarse_step_body(
        box, COARSE_REACH, source, trial, pairs, guess, residual, params, finish_once
    )

    base = lax.axis_index("slab") * own_depth
    if final:

        def finish_result(plane, i, at, size, value):
            where = (i, plane, pl.ds(at - side, size), slice(None))
            once = second[i, plane + 2, pl.ds(PAD + at, size), :]
            result[0, plane - base, pl.ds(at - side, size), i * LANES : (i + 1) * LANES] = jnp.where(
                core == 1, value + joined[where], once + first_end[where]
            )

        coarse_step_body(
            box, 0, second, trial, pairs, guess, residual, params, finish_result, base, own_depth
        )
        return

    def finish_twice(plane, i, at, size, value):
        where = (i, plane, pl.ds(at - box.side, size), slice(None))
        total[where] = value + joined[where]

    coarse_step_body(box, 0, second, trial, pairs, guess, residual, params, finish_twice)

    @pl.when(core == 0)
    def _():
        for i in range(box.tiles):
            result[0, :, :, i * LANES : (i + 1) * LANES] = (
                first_end[i, pl.ds(base, own_depth)]
                + second[i, pl.ds(base + 2, own_depth), PAD + side : PAD + side + rows, :]
            )

    @pl.when(core == 1)
    def _():
        for i in range(box.tiles):
            result[0, :, :, i * LANES : (i + 1) * LANES] = total[i, pl.ds(base, own_depth)]

    pack(box, total, *leaving)


def run(body, outs, scratch, *args, aliases={}):
    return pl.pallas_call(
        body,
        out_shape=[jax.ShapeDtypeStruct(shape, jnp.float32) for shape in outs],
        in_specs=[pl.BlockSpec(memory_space=pltpu.VMEM)] * len(args),
        out_specs=[pl.BlockSpec(memory_space=pltpu.VMEM)] * len(outs),
        scratch_shapes=scratch,
        input_output_aliases=aliases,
        compiler_params=pltpu.CompilerParams(vmem_limit_bytes=20 * 1024 * 1024),
    )(*args)


def slab_blocks(block):
    count = lax.axis_size("slab")
    if count == 1:
        return [block]
    if count == 2:
        return [block, lax.ppermute(block, "slab", [(0, 1), (1, 0)])]
    gathered = lax.all_gather(block, "slab", axis=0)
    return [gathered[i] for i in range(count)]


def row_swaps(hop, away):
    windows, count = lax.axis_size("tm"), lax.axis_size("coarse")
    rounds = []
    for first in (0, 1):
        pairs = []
        for place in range(count):
            other = place + 1 if place % 2 == first else place - 1
            for t in range(windows):
                inside = 0 <= other < count
                target = (hop(t), other) if inside else (away(t), place)
                pairs.append((t * count + place, target[0] * count + target[1]))
        rounds.append(pairs)
    return rounds


def row_pieces(block, width, rounds):
    rows = block.shape[-2]
    axis = block.ndim - 2
    both = ("tm", "coarse")
    odd = lax.axis_index("coarse") % 2 == 1
    pieces = []
    up, down = block, block
    left = width
    while left > 0:
        size = min(rows, left)
        if size == rows and up is down:
            send_one = send_two = block
        else:
            high = lax.slice_in_dim(up, up.shape[axis] - size, None, axis=axis)
            low = lax.slice_in_dim(down, 0, size, axis=axis)
            send_one, send_two = jnp.where(odd, low, high), jnp.where(odd, high, low)
        got_one = lax.ppermute(send_one, both, rounds[0])
        got_two = lax.ppermute(send_two, both, rounds[1])
        pieces += [got_one, got_two]
        left -= size
        if left > 0:
            up, down = jnp.where(odd, got_one, got_two), jnp.where(odd, got_two, got_one)
    return pieces


def core_swapped(block):
    count = lax.axis_size("tm")
    assert count % 2 == 0
    return lax.ppermute(block, "tm", [(i, i ^ 1) for i in range(count)])


def per_device(states, diffusivity, velocity):
    windows = lax.axis_size("tm")
    place = lax.axis_index("tm")
    own_depth, rows, columns = diffusivity.shape
    side = round_up(FINE_REACH + COARSE_REACH, 8)
    depth = own_depth * lax.axis_size("slab")
    box = Box(depth, rows, side, columns)
    tiles, height, half = box.tiles, box.height, depth // 2

    second = place % 2 == 1
    slot = lax.broadcasted_iota(jnp.int32, (3, 1, 1, 1), 0)
    parcel = jnp.where(
        (slot == 0) != second, velocity, jnp.where(slot == 1, diffusivity[None], states)
    )
    rounds = row_swaps(lambda t: t, lambda t: t ^ 1)
    blocks = slab_blocks(parcel)
    swapped = [core_swapped(block) for block in blocks]
    near = row_pieces(blocks[0], side, rounds)
    near_swapped = [core_swapped(piece) for piece in near]
    count = len(blocks)
    shapes = [(n, tiles, depth, height, LANES) for n in (2, 4, 7)]
    placed = run(
        functools.partial(early_body, box, own_depth, count),
        shapes,
        [],
        *blocks,
        *near,
        *swapped,
        *near_swapped,
    )
    far = []
    for block in blocks[1:]:
        far += row_pieces(block, side, rounds)
    far = [piece for which in (1, 0) for piece in far[which::2]]
    far_swapped = [core_swapped(piece) for piece in far]
    cut = len(far) // 2
    if far:
        placed = run(
            functools.partial(late_body, box, own_depth, count),
            shapes,
            [],
            *far[:cut],
            *far_swapped[:cut],
            *placed,
            aliases={2 * cut + n: n for n in range(3)},
        )
    first, last = box.span(COARSE_REACH)
    end, starts, coeff, weights = run(
        functools.partial(fine_body, box, COARSE_REACH, own_depth, count),
        [(tiles, depth, last - first, LANES)] + shapes,
        [box.scratch(), box.scratch()],
        *far[cut:],
        *far_swapped[cut:],
        *placed,
        aliases={2 * cut + n: 1 + n for n in range(3)},
    )
    params = run(
        functools.partial(prepare_body, box),
        [(7, tiles, half, height, LANES), (tiles, depth, height, LANES)],
        [pltpu.VMEM((4, *box.scratch(half).shape), jnp.float32)],
        coeff,
    )
    params = [weights, *params]
    width = 2 * COARSE_REACH
    assert rows >= width
    leaving_shapes = [(tiles, half, rows, LANES), (tiles, depth * width, LANES)]
    joined, first_end, *leaving = run(
        functools.partial(pair_body, box),
        [(tiles, depth, rows, LANES)] * 2 + leaving_shapes,
        [box.scratch()] + coarse_scratch(box),
        end,
        core_swapped(end),
        starts,
        *params,
    )
    ends = jnp.where(place % 2 == 1, joined, first_end)
    ends = jnp.concatenate([ends[i] for i in range(tiles)], axis=-1)
    base = lax.axis_index("slab") * own_depth
    result = lax.dynamic_slice_in_dim(ends, base, own_depth, 0)[None]
    hop = lambda t: (t + 2) % windows
    one, two = row_swaps(hop, hop)
    across = [(t, hop(t)) for t in range(windows)]
    count = lax.axis_size("coarse")
    aside = [
        pair for pairs, core in ((one, 0), (two, 1)) for pair in pairs if pair[0] // count % 2 == core
    ]
    for turn in range(1, windows // 2):
        arrived = [
            lax.ppermute(leaving[0], "tm", across),
            lax.ppermute(leaving[1], ("tm", "coarse"), aside),
        ]
        arrived += [core_swapped(piece) for piece in arrived]
        final = turn == windows // 2 - 1
        out, *leaving = run(
            functools.partial(last_body, box, own_depth, turn, final),
            [(1, own_depth, rows, columns)] + ([] if final else leaving_shapes),
            [box.scratch()] * 2
            + coarse_scratch(box)
            + [pltpu.VMEM((tiles, depth, rows, LANES), jnp.float32)],
            first_end,
            joined,
            *arrived,
            starts,
            *params,
        )
        result = out if turn == 1 else jnp.where(place // 2 >= turn, out, result)
    return result


def solution(mesh):
    return jax.shard_map(
        per_device,
        mesh=mesh,
        in_specs=(
            P("tm", "slab", "coarse", None),
            P("slab", "coarse", None),
            P(None, "slab", "coarse", None),
        ),
        out_specs=P("tm", "slab", "coarse", None),
        check_vma=False,
    )
```

```python
import functools

import jax
import jax.numpy as jnp
from jax import lax
from jax.experimental import pallas as pl
from jax.experimental.pallas import tpu as pltpu
from jax.sharding import PartitionSpec as P

SECTIONS = 4
FINE_STEPS = 2
FINE_STEP = 1.0
RELAX = 0.8
INTERVAL = FINE_STEPS * FINE_STEP
LANES = 128
PAD = 8
COARSE_REACH = 6
FINE_REACH = SECTIONS * FINE_STEPS


def chebyshev_coefficients(sections):
    damping = 0.05
    centre_point = 1.0 + damping / (sections * sections)
    chebyshev = [1.0, centre_point]
    slopes = [0.0, 1.0]
    for degree in range(2, sections + 1):
        chebyshev.append(2.0 * centre_point * chebyshev[degree - 1] - chebyshev[degree - 2])
        slopes.append(
            2.0 * chebyshev[degree - 1]
            + 2.0 * centre_point * slopes[degree - 1]
            - slopes[degree - 2]
        )
    slope_ratio = chebyshev[sections] / slopes[sections]
    weights = [1.0 / entry for entry in chebyshev]
    scales = [0.0, 0.0]
    carries = [0.0, 0.0]
    tildes = [0.0, slope_ratio / centre_point]
    for degree in range(2, sections + 1):
        scales.append(2.0 * weights[degree] * centre_point / weights[degree - 1])
        carries.append(-weights[degree] / weights[degree - 2])
        tildes.append(2.0 * weights[degree] * slope_ratio / weights[degree - 1])
    return (scales, carries, tildes)


def round_up(value, unit):
    return -(-value // unit) * unit


class Box:
    def __init__(self, depth, rows, side, columns):
        self.depth, self.rows, self.side, self.columns = depth, rows, side, columns
        self.height = rows + 2 * side
        self.tiles = columns // LANES

    def scratch(self, depth=None):
        depth = self.depth if depth is None else depth
        return pltpu.VMEM(
            (self.tiles, depth + 4, self.height + 2 * PAD, LANES), jnp.float32
        )

    def span(self, margin):
        size = round_up(self.rows + 2 * margin, 8)
        first = self.side - (size - self.rows) // 2
        assert first >= 0 and first % 2 == 0
        return first, first + size


CHUNK = 8
FINE_CHUNK = 24
AFTER_DEPTH, BEFORE_DEPTH, AFTER_ROW, BEFORE_ROW, AFTER_COLUMN, BEFORE_COLUMN, CENTRE = range(7)


def chunks(first, last, most):
    at = first
    while at < last:
        size = min(most, last - at)
        yield at, size
        at += size


def sweep(count, first, last, body, most=CHUNK):
    if count <= 8:
        for at, size in chunks(first, last, most):
            cache = {}
            for plane in range(count):
                body(plane, at, size, cache)
    else:

        def step(plane, carry):
            for at, size in chunks(first, last, most):
                body(plane, at, size, None)
            return carry

        lax.fori_loop(0, count, step, 0)


def lane_index(size):
    return lax.broadcasted_iota(jnp.int32, (size, LANES), 1)


def row_index(size):
    return lax.broadcasted_iota(jnp.int32, (size, LANES), 0)


def sideways(values, step):
    lane = lane_index(values[0].shape[0])
    back = [pltpu.roll(entry, LANES - step, 1) for entry in values]
    forth = [pltpu.roll(entry, step, 1) for entry in values]
    count = len(values)
    after = [
        jnp.where(lane >= LANES - step, back[i + 1], back[i]) if i + 1 < count else back[i]
        for i in range(count)
    ]
    before = [jnp.where(lane < step, forth[i - 1], forth[i]) if i else forth[i] for i in range(count)]
    return after, before


def neighbours(field, weights, plane, at, size, step, cache):
    tiles = field.shape[0]

    def level(i, index):
        if cache is None:
            return field[i, index, pl.ds(PAD + at, size), :]
        if (i, index) not in cache:
            cache[i, index] = field[i, index, pl.ds(PAD + at, size), :]
        return cache[i, index]

    def weight(kind, i):
        return weights[kind, i, plane, pl.ds(at, size), :]

    centre = [level(i, plane + 2) for i in range(tiles)]
    after, before = sideways(centre, step)
    result = []
    for i in range(tiles):
        row_after = field[i, plane + 2, pl.ds(PAD + at + step, size), :]
        row_before = field[i, plane + 2, pl.ds(PAD + at - step, size), :]
        deep = weight(AFTER_DEPTH, i) * level(i, plane + 3) + weight(BEFORE_DEPTH, i) * level(
            i, plane + 1
        )
        down = weight(AFTER_ROW, i) * row_after + weight(BEFORE_ROW, i) * row_before
        along = weight(AFTER_COLUMN, i) * after[i] + weight(BEFORE_COLUMN, i) * before[i]
        result.append(((deep + down) + along, centre[i]))
    return result


def set_weights(weights, where, c, scale, drift_scale, tile, tiles, step):
    size = c[0].shape[-2]
    base = scale * c[0]
    for axis in range(3):
        drift = drift_scale * c[axis + 1]
        after, before = base - drift, base + drift
        if axis == 2 and tile == tiles - 1:
            after = jnp.where(lane_index(size) >= LANES - step, 0.0, after)
        if axis == 2 and tile == 0:
            before = jnp.where(lane_index(size) < step, 0.0, before)
        weights[(2 * axis,) + where] = after
        weights[(2 * axis + 1,) + where] = before


def clear_ends(field, first, last):
    tiles, planes = field.shape[:2]
    plane = jnp.zeros((tiles, 1, last - first, LANES), jnp.float32)
    field[:, 1:2, PAD + first : PAD + last, :] = plane
    field[:, planes - 2 : planes - 1, PAD + first : PAD + last, :] = plane


def fine_scheme():
    scales, carries, tildes = chebyshev_coefficients(SECTIONS)
    centre = INTERVAL / (tildes[1] * FINE_STEP)
    factors = [1.0]
    for degree in range(1, SECTIONS + 1):
        factors.append(factors[-1] * tildes[degree] * FINE_STEP / INTERVAL)
    back = [0.0, 0.0]
    for degree in range(2, SECTIONS + 1):
        back.append(carries[degree] * factors[degree - 2] / factors[degree])
    return centre, back, factors[SECTIONS]


def row_places(box, sizes):
    place, count = lax.axis_index("coarse"), lax.axis_size("coarse")
    odd = place % 2
    result = []
    gone = 0
    for step, size in enumerate(sizes, 1):
        below = pl.multiple_of(box.side - gone - size, 8)
        above = pl.multiple_of(box.side + box.rows + gone, 8)
        gone += size
        one = pl.multiple_of(jnp.where(odd == 1, below, above), 8)
        two = pl.multiple_of(jnp.where(odd == 1, above, below), 8)
        below_valid, above_valid = place >= step, place + step < count
        one_valid = jnp.where(odd == 1, below_valid, above_valid)
        two_valid = jnp.where(odd == 1, above_valid, below_valid)
        result.append(((one, one_valid), (two, two_valid)))
    return result


def place_pieces(box, own_depth, pieces, starts, coeff, weights):
    core = lax.axis_index("tm") % 2
    centre_constant = fine_scheme()[0]
    for own, other, block, blocks, at, valid in pieces:
        shift = lax.axis_index("slab") if blocks == 2 else 0
        base = (block + shift) % blocks * own_depth
        size = own.shape[-2]
        for plane in range(own_depth):
            for i in range(box.tiles):
                cols = slice(i * LANES, (i + 1) * LANES)
                where = (i, base + plane, pl.ds(at, size), slice(None))
                for ref, rank in ((own, core), (other, 1 - core)):
                    for slot, kind in ((2 - 2 * rank, None), (rank, 1 + rank), (1 + rank, 3 * rank)):
                        value = ref[slot, plane, :, cols]
                        if valid is not None:
                            value = jnp.where(valid, value, 0.0)
                        if kind is None:
                            starts[(rank,) + where] = value
                        else:
                            coeff[(kind,) + where] = value
                c = [coeff[(k,) + where] for k in range(4)]
                set_weights(weights, where, c, INTERVAL, 0.5 * INTERVAL, i, box.tiles, 1)
                weights[(CENTRE,) + where] = centre_constant - 6.0 * INTERVAL * c[0]


def early_body(box, own_depth, blocks, *refs):
    starts, coeff, weights = refs[-3:]
    half = (len(refs) - 3) // 2
    own, other = refs[:half], refs[half : 2 * half]
    places = row_places(box, [ref.shape[-2] for ref in own[blocks::2]])
    moves = [(own[block], other[block], block, blocks, box.side, None) for block in range(blocks)]
    for step, pair in enumerate(places):
        for which, (at, valid) in enumerate(pair):
            index = blocks + 2 * step + which
            moves.append((own[index], other[index], 0, blocks, at, valid))
    place_pieces(box, own_depth, moves, starts, coeff, weights)


def late_moves(box, blocks, own, other, which):
    if blocks == 1:
        return []
    steps = len(own) // (blocks - 1)
    places = row_places(box, [ref.shape[-2] for ref in own[:steps]])
    return [
        (own[n], other[n], 1 + n // steps, blocks, *places[n % steps][which]) for n in range(len(own))
    ]


def late_body(box, own_depth, blocks, *refs):
    half = (len(refs) - 6) // 2
    moves = late_moves(box, blocks, refs[:half], refs[half : 2 * half], 1)
    place_pieces(box, own_depth, moves, *refs[-3:])


def fine_body(box, margin, own_depth, blocks, *refs):
    end, starts, coeff, weights, one, two = refs[-6:]
    half = (len(refs) - 9) // 2
    core = lax.axis_index("tm") % 2
    moves = late_moves(box, blocks, refs[:half], refs[half : 2 * half], 0)
    place_pieces(box, own_depth, moves, starts, coeff, weights)
    clear_ends(one, 0, box.height)
    clear_ends(two, 0, box.height)
    one[:, 2 : 2 + box.depth, PAD : PAD + box.height, :] = starts[core]
    _, back, factor = fine_scheme()
    stage = 0
    current, other_field = one, two
    first, last = box.span(margin)
    for repeat in range(FINE_STEPS):
        for degree in range(1, SECTIONS + 1):
            stage += 1
            final = stage == FINE_REACH

            def body(plane, at, size, cache, current=current, old=other_field, degree=degree, final=final):
                values = neighbours(current, weights, plane, at, size, 1, cache)
                for i, (total, centre) in enumerate(values):
                    value = total + weights[CENTRE, i, plane, pl.ds(at, size), :] * centre
                    where = (i, plane + 2, pl.ds(PAD + at, size), slice(None))
                    if degree > 1:
                        value = value + back[degree] * old[where]
                    if final:
                        end[i, plane, pl.ds(at - first, size), :] = factor**FINE_STEPS * value
                    else:
                        old[where] = value

            sweep(box.depth, *box.span(margin + FINE_REACH - stage), body, FINE_CHUNK)
            current, other_field = other_field, current


def pair_columns(value):
    lane = lane_index(value.shape[0])
    other = jnp.where(
        lane % 2 == 0, pltpu.roll(value, LANES - 1, 1), pltpu.roll(value, 1, 1)
    )
    return value + other


def pair_rows(field, i, plane, at, size):
    row = row_index(size)
    other = jnp.where(
        row % 2 == 0,
        field[i, plane + 2, pl.ds(PAD + at + 1, size), :],
        field[i, plane + 2, pl.ds(PAD + at - 1, size), :],
    )
    return field[i, plane + 2, pl.ds(PAD + at, size), :] + other


def prepare_body(box, coeff, coarse, weight, work):
    half = box.depth // 2
    for k in range(4):
        def columns(plane, at, size, cache, k=k):
            for i in range(box.tiles):
                low = coeff[k, i, 2 * plane, pl.ds(at, size), :]
                high = coeff[k, i, 2 * plane + 1, pl.ds(at, size), :]
                work[k, i, plane + 2, pl.ds(PAD + at, size), :] = pair_columns(low + high)
                if k == 0:
                    for offset, value in ((0, low), (1, high)):
                        weight[i, 2 * plane + offset, pl.ds(at, size), :] = RELAX / (
                            1.0 + 6.0 * INTERVAL * value
                        )

        sweep(half, 0, box.height, columns)

    def rows(plane, at, size, cache):
        for i in range(box.tiles):
            where = (i, plane, pl.ds(at, size), slice(None))
            c = [0.125 * pair_rows(work.at[k], i, plane, at, size) for k in range(4)]
            set_weights(coarse, where, c, INTERVAL / 4.0, INTERVAL / 4.0, i, box.tiles, 2)
            coarse[(CENTRE,) + where] = RELAX / (1.0 + 6.0 * INTERVAL / 4.0 * c[0])

    sweep(half, 0, box.height, rows)


def coarse_step_body(
    box, margin, source, trial, pairs, guess, residual, params, finish, base=0, planes=None
):
    weights, coarse, weight = params
    half = box.depth // 2
    centre_constant = fine_scheme()[0]

    def smooth(plane, at, size, cache):
        values = neighbours(source, weights, plane, at, size, 1, cache)
        for i, (total, centre) in enumerate(values):
            trial[i, plane + 2, pl.ds(PAD + at, size), :] = (1.0 - RELAX) * centre + weight[
                i, plane, pl.ds(at, size), :
            ] * (centre + total)

    first, last = box.span(margin + 5)
    clear_ends(trial, first, last)
    sweep(box.depth, first, last, smooth)

    def restrict(plane, at, size, cache):
        sums = [None] * box.tiles
        for half_plane in range(2):
            fine_plane = 2 * plane + half_plane
            values = neighbours(trial, weights, fine_plane, at, size, 1, cache)
            for i, (total, centre) in enumerate(values):
                given = source[i, fine_plane + 2, pl.ds(PAD + at, size), :]
                inner = weights[CENTRE, i, fine_plane, pl.ds(at, size), :] - (1.0 + centre_constant)
                misfit = (given + total) + inner * centre
                sums[i] = misfit if sums[i] is None else sums[i] + misfit
        for i in range(box.tiles):
            pairs[i, plane + 2, pl.ds(PAD + at, size), :] = sums[i]

    first, last = box.span(margin + 4)
    sweep(half, first, last, restrict)

    def first_guess(plane, at, size, cache):
        for i in range(box.tiles):
            mean = 0.125 * pair_columns(pair_rows(pairs, i, plane, at, size))
            residual[i, plane + 2, pl.ds(PAD + at, size), :] = mean
            guess[i, plane + 2, pl.ds(PAD + at, size), :] = (
                coarse[CENTRE, i, plane, pl.ds(at, size), :] * mean
            )

    clear_ends(guess, first, last)
    sweep(half, first, last, first_guess)

    def correct(plane, at, size, cache):
        values = neighbours(guess, coarse, plane, at, size, 2, cache)
        for i, (total, centre) in enumerate(values):
            rest = residual[i, plane + 2, pl.ds(PAD + at, size), :] + total
            fix = (1.0 - RELAX) * centre + coarse[CENTRE, i, plane, pl.ds(at, size), :] * rest
            for half_plane in range(2):
                where = (i, 2 * plane + half_plane + 2, pl.ds(PAD + at, size), slice(None))
                trial[where] = trial[where] + fix

    sweep(half, *box.span(margin + 2), correct)

    def smooth_again(plane, at, size, cache):
        values = neighbours(trial, weights, plane, at, size, 1, cache)
        for i, (total, centre) in enumerate(values):
            given = source[i, plane + 2, pl.ds(PAD + at, size), :]
            value = (1.0 - RELAX) * centre + weight[i, plane, pl.ds(at, size), :] * (given + total)
            finish(plane, i, at, size, value)

    if planes is None:
        sweep(box.depth, *box.span(margin), smooth_again)
    else:
        sweep(
            planes,
            *box.span(margin),
            lambda plane, at, size, cache: smooth_again(base + plane, at, size, None),
        )


def coarse_scratch(box):
    half = box.depth // 2
    return [box.scratch(), box.scratch(half), box.scratch(half), box.scratch(half)]


def pair_body(box, own_end, other_end, starts, *rest):
    params, out, first_out, leaving = rest[:3], rest[3], rest[4], rest[5:7]
    source, trial, pairs, guess, residual = rest[7:]
    core = lax.axis_index("tm") % 2
    first, last = box.span(COARSE_REACH)
    clear_ends(source, first, last)

    def put(first_end, second_end):
        source[:, 2 : 2 + box.depth, PAD + first : PAD + last, :] = (
            first_end[...] - starts[1, :, :, first:last, :]
        )
        inner = slice(box.side - first, box.side - first + box.rows)
        out[...] = second_end[:, :, inner, :]
        first_out[...] = first_end[:, :, inner, :]

    @pl.when(core == 0)
    def _():
        put(own_end, other_end)

    @pl.when(core == 1)
    def _():
        put(other_end, own_end)

    def finish(plane, i, at, size, value):
        where = (i, plane, pl.ds(at - box.side, size), slice(None))
        out[where] = value + out[where]

    coarse_step_body(box, 0, source, trial, pairs, guess, residual, params, finish)
    pack(box, out, *leaving)


def pack(box, field, centre, edge):
    core, place = lax.axis_index("tm") % 2, lax.axis_index("coarse")
    half = box.depth // 2
    centre[...] = field[:, pl.ds(core * half, half)]
    width = edge.shape[1] // box.depth
    up = place % 2 == core
    for i in range(box.tiles):
        for plane in range(box.depth):
            edge[i, plane * width : (plane + 1) * width, :] = jnp.where(
                up, field[i, plane, box.rows - width :, :], field[i, plane, :width, :]
            )


def last_body(box, own_depth, turn, final, first_end, joined, *rest):
    arrived, rest = rest[:4], rest[4:]
    starts, params, result, leaving = rest[0], rest[1:4], rest[4], rest[5:-7]
    source, second, trial, pairs, guess, residual, total = rest[-7:]
    place = lax.axis_index("tm")
    core = place % 2
    active = place // 2 == turn
    side, rows = box.side, box.rows
    half = box.depth // 2
    clear_ends(source, *box.span(2 * COARSE_REACH))
    clear_ends(second, *box.span(COARSE_REACH))

    @pl.when(jnp.logical_not(active))
    def _():
        source[:, 2 : 2 + box.depth, PAD : PAD + box.height, :] = jnp.zeros(
            (box.tiles, box.depth, box.height, LANES), jnp.float32
        )

    @pl.when(active)
    def _():
        centre, edge, other_centre, other_edge = arrived
        for piece, rank in ((centre, core), (other_centre, 1 - core)):
            base = rank * half
            for i in range(box.tiles):
                for plane in range(half):
                    source[i, base + plane + 2, PAD + side : PAD + side + rows, :] = (
                        piece[i, plane] - starts[0, i, base + plane, side : side + rows, :]
                    )
        width = edge.shape[1] // box.depth
        row_place, count = lax.axis_index("coarse"), lax.axis_size("coarse")
        below = row_place % 2 != core

        def edges(low, high):
            for ref, at, valid in (
                (low, side - width, row_place > 0),
                (high, side + rows, row_place < count - 1),
            ):
                for i in range(box.tiles):
                    for plane in range(box.depth):
                        value = ref[i, plane * width : (plane + 1) * width, :]
                        source[i, plane + 2, PAD + at : PAD + at + width, :] = (
                            jnp.where(valid, value, 0.0) - starts[0, i, plane, at : at + width, :]
                        )

        @pl.when(below)
        def _():
            edges(edge, other_edge)

        @pl.when(jnp.logical_not(below))
        def _():
            edges(other_edge, edge)

    def finish_once(plane, i, at, size, value):
        second[i, plane + 2, pl.ds(PAD + at, size), :] = value

    coarse_step_body(
        box, COARSE_REACH, source, trial, pairs, guess, residual, params, finish_once
    )

    base = lax.axis_index("slab") * own_depth
    if final:

        def finish_result(plane, i, at, size, value):
            where = (i, plane, pl.ds(at - side, size), slice(None))
            once = second[i, plane + 2, pl.ds(PAD + at, size), :]
            result[0, plane - base, pl.ds(at - side, size), i * LANES : (i + 1) * LANES] = jnp.where(
                core == 1, value + joined[where], once + first_end[where]
            )

        coarse_step_body(
            box, 0, second, trial, pairs, guess, residual, params, finish_result, base, own_depth
        )
        return

    def finish_twice(plane, i, at, size, value):
        where = (i, plane, pl.ds(at - box.side, size), slice(None))
        total[where] = value + joined[where]

    coarse_step_body(box, 0, second, trial, pairs, guess, residual, params, finish_twice)

    @pl.when(core == 0)
    def _():
        for i in range(box.tiles):
            result[0, :, :, i * LANES : (i + 1) * LANES] = (
                first_end[i, pl.ds(base, own_depth)]
                + second[i, pl.ds(base + 2, own_depth), PAD + side : PAD + side + rows, :]
            )

    @pl.when(core == 1)
    def _():
        for i in range(box.tiles):
            result[0, :, :, i * LANES : (i + 1) * LANES] = total[i, pl.ds(base, own_depth)]

    pack(box, total, *leaving)


def run(body, outs, scratch, *args, aliases={}):
    return pl.pallas_call(
        body,
        out_shape=[jax.ShapeDtypeStruct(shape, jnp.float32) for shape in outs],
        in_specs=[pl.BlockSpec(memory_space=pltpu.VMEM)] * len(args),
        out_specs=[pl.BlockSpec(memory_space=pltpu.VMEM)] * len(outs),
        scratch_shapes=scratch,
        input_output_aliases=aliases,
        compiler_params=pltpu.CompilerParams(
            vmem_limit_bytes=20 * 1024 * 1024,
        ),
    )(*args)


def slab_blocks(block):
    count = lax.axis_size("slab")
    if count == 1:
        return [block]
    if count == 2:
        return [block, lax.ppermute(block, "slab", [(0, 1), (1, 0)])]
    gathered = lax.all_gather(block, "slab", axis=0)
    return [gathered[i] for i in range(count)]


def row_swaps(hop, away):
    windows, count = lax.axis_size("tm"), lax.axis_size("coarse")
    rounds = []
    for first in (0, 1):
        pairs = []
        for place in range(count):
            other = place + 1 if place % 2 == first else place - 1
            for t in range(windows):
                inside = 0 <= other < count
                target = (hop(t), other) if inside else (away(t), place)
                pairs.append((t * count + place, target[0] * count + target[1]))
        rounds.append(pairs)
    return rounds


def row_pieces(block, width, rounds):
    rows = block.shape[-2]
    axis = block.ndim - 2
    both = ("tm", "coarse")
    odd = lax.axis_index("coarse") % 2 == 1
    pieces = []
    up, down = block, block
    left = width
    while left > 0:
        size = min(rows, left)
        if size == rows and up is down:
            send_one = send_two = block
        else:
            high = lax.slice_in_dim(up, up.shape[axis] - size, None, axis=axis)
            low = lax.slice_in_dim(down, 0, size, axis=axis)
            send_one, send_two = jnp.where(odd, low, high), jnp.where(odd, high, low)
        got_one = lax.ppermute(send_one, both, rounds[0])
        got_two = lax.ppermute(send_two, both, rounds[1])
        pieces += [got_one, got_two]
        left -= size
        if left > 0:
            up, down = jnp.where(odd, got_one, got_two), jnp.where(odd, got_two, got_one)
    return pieces


def core_swapped(block):
    count = lax.axis_size("tm")
    assert count % 2 == 0
    return lax.ppermute(block, "tm", [(i, i ^ 1) for i in range(count)])


def per_device(states, diffusivity, velocity):
    windows = lax.axis_size("tm")
    place = lax.axis_index("tm")
    own_depth, rows, columns = diffusivity.shape
    side = round_up(FINE_REACH + COARSE_REACH, 8)
    depth = own_depth * lax.axis_size("slab")
    box = Box(depth, rows, side, columns)
    tiles, height, half = box.tiles, box.height, depth // 2

    second = place % 2 == 1
    slot = lax.broadcasted_iota(jnp.int32, (3, 1, 1, 1), 0)
    parcel = jnp.where(
        (slot == 0) != second, velocity, jnp.where(slot == 1, diffusivity[None], states)
    )
    rounds = row_swaps(lambda t: t, lambda t: t ^ 1)
    blocks = slab_blocks(parcel)
    swapped = [core_swapped(block) for block in blocks]
    near = row_pieces(blocks[0], side, rounds)
    near_swapped = [core_swapped(piece) for piece in near]
    count = len(blocks)
    shapes = [(n, tiles, depth, height, LANES) for n in (2, 4, 7)]
    placed = run(
        functools.partial(early_body, box, own_depth, count),
        shapes,
        [],
        *blocks,
        *near,
        *swapped,
        *near_swapped,
    )
    far = []
    for block in blocks[1:]:
        far += row_pieces(block, side, rounds)
    far = [piece for which in (1, 0) for piece in far[which::2]]
    far_swapped = [core_swapped(piece) for piece in far]
    cut = len(far) // 2
    if far:
        placed = run(
            functools.partial(late_body, box, own_depth, count),
            shapes,
            [],
            *far[:cut],
            *far_swapped[:cut],
            *placed,
            aliases={2 * cut + n: n for n in range(3)},
        )
    first, last = box.span(COARSE_REACH)
    end, starts, coeff, weights = run(
        functools.partial(fine_body, box, COARSE_REACH, own_depth, count),
        [(tiles, depth, last - first, LANES)] + shapes,
        [box.scratch(), box.scratch()],
        *far[cut:],
        *far_swapped[cut:],
        *placed,
        aliases={2 * cut + n: 1 + n for n in range(3)},
    )
    params = run(
        functools.partial(prepare_body, box),
        [(7, tiles, half, height, LANES), (tiles, depth, height, LANES)],
        [pltpu.VMEM((4, *box.scratch(half).shape), jnp.float32)],
        coeff,
    )
    params = [weights, *params]
    width = 2 * COARSE_REACH
    assert rows >= width
    leaving_shapes = [(tiles, half, rows, LANES), (tiles, depth * width, LANES)]
    joined, first_end, *leaving = run(
        functools.partial(pair_body, box),
        [(tiles, depth, rows, LANES)] * 2 + leaving_shapes,
        [box.scratch()] + coarse_scratch(box),
        end,
        core_swapped(end),
        starts,
        *params,
    )
    ends = jnp.where(place % 2 == 1, joined, first_end)
    ends = jnp.concatenate([ends[i] for i in range(tiles)], axis=-1)
    base = lax.axis_index("slab") * own_depth
    result = lax.dynamic_slice_in_dim(ends, base, own_depth, 0)[None]
    hop = lambda t: (t + 2) % windows
    one, two = row_swaps(hop, hop)
    across = [(t, hop(t)) for t in range(windows)]
    count = lax.axis_size("coarse")
    aside = [
        pair for pairs, core in ((one, 0), (two, 1)) for pair in pairs if pair[0] // count % 2 == core
    ]
    for turn in range(1, windows // 2):
        arrived = [
            lax.ppermute(leaving[0], "tm", across),
            lax.ppermute(leaving[1], ("tm", "coarse"), aside),
        ]
        arrived += [core_swapped(piece) for piece in arrived]
        final = turn == windows // 2 - 1
        out, *leaving = run(
            functools.partial(last_body, box, own_depth, turn, final),
            [(1, own_depth, rows, columns)] + ([] if final else leaving_shapes),
            [box.scratch()] * 2
            + coarse_scratch(box)
            + [pltpu.VMEM((tiles, depth, rows, LANES), jnp.float32)],
            first_end,
            joined,
            *arrived,
            starts,
            *params,
        )
        result = out if turn == 1 else jnp.where(place // 2 >= turn, out, result)
    return result


def solution(mesh):
    return jax.shard_map(
        per_device,
        mesh=mesh,
        in_specs=(
            P("tm", "slab", "coarse", None),
            P("slab", "coarse", None),
            P(None, "slab", "coarse", None),
        ),
        out_specs=P("tm", "slab", "coarse", None),
        check_vma=False,
    )
```

```python
import functools

import jax
import jax.numpy as jnp
from jax import lax
from jax.experimental import pallas as pl
from jax.experimental.pallas import tpu as pltpu
from jax.sharding import PartitionSpec as P

SECTIONS = 4
FINE_STEPS = 2
FINE_STEP = 1.0
RELAX = 0.8
INTERVAL = FINE_STEPS * FINE_STEP
LANES = 128
PAD = 8
COARSE_REACH = 6
FINE_REACH = SECTIONS * FINE_STEPS


def chebyshev_coefficients(sections):
    damping = 0.05
    centre_point = 1.0 + damping / (sections * sections)
    chebyshev = [1.0, centre_point]
    slopes = [0.0, 1.0]
    for degree in range(2, sections + 1):
        chebyshev.append(2.0 * centre_point * chebyshev[degree - 1] - chebyshev[degree - 2])
        slopes.append(
            2.0 * chebyshev[degree - 1]
            + 2.0 * centre_point * slopes[degree - 1]
            - slopes[degree - 2]
        )
    slope_ratio = chebyshev[sections] / slopes[sections]
    weights = [1.0 / entry for entry in chebyshev]
    scales = [0.0, 0.0]
    carries = [0.0, 0.0]
    tildes = [0.0, slope_ratio / centre_point]
    for degree in range(2, sections + 1):
        scales.append(2.0 * weights[degree] * centre_point / weights[degree - 1])
        carries.append(-weights[degree] / weights[degree - 2])
        tildes.append(2.0 * weights[degree] * slope_ratio / weights[degree - 1])
    return (scales, carries, tildes)


def round_up(value, unit):
    return -(-value // unit) * unit


class Box:
    def __init__(self, depth, rows, side, columns):
        self.depth, self.rows, self.side, self.columns = depth, rows, side, columns
        self.height = rows + 2 * side
        self.tiles = columns // LANES

    def scratch(self, depth=None):
        depth = self.depth if depth is None else depth
        return pltpu.VMEM(
            (self.tiles, depth + 4, self.height + 2 * PAD, LANES), jnp.float32
        )

    def span(self, margin):
        size = round_up(self.rows + 2 * margin, 8)
        first = self.side - (size - self.rows) // 2
        assert first >= 0 and first % 2 == 0
        return first, first + size


CHUNK = 8
FINE_CHUNK = 24
AFTER_DEPTH, BEFORE_DEPTH, AFTER_ROW, BEFORE_ROW, AFTER_COLUMN, BEFORE_COLUMN, CENTRE = range(7)


def chunks(first, last, most):
    at = first
    while at < last:
        size = min(most, last - at)
        yield at, size
        at += size


def sweep(count, first, last, body, most=CHUNK):
    if count <= 8:
        for at, size in chunks(first, last, most):
            cache = {}
            for plane in range(count):
                body(plane, at, size, cache)
    else:

        def step(plane, carry):
            for at, size in chunks(first, last, most):
                body(plane, at, size, None)
            return carry

        lax.fori_loop(0, count, step, 0)


def lane_index(size):
    return lax.broadcasted_iota(jnp.int32, (size, LANES), 1)


def row_index(size):
    return lax.broadcasted_iota(jnp.int32, (size, LANES), 0)


def sideways(values, step):
    lane = lane_index(values[0].shape[0])
    back = [pltpu.roll(entry, LANES - step, 1) for entry in values]
    forth = [pltpu.roll(entry, step, 1) for entry in values]
    count = len(values)
    after = [
        jnp.where(lane >= LANES - step, back[i + 1], back[i]) if i + 1 < count else back[i]
        for i in range(count)
    ]
    before = [jnp.where(lane < step, forth[i - 1], forth[i]) if i else forth[i] for i in range(count)]
    return after, before


def neighbours(field, weights, plane, at, size, step, cache):
    tiles = field.shape[0]

    def level(i, index):
        if cache is None:
            return field[i, index, pl.ds(PAD + at, size), :]
        if (i, index) not in cache:
            cache[i, index] = field[i, index, pl.ds(PAD + at, size), :]
        return cache[i, index]

    def weight(kind, i):
        return weights[kind, i, plane, pl.ds(at, size), :]

    centre = [level(i, plane + 2) for i in range(tiles)]
    after, before = sideways(centre, step)
    result = []
    for i in range(tiles):
        row_after = field[i, plane + 2, pl.ds(PAD + at + step, size), :]
        row_before = field[i, plane + 2, pl.ds(PAD + at - step, size), :]
        deep = weight(AFTER_DEPTH, i) * level(i, plane + 3) + weight(BEFORE_DEPTH, i) * level(
            i, plane + 1
        )
        down = weight(AFTER_ROW, i) * row_after + weight(BEFORE_ROW, i) * row_before
        along = weight(AFTER_COLUMN, i) * after[i] + weight(BEFORE_COLUMN, i) * before[i]
        result.append(((deep + down) + along, centre[i]))
    return result


def set_weights(weights, where, c, scale, drift_scale, tile, tiles, step):
    size = c[0].shape[-2]
    base = scale * c[0]
    for axis in range(3):
        drift = drift_scale * c[axis + 1]
        after, before = base - drift, base + drift
        if axis == 2 and tile == tiles - 1:
            after = jnp.where(lane_index(size) >= LANES - step, 0.0, after)
        if axis == 2 and tile == 0:
            before = jnp.where(lane_index(size) < step, 0.0, before)
        weights[(2 * axis,) + where] = after
        weights[(2 * axis + 1,) + where] = before


def clear_ends(field, first, last):
    tiles, planes = field.shape[:2]
    plane = jnp.zeros((tiles, 1, last - first, LANES), jnp.float32)
    field[:, 1:2, PAD + first : PAD + last, :] = plane
    field[:, planes - 2 : planes - 1, PAD + first : PAD + last, :] = plane


def fine_scheme():
    scales, carries, tildes = chebyshev_coefficients(SECTIONS)
    centre = INTERVAL / (tildes[1] * FINE_STEP)
    factors = [1.0]
    for degree in range(1, SECTIONS + 1):
        factors.append(factors[-1] * tildes[degree] * FINE_STEP / INTERVAL)
    back = [0.0, 0.0]
    for degree in range(2, SECTIONS + 1):
        back.append(carries[degree] * factors[degree - 2] / factors[degree])
    return centre, back, factors[SECTIONS]


def row_places(box, sizes):
    place, count = lax.axis_index("coarse"), lax.axis_size("coarse")
    odd = place % 2
    result = []
    gone = 0
    for step, size in enumerate(sizes, 1):
        below = pl.multiple_of(box.side - gone - size, 8)
        above = pl.multiple_of(box.side + box.rows + gone, 8)
        gone += size
        one = pl.multiple_of(jnp.where(odd == 1, below, above), 8)
        two = pl.multiple_of(jnp.where(odd == 1, above, below), 8)
        below_valid, above_valid = place >= step, place + step < count
        one_valid = jnp.where(odd == 1, below_valid, above_valid)
        two_valid = jnp.where(odd == 1, above_valid, below_valid)
        result.append(((one, one_valid), (two, two_valid)))
    return result


def place_pieces(box, own_depth, pieces, starts, coeff, weights):
    core = lax.axis_index("tm") % 2
    centre_constant = fine_scheme()[0]
    for own, other, block, blocks, at, valid in pieces:
        shift = lax.axis_index("slab") if blocks == 2 else 0
        base = (block + shift) % blocks * own_depth
        size = own.shape[-2]
        for plane in range(own_depth):
            for i in range(box.tiles):
                cols = slice(i * LANES, (i + 1) * LANES)
                where = (i, base + plane, pl.ds(at, size), slice(None))
                for ref, rank in ((own, core), (other, 1 - core)):
                    for slot, kind in ((2 - 2 * rank, None), (rank, 1 + rank), (1 + rank, 3 * rank)):
                        value = ref[slot, plane, :, cols]
                        if valid is not None:
                            value = jnp.where(valid, value, 0.0)
                        if kind is None:
                            starts[(rank,) + where] = value
                        else:
                            coeff[(kind,) + where] = value
                c = [coeff[(k,) + where] for k in range(4)]
                set_weights(weights, where, c, INTERVAL, 0.5 * INTERVAL, i, box.tiles, 1)
                weights[(CENTRE,) + where] = centre_constant - 6.0 * INTERVAL * c[0]


def early_body(box, own_depth, blocks, *refs):
    starts, coeff, weights = refs[-3:]
    half = (len(refs) - 3) // 2
    own, other = refs[:half], refs[half : 2 * half]
    places = row_places(box, [ref.shape[-2] for ref in own[blocks::2]])
    moves = [(own[block], other[block], block, blocks, box.side, None) for block in range(blocks)]
    for step, pair in enumerate(places):
        for which, (at, valid) in enumerate(pair):
            index = blocks + 2 * step + which
            moves.append((own[index], other[index], 0, blocks, at, valid))
    place_pieces(box, own_depth, moves, starts, coeff, weights)


def late_moves(box, blocks, own, other, which):
    if blocks == 1:
        return []
    steps = len(own) // (blocks - 1)
    places = row_places(box, [ref.shape[-2] for ref in own[:steps]])
    return [
        (own[n], other[n], 1 + n // steps, blocks, *places[n % steps][which]) for n in range(len(own))
    ]


def late_body(box, own_depth, blocks, *refs):
    half = (len(refs) - 6) // 2
    moves = late_moves(box, blocks, refs[:half], refs[half : 2 * half], 0)
    place_pieces(box, own_depth, moves, *refs[-3:])


def fine_body(box, margin, own_depth, blocks, *refs):
    end, starts, coeff, weights, one, two = refs[-6:]
    half = (len(refs) - 9) // 2
    core = lax.axis_index("tm") % 2
    moves = late_moves(box, blocks, refs[:half], refs[half : 2 * half], 1)
    place_pieces(box, own_depth, moves, starts, coeff, weights)
    clear_ends(one, 0, box.height)
    clear_ends(two, 0, box.height)
    one[:, 2 : 2 + box.depth, PAD : PAD + box.height, :] = starts[core]
    _, back, factor = fine_scheme()
    stage = 0
    current, other_field = one, two
    first, last = box.span(margin)
    for repeat in range(FINE_STEPS):
        for degree in range(1, SECTIONS + 1):
            stage += 1
            final = stage == FINE_REACH

            def body(plane, at, size, cache, current=current, old=other_field, degree=degree, final=final):
                values = neighbours(current, weights, plane, at, size, 1, cache)
                for i, (total, centre) in enumerate(values):
                    value = total + weights[CENTRE, i, plane, pl.ds(at, size), :] * centre
                    where = (i, plane + 2, pl.ds(PAD + at, size), slice(None))
                    if degree > 1:
                        value = value + back[degree] * old[where]
                    if final:
                        end[i, plane, pl.ds(at - first, size), :] = factor**FINE_STEPS * value
                    else:
                        old[where] = value

            sweep(box.depth, *box.span(margin + FINE_REACH - stage), body, FINE_CHUNK)
            current, other_field = other_field, current


def pair_columns(value):
    lane = lane_index(value.shape[0])
    other = jnp.where(
        lane % 2 == 0, pltpu.roll(value, LANES - 1, 1), pltpu.roll(value, 1, 1)
    )
    return value + other


def pair_rows(field, i, plane, at, size):
    row = row_index(size)
    other = jnp.where(
        row % 2 == 0,
        field[i, plane + 2, pl.ds(PAD + at + 1, size), :],
        field[i, plane + 2, pl.ds(PAD + at - 1, size), :],
    )
    return field[i, plane + 2, pl.ds(PAD + at, size), :] + other


def prepare_body(box, coeff, coarse, weight, work):
    half = box.depth // 2
    for k in range(4):
        def columns(plane, at, size, cache, k=k):
            for i in range(box.tiles):
                low = coeff[k, i, 2 * plane, pl.ds(at, size), :]
                high = coeff[k, i, 2 * plane + 1, pl.ds(at, size), :]
                work[k, i, plane + 2, pl.ds(PAD + at, size), :] = pair_columns(low + high)
                if k == 0:
                    for offset, value in ((0, low), (1, high)):
                        weight[i, 2 * plane + offset, pl.ds(at, size), :] = RELAX / (
                            1.0 + 6.0 * INTERVAL * value
                        )

        sweep(half, 0, box.height, columns)

    def rows(plane, at, size, cache):
        for i in range(box.tiles):
            where = (i, plane, pl.ds(at, size), slice(None))
            c = [0.125 * pair_rows(work.at[k], i, plane, at, size) for k in range(4)]
            set_weights(coarse, where, c, INTERVAL / 4.0, INTERVAL / 4.0, i, box.tiles, 2)
            coarse[(CENTRE,) + where] = RELAX / (1.0 + 6.0 * INTERVAL / 4.0 * c[0])

    sweep(half, 0, box.height, rows)


def coarse_step_body(
    box, margin, source, trial, pairs, guess, residual, params, finish, base=0, planes=None
):
    weights, coarse, weight = params
    half = box.depth // 2
    centre_constant = fine_scheme()[0]

    def smooth(plane, at, size, cache):
        values = neighbours(source, weights, plane, at, size, 1, cache)
        for i, (total, centre) in enumerate(values):
            trial[i, plane + 2, pl.ds(PAD + at, size), :] = (1.0 - RELAX) * centre + weight[
                i, plane, pl.ds(at, size), :
            ] * (centre + total)

    first, last = box.span(margin + 5)
    clear_ends(trial, first, last)
    sweep(box.depth, first, last, smooth)

    def restrict(plane, at, size, cache):
        sums = [None] * box.tiles
        for half_plane in range(2):
            fine_plane = 2 * plane + half_plane
            values = neighbours(trial, weights, fine_plane, at, size, 1, cache)
            for i, (total, centre) in enumerate(values):
                given = source[i, fine_plane + 2, pl.ds(PAD + at, size), :]
                inner = weights[CENTRE, i, fine_plane, pl.ds(at, size), :] - (1.0 + centre_constant)
                misfit = (given + total) + inner * centre
                sums[i] = misfit if sums[i] is None else sums[i] + misfit
        for i in range(box.tiles):
            pairs[i, plane + 2, pl.ds(PAD + at, size), :] = sums[i]

    first, last = box.span(margin + 4)
    sweep(half, first, last, restrict)

    def first_guess(plane, at, size, cache):
        for i in range(box.tiles):
            mean = 0.125 * pair_columns(pair_rows(pairs, i, plane, at, size))
            residual[i, plane + 2, pl.ds(PAD + at, size), :] = mean
            guess[i, plane + 2, pl.ds(PAD + at, size), :] = (
                coarse[CENTRE, i, plane, pl.ds(at, size), :] * mean
            )

    clear_ends(guess, first, last)
    sweep(half, first, last, first_guess)

    def correct(plane, at, size, cache):
        values = neighbours(guess, coarse, plane, at, size, 2, cache)
        for i, (total, centre) in enumerate(values):
            rest = residual[i, plane + 2, pl.ds(PAD + at, size), :] + total
            fix = (1.0 - RELAX) * centre + coarse[CENTRE, i, plane, pl.ds(at, size), :] * rest
            for half_plane in range(2):
                where = (i, 2 * plane + half_plane + 2, pl.ds(PAD + at, size), slice(None))
                trial[where] = trial[where] + fix

    sweep(half, *box.span(margin + 2), correct)

    def smooth_again(plane, at, size, cache):
        values = neighbours(trial, weights, plane, at, size, 1, cache)
        for i, (total, centre) in enumerate(values):
            given = source[i, plane + 2, pl.ds(PAD + at, size), :]
            value = (1.0 - RELAX) * centre + weight[i, plane, pl.ds(at, size), :] * (given + total)
            finish(plane, i, at, size, value)

    if planes is None:
        sweep(box.depth, *box.span(margin), smooth_again)
    else:
        sweep(
            planes,
            *box.span(margin),
            lambda plane, at, size, cache: smooth_again(base + plane, at, size, None),
        )


def coarse_scratch(box):
    half = box.depth // 2
    return [box.scratch(), box.scratch(half), box.scratch(half), box.scratch(half)]


def pair_body(box, own_end, other_end, starts, *rest):
    params, out, first_out, leaving = rest[:3], rest[3], rest[4], rest[5:7]
    source, trial, pairs, guess, residual = rest[7:]
    core = lax.axis_index("tm") % 2
    first, last = box.span(COARSE_REACH)
    clear_ends(source, first, last)

    def put(first_end, second_end):
        source[:, 2 : 2 + box.depth, PAD + first : PAD + last, :] = (
            first_end[...] - starts[1, :, :, first:last, :]
        )
        inner = slice(box.side - first, box.side - first + box.rows)
        out[...] = second_end[:, :, inner, :]
        first_out[...] = first_end[:, :, inner, :]

    @pl.when(core == 0)
    def _():
        put(own_end, other_end)

    @pl.when(core == 1)
    def _():
        put(other_end, own_end)

    def finish(plane, i, at, size, value):
        where = (i, plane, pl.ds(at - box.side, size), slice(None))
        out[where] = value + out[where]

    coarse_step_body(box, 0, source, trial, pairs, guess, residual, params, finish)
    pack(box, out, *leaving)


def pack(box, field, centre, edge):
    core, place = lax.axis_index("tm") % 2, lax.axis_index("coarse")
    half = box.depth // 2
    centre[...] = field[:, pl.ds(core * half, half)]
    width = edge.shape[1] // box.depth
    up = place % 2 == core
    for i in range(box.tiles):
        for plane in range(box.depth):
            edge[i, plane * width : (plane + 1) * width, :] = jnp.where(
                up, field[i, plane, box.rows - width :, :], field[i, plane, :width, :]
            )


def last_body(box, own_depth, turn, final, first_end, joined, *rest):
    arrived, rest = rest[:4], rest[4:]
    starts, params, result, leaving = rest[0], rest[1:4], rest[4], rest[5:-7]
    source, second, trial, pairs, guess, residual, total = rest[-7:]
    place = lax.axis_index("tm")
    core = place % 2
    active = place // 2 == turn
    side, rows = box.side, box.rows
    half = box.depth // 2
    clear_ends(source, *box.span(2 * COARSE_REACH))
    clear_ends(second, *box.span(COARSE_REACH))

    @pl.when(jnp.logical_not(active))
    def _():
        source[:, 2 : 2 + box.depth, PAD : PAD + box.height, :] = jnp.zeros(
            (box.tiles, box.depth, box.height, LANES), jnp.float32
        )

    @pl.when(active)
    def _():
        centre, edge, other_centre, other_edge = arrived
        for piece, rank in ((centre, core), (other_centre, 1 - core)):
            base = rank * half
            for i in range(box.tiles):
                for plane in range(half):
                    source[i, base + plane + 2, PAD + side : PAD + side + rows, :] = (
                        piece[i, plane] - starts[0, i, base + plane, side : side + rows, :]
                    )
        width = edge.shape[1] // box.depth
        row_place, count = lax.axis_index("coarse"), lax.axis_size("coarse")
        below = row_place % 2 != core

        def edges(low, high):
            for ref, at, valid in (
                (low, side - width, row_place > 0),
                (high, side + rows, row_place < count - 1),
            ):
                for i in range(box.tiles):
                    for plane in range(box.depth):
                        value = ref[i, plane * width : (plane + 1) * width, :]
                        source[i, plane + 2, PAD + at : PAD + at + width, :] = (
                            jnp.where(valid, value, 0.0) - starts[0, i, plane, at : at + width, :]
                        )

        @pl.when(below)
        def _():
            edges(edge, other_edge)

        @pl.when(jnp.logical_not(below))
        def _():
            edges(other_edge, edge)

    def finish_once(plane, i, at, size, value):
        second[i, plane + 2, pl.ds(PAD + at, size), :] = value

    coarse_step_body(
        box, COARSE_REACH, source, trial, pairs, guess, residual, params, finish_once
    )

    base = lax.axis_index("slab") * own_depth
    if final:

        def finish_result(plane, i, at, size, value):
            where = (i, plane, pl.ds(at - side, size), slice(None))
            once = second[i, plane + 2, pl.ds(PAD + at, size), :]
            result[0, plane - base, pl.ds(at - side, size), i * LANES : (i + 1) * LANES] = jnp.where(
                core == 1, value + joined[where], once + first_end[where]
            )

        coarse_step_body(
            box, 0, second, trial, pairs, guess, residual, params, finish_result, base, own_depth
        )
        return

    def finish_twice(plane, i, at, size, value):
        where = (i, plane, pl.ds(at - box.side, size), slice(None))
        total[where] = value + joined[where]

    coarse_step_body(box, 0, second, trial, pairs, guess, residual, params, finish_twice)

    @pl.when(core == 0)
    def _():
        for i in range(box.tiles):
            result[0, :, :, i * LANES : (i + 1) * LANES] = (
                first_end[i, pl.ds(base, own_depth)]
                + second[i, pl.ds(base + 2, own_depth), PAD + side : PAD + side + rows, :]
            )

    @pl.when(core == 1)
    def _():
        for i in range(box.tiles):
            result[0, :, :, i * LANES : (i + 1) * LANES] = total[i, pl.ds(base, own_depth)]

    pack(box, total, *leaving)


def run(body, outs, scratch, *args, aliases={}):
    return pl.pallas_call(
        body,
        out_shape=[jax.ShapeDtypeStruct(shape, jnp.float32) for shape in outs],
        in_specs=[pl.BlockSpec(memory_space=pltpu.VMEM)] * len(args),
        out_specs=[pl.BlockSpec(memory_space=pltpu.VMEM)] * len(outs),
        scratch_shapes=scratch,
        input_output_aliases=aliases,
        compiler_params=pltpu.CompilerParams(
            vmem_limit_bytes=20 * 1024 * 1024,
        ),
    )(*args)


def slab_blocks(block):
    count = lax.axis_size("slab")
    if count == 1:
        return [block]
    if count == 2:
        return [block, lax.ppermute(block, "slab", [(0, 1), (1, 0)])]
    gathered = lax.all_gather(block, "slab", axis=0)
    return [gathered[i] for i in range(count)]


def row_swaps(hop, away):
    windows, count = lax.axis_size("tm"), lax.axis_size("coarse")
    rounds = []
    for first in (0, 1):
        pairs = []
        for place in range(count):
            other = place + 1 if place % 2 == first else place - 1
            for t in range(windows):
                inside = 0 <= other < count
                target = (hop(t), other) if inside else (away(t), place)
                pairs.append((t * count + place, target[0] * count + target[1]))
        rounds.append(pairs)
    return rounds


def row_pieces(block, width, rounds):
    rows = block.shape[-2]
    axis = block.ndim - 2
    both = ("tm", "coarse")
    odd = lax.axis_index("coarse") % 2 == 1
    pieces = []
    up, down = block, block
    left = width
    while left > 0:
        size = min(rows, left)
        if size == rows and up is down:
            send_one = send_two = block
        else:
            high = lax.slice_in_dim(up, up.shape[axis] - size, None, axis=axis)
            low = lax.slice_in_dim(down, 0, size, axis=axis)
            send_one, send_two = jnp.where(odd, low, high), jnp.where(odd, high, low)
        got_two = lax.ppermute(send_two, both, rounds[1])
        got_one = lax.ppermute(send_one, both, rounds[0])
        pieces += [got_one, got_two]
        left -= size
        if left > 0:
            up, down = jnp.where(odd, got_one, got_two), jnp.where(odd, got_two, got_one)
    return pieces


def core_swapped(block):
    count = lax.axis_size("tm")
    assert count % 2 == 0
    return lax.ppermute(block, "tm", [(i, i ^ 1) for i in range(count)])


def per_device(states, diffusivity, velocity):
    windows = lax.axis_size("tm")
    place = lax.axis_index("tm")
    own_depth, rows, columns = diffusivity.shape
    side = round_up(FINE_REACH + COARSE_REACH, 8)
    depth = own_depth * lax.axis_size("slab")
    box = Box(depth, rows, side, columns)
    tiles, height, half = box.tiles, box.height, depth // 2

    second = place % 2 == 1
    slot = lax.broadcasted_iota(jnp.int32, (3, 1, 1, 1), 0)
    parcel = jnp.where(
        (slot == 0) != second, velocity, jnp.where(slot == 1, diffusivity[None], states)
    )
    rounds = row_swaps(lambda t: t, lambda t: t ^ 1)
    blocks = slab_blocks(parcel)
    swapped = [core_swapped(block) for block in blocks]
    near = row_pieces(blocks[0], side, rounds)
    near_swapped = [core_swapped(piece) for piece in near]
    count = len(blocks)
    shapes = [(n, tiles, depth, height, LANES) for n in (2, 4, 7)]
    placed = run(
        functools.partial(early_body, box, own_depth, count),
        shapes,
        [],
        *blocks,
        *near,
        *swapped,
        *near_swapped,
    )
    far = []
    for block in blocks[1:]:
        far += row_pieces(block, side, rounds)
    far = [piece for which in (0, 1) for piece in far[which::2]]
    far_swapped = [core_swapped(piece) for piece in far]
    cut = len(far) // 2
    if far:
        placed = run(
            functools.partial(late_body, box, own_depth, count),
            shapes,
            [],
            *far[:cut],
            *far_swapped[:cut],
            *placed,
            aliases={2 * cut + n: n for n in range(3)},
        )
    first, last = box.span(COARSE_REACH)
    end, starts, coeff, weights = run(
        functools.partial(fine_body, box, COARSE_REACH, own_depth, count),
        [(tiles, depth, last - first, LANES)] + shapes,
        [box.scratch(), box.scratch()],
        *far[cut:],
        *far_swapped[cut:],
        *placed,
        aliases={2 * cut + n: 1 + n for n in range(3)},
    )
    params = run(
        functools.partial(prepare_body, box),
        [(7, tiles, half, height, LANES), (tiles, depth, height, LANES)],
        [pltpu.VMEM((4, *box.scratch(half).shape), jnp.float32)],
        coeff,
    )
    params = [weights, *params]
    width = 2 * COARSE_REACH
    assert rows >= width
    leaving_shapes = [(tiles, half, rows, LANES), (tiles, depth * width, LANES)]
    joined, first_end, *leaving = run(
        functools.partial(pair_body, box),
        [(tiles, depth, rows, LANES)] * 2 + leaving_shapes,
        [box.scratch()] + coarse_scratch(box),
        end,
        core_swapped(end),
        starts,
        *params,
    )
    ends = jnp.where(place % 2 == 1, joined, first_end)
    ends = jnp.concatenate([ends[i] for i in range(tiles)], axis=-1)
    base = lax.axis_index("slab") * own_depth
    result = lax.dynamic_slice_in_dim(ends, base, own_depth, 0)[None]
    hop = lambda t: (t + 2) % windows
    one, two = row_swaps(hop, hop)
    across = [(t, hop(t)) for t in range(windows)]
    count = lax.axis_size("coarse")
    aside = [
        pair for pairs, core in ((one, 0), (two, 1)) for pair in pairs if pair[0] // count % 2 == core
    ]
    for turn in range(1, windows // 2):
        arrived = [
            lax.ppermute(leaving[0], "tm", across),
            lax.ppermute(leaving[1], ("tm", "coarse"), aside),
        ]
        arrived += [core_swapped(piece) for piece in arrived]
        final = turn == windows // 2 - 1
        out, *leaving = run(
            functools.partial(last_body, box, own_depth, turn, final),
            [(1, own_depth, rows, columns)] + ([] if final else leaving_shapes),
            [box.scratch()] * 2
            + coarse_scratch(box)
            + [pltpu.VMEM((tiles, depth, rows, LANES), jnp.float32)],
            first_end,
            joined,
            *arrived,
            starts,
            *params,
        )
        result = out if turn == 1 else jnp.where(place // 2 >= turn, out, result)
    return result


def solution(mesh):
    return jax.shard_map(
        per_device,
        mesh=mesh,
        in_specs=(
            P("tm", "slab", "coarse", None),
            P("slab", "coarse", None),
            P(None, "slab", "coarse", None),
        ),
        out_specs=P("tm", "slab", "coarse", None),
        check_vma=False,
    )
```

```python
import functools

import jax
import jax.numpy as jnp
from jax import lax
from jax.experimental import pallas as pl
from jax.experimental.pallas import tpu as pltpu
from jax.sharding import PartitionSpec as P


SECTIONS = 4
FINE_STEPS = 2
FINE_STEP = 1.0
RELAX = 0.8
INTERVAL = FINE_STEPS * FINE_STEP
LANES = 128
PAD = 8
COARSE_REACH = 6
FINE_REACH = SECTIONS * FINE_STEPS


def chebyshev_coefficients(sections):
    damping = 0.05
    centre_point = 1.0 + damping / (sections * sections)
    chebyshev = [1.0, centre_point]
    slopes = [0.0, 1.0]
    for degree in range(2, sections + 1):
        chebyshev.append(2.0 * centre_point * chebyshev[degree - 1] - chebyshev[degree - 2])
        slopes.append(
            2.0 * chebyshev[degree - 1]
            + 2.0 * centre_point * slopes[degree - 1]
            - slopes[degree - 2]
        )
    slope_ratio = chebyshev[sections] / slopes[sections]
    weights = [1.0 / entry for entry in chebyshev]
    scales = [0.0, 0.0]
    carries = [0.0, 0.0]
    tildes = [0.0, slope_ratio / centre_point]
    for degree in range(2, sections + 1):
        scales.append(2.0 * weights[degree] * centre_point / weights[degree - 1])
        carries.append(-weights[degree] / weights[degree - 2])
        tildes.append(2.0 * weights[degree] * slope_ratio / weights[degree - 1])
    return (scales, carries, tildes)


def round_up(value, unit):
    return -(-value // unit) * unit


class Box:
    def __init__(self, depth, rows, side, columns):
        self.depth, self.rows, self.side, self.columns = depth, rows, side, columns
        self.height = rows + 2 * side
        self.tiles = columns // LANES

    def scratch(self, depth=None):
        depth = self.depth if depth is None else depth
        return pltpu.VMEM(
            (self.tiles, depth + 4, self.height + 2 * PAD, LANES), jnp.float32
        )

    def span(self, margin):
        size = round_up(self.rows + 2 * margin, 8)
        first = self.side - (size - self.rows) // 2
        assert first >= 0 and first % 2 == 0
        return first, first + size


CHUNK = 8
FINE_CHUNK = 24
AFTER_DEPTH, BEFORE_DEPTH, AFTER_ROW, BEFORE_ROW, AFTER_COLUMN, BEFORE_COLUMN, CENTRE = range(7)


def chunks(first, last, most):
    at = first
    while at < last:
        size = min(most, last - at)
        yield at, size
        at += size


def sweep(count, first, last, body, most=CHUNK):
    if count <= 8:
        for at, size in chunks(first, last, most):
            cache = {}
            for plane in range(count):
                body(plane, at, size, cache)
    else:

        def step(plane, carry):
            for at, size in chunks(first, last, most):
                body(plane, at, size, None)
            return carry

        lax.fori_loop(0, count, step, 0)


def lane_index(size):
    return lax.broadcasted_iota(jnp.int32, (size, LANES), 1)


def row_index(size):
    return lax.broadcasted_iota(jnp.int32, (size, LANES), 0)


def sideways(values, step):
    lane = lane_index(values[0].shape[0])
    back = [pltpu.roll(entry, LANES - step, 1) for entry in values]
    forth = [pltpu.roll(entry, step, 1) for entry in values]
    count = len(values)
    after = [
        jnp.where(lane >= LANES - step, back[i + 1], back[i]) if i + 1 < count else back[i]
        for i in range(count)
    ]
    before = [jnp.where(lane < step, forth[i - 1], forth[i]) if i else forth[i] for i in range(count)]
    return after, before


def neighbours(field, weights, plane, at, size, step, cache):
    tiles = field.shape[0]

    def level(i, index):
        if cache is None:
            return field[i, index, pl.ds(PAD + at, size), :]
        if (i, index) not in cache:
            cache[i, index] = field[i, index, pl.ds(PAD + at, size), :]
        return cache[i, index]

    def weight(kind, i):
        return weights[kind, i, plane, pl.ds(at, size), :]

    centre = [level(i, plane + 2) for i in range(tiles)]
    after, before = sideways(centre, step)
    result = []
    for i in range(tiles):
        row_after = field[i, plane + 2, pl.ds(PAD + at + step, size), :]
        row_before = field[i, plane + 2, pl.ds(PAD + at - step, size), :]
        deep = weight(AFTER_DEPTH, i) * level(i, plane + 3) + weight(BEFORE_DEPTH, i) * level(
            i, plane + 1
        )
        down = weight(AFTER_ROW, i) * row_after + weight(BEFORE_ROW, i) * row_before
        along = weight(AFTER_COLUMN, i) * after[i] + weight(BEFORE_COLUMN, i) * before[i]
        result.append(((deep + down) + along, centre[i]))
    return result


def set_weights(weights, where, c, scale, drift_scale, tile, tiles, step):
    size = c[0].shape[-2]
    base = scale * c[0]
    for axis in range(3):
        drift = drift_scale * c[axis + 1]
        after, before = base - drift, base + drift
        if axis == 2 and tile == tiles - 1:
            after = jnp.where(lane_index(size) >= LANES - step, 0.0, after)
        if axis == 2 and tile == 0:
            before = jnp.where(lane_index(size) < step, 0.0, before)
        weights[(2 * axis,) + where] = after
        weights[(2 * axis + 1,) + where] = before


def clear_ends(field, first, last):
    tiles, planes = field.shape[:2]
    plane = jnp.zeros((tiles, 1, last - first, LANES), jnp.float32)
    field[:, 1:2, PAD + first : PAD + last, :] = plane
    field[:, planes - 2 : planes - 1, PAD + first : PAD + last, :] = plane


def fine_scheme():
    _, carries, tildes = chebyshev_coefficients(SECTIONS)
    centre = INTERVAL / (tildes[1] * FINE_STEP)
    factors = [1.0]
    for degree in range(1, SECTIONS + 1):
        factors.append(factors[-1] * tildes[degree] * FINE_STEP / INTERVAL)
    back = [0.0, 0.0]
    for degree in range(2, SECTIONS + 1):
        back.append(carries[degree] * factors[degree - 2] / factors[degree])
    return centre, back, factors[SECTIONS]


def row_places(box, sizes):
    place, count = lax.axis_index("coarse"), lax.axis_size("coarse")
    odd = place % 2
    result = []
    gone = 0
    for step, size in enumerate(sizes, 1):
        below = pl.multiple_of(box.side - gone - size, 8)
        above = pl.multiple_of(box.side + box.rows + gone, 8)
        gone += size
        one = pl.multiple_of(jnp.where(odd == 1, below, above), 8)
        two = pl.multiple_of(jnp.where(odd == 1, above, below), 8)
        below_valid, above_valid = place >= step, place + step < count
        one_valid = jnp.where(odd == 1, below_valid, above_valid)
        two_valid = jnp.where(odd == 1, above_valid, below_valid)
        result.append(((one, one_valid), (two, two_valid)))
    return result


def place_pieces(box, own_depth, pieces, starts, coeff, weights):
    core = lax.axis_index("tm") % 2
    centre_constant = fine_scheme()[0]
    for own, other, block, blocks, at, valid in pieces:
        shift = lax.axis_index("slab") if blocks == 2 else 0
        base = (block + shift) % blocks * own_depth
        size = own.shape[-2]
        for plane in range(own_depth):
            for i in range(box.tiles):
                cols = slice(i * LANES, (i + 1) * LANES)
                where = (i, base + plane, pl.ds(at, size), slice(None))
                for ref, rank in ((own, core), (other, 1 - core)):
                    for slot, kind in ((2 - 2 * rank, None), (rank, 1 + rank), (1 + rank, 3 * rank)):
                        value = ref[slot, plane, :, cols]
                        if valid is not None:
                            value = jnp.where(valid, value, 0.0)
                        if kind is None:
                            starts[(rank,) + where] = value
                        else:
                            coeff[(kind,) + where] = value
                c = [coeff[(k,) + where] for k in range(4)]
                set_weights(weights, where, c, INTERVAL, 0.5 * INTERVAL, i, box.tiles, 1)
                weights[(CENTRE,) + where] = centre_constant - 6.0 * INTERVAL * c[0]


def early_body(box, own_depth, blocks, *refs):
    starts, coeff, weights = refs[-3:]
    half = (len(refs) - 3) // 2
    own, other = refs[:half], refs[half : 2 * half]
    places = row_places(box, [ref.shape[-2] for ref in own[blocks::2]])
    moves = [(own[block], other[block], block, blocks, box.side, None) for block in range(blocks)]
    for step, pair in enumerate(places):
        for which, (at, valid) in enumerate(pair):
            index = blocks + 2 * step + which
            moves.append((own[index], other[index], 0, blocks, at, valid))
    place_pieces(box, own_depth, moves, starts, coeff, weights)


def late_moves(box, blocks, own, other, which):
    if blocks == 1:
        return []
    steps = len(own) // (blocks - 1)
    places = row_places(box, [ref.shape[-2] for ref in own[:steps]])
    return [
        (own[n], other[n], 1 + n // steps, blocks, *places[n % steps][which]) for n in range(len(own))
    ]


def late_body(box, own_depth, blocks, *refs):
    half = (len(refs) - 6) // 2
    moves = late_moves(box, blocks, refs[:half], refs[half : 2 * half], 0)
    place_pieces(box, own_depth, moves, *refs[-3:])


def fine_body(box, margin, own_depth, blocks, *refs):
    end, starts, coeff, weights, one, two = refs[-6:]
    half = (len(refs) - 9) // 2
    core = lax.axis_index("tm") % 2
    moves = late_moves(box, blocks, refs[:half], refs[half : 2 * half], 1)
    place_pieces(box, own_depth, moves, starts, coeff, weights)
    clear_ends(one, 0, box.height)
    clear_ends(two, 0, box.height)
    one[:, 2 : 2 + box.depth, PAD : PAD + box.height, :] = starts[core]
    _, back, factor = fine_scheme()
    stage = 0
    current, other_field = one, two
    first, _ = box.span(margin)
    for _ in range(FINE_STEPS):
        for degree in range(1, SECTIONS + 1):
            stage += 1
            final = stage == FINE_REACH

            def body(plane, at, size, cache, current=current, old=other_field, degree=degree, final=final):
                values = neighbours(current, weights, plane, at, size, 1, cache)
                for i, (total, centre) in enumerate(values):
                    value = total + weights[CENTRE, i, plane, pl.ds(at, size), :] * centre
                    where = (i, plane + 2, pl.ds(PAD + at, size), slice(None))
                    if degree > 1:
                        value = value + back[degree] * old[where]
                    if final:
                        end[i, plane, pl.ds(at - first, size), :] = factor**FINE_STEPS * value
                    else:
                        old[where] = value

            sweep(box.depth, *box.span(margin + FINE_REACH - stage), body, FINE_CHUNK)
            current, other_field = other_field, current


def pair_columns(value):
    lane = lane_index(value.shape[0])
    other = jnp.where(
        lane % 2 == 0, pltpu.roll(value, LANES - 1, 1), pltpu.roll(value, 1, 1)
    )
    return value + other


def pair_rows(field, i, plane, at, size):
    row = row_index(size)
    other = jnp.where(
        row % 2 == 0,
        field[i, plane + 2, pl.ds(PAD + at + 1, size), :],
        field[i, plane + 2, pl.ds(PAD + at - 1, size), :],
    )
    return field[i, plane + 2, pl.ds(PAD + at, size), :] + other


def prepare_body(box, coeff, coarse, weight, work):
    half = box.depth // 2
    for k in range(4):
        def columns(plane, at, size, cache, k=k):
            for i in range(box.tiles):
                low = coeff[k, i, 2 * plane, pl.ds(at, size), :]
                high = coeff[k, i, 2 * plane + 1, pl.ds(at, size), :]
                work[k, i, plane + 2, pl.ds(PAD + at, size), :] = pair_columns(low + high)
                if k == 0:
                    for offset, value in ((0, low), (1, high)):
                        weight[i, 2 * plane + offset, pl.ds(at, size), :] = RELAX / (
                            1.0 + 6.0 * INTERVAL * value
                        )

        sweep(half, 0, box.height, columns)

    def rows(plane, at, size, cache):
        for i in range(box.tiles):
            where = (i, plane, pl.ds(at, size), slice(None))
            c = [0.125 * pair_rows(work.at[k], i, plane, at, size) for k in range(4)]
            set_weights(coarse, where, c, INTERVAL / 4.0, INTERVAL / 4.0, i, box.tiles, 2)
            coarse[(CENTRE,) + where] = RELAX / (1.0 + 6.0 * INTERVAL / 4.0 * c[0])

    sweep(half, 0, box.height, rows)


def coarse_step_body(
    box, margin, source, trial, pairs, guess, residual, params, finish, base=0, planes=None
):
    weights, coarse, weight = params
    half = box.depth // 2
    centre_constant = fine_scheme()[0]

    def smooth(plane, at, size, cache):
        values = neighbours(source, weights, plane, at, size, 1, cache)
        for i, (total, centre) in enumerate(values):
            trial[i, plane + 2, pl.ds(PAD + at, size), :] = (1.0 - RELAX) * centre + weight[
                i, plane, pl.ds(at, size), :
            ] * (centre + total)

    first, last = box.span(margin + 5)
    clear_ends(trial, first, last)
    sweep(box.depth, first, last, smooth)

    def restrict(plane, at, size, cache):
        sums = [None] * box.tiles
        for half_plane in range(2):
            fine_plane = 2 * plane + half_plane
            values = neighbours(trial, weights, fine_plane, at, size, 1, cache)
            for i, (total, centre) in enumerate(values):
                given = source[i, fine_plane + 2, pl.ds(PAD + at, size), :]
                inner = weights[CENTRE, i, fine_plane, pl.ds(at, size), :] - (1.0 + centre_constant)
                misfit = (given + total) + inner * centre
                sums[i] = misfit if sums[i] is None else sums[i] + misfit
        for i in range(box.tiles):
            pairs[i, plane + 2, pl.ds(PAD + at, size), :] = sums[i]

    first, last = box.span(margin + 4)
    sweep(half, first, last, restrict)

    def first_guess(plane, at, size, cache):
        for i in range(box.tiles):
            mean = 0.125 * pair_columns(pair_rows(pairs, i, plane, at, size))
            residual[i, plane + 2, pl.ds(PAD + at, size), :] = mean
            guess[i, plane + 2, pl.ds(PAD + at, size), :] = (
                coarse[CENTRE, i, plane, pl.ds(at, size), :] * mean
            )

    clear_ends(guess, first, last)
    sweep(half, first, last, first_guess)

    def correct(plane, at, size, cache):
        values = neighbours(guess, coarse, plane, at, size, 2, cache)
        for i, (total, centre) in enumerate(values):
            rest = residual[i, plane + 2, pl.ds(PAD + at, size), :] + total
            fix = (1.0 - RELAX) * centre + coarse[CENTRE, i, plane, pl.ds(at, size), :] * rest
            for half_plane in range(2):
                where = (i, 2 * plane + half_plane + 2, pl.ds(PAD + at, size), slice(None))
                trial[where] = trial[where] + fix

    sweep(half, *box.span(margin + 2), correct)

    def smooth_again(plane, at, size, cache):
        values = neighbours(trial, weights, plane, at, size, 1, cache)
        for i, (total, centre) in enumerate(values):
            given = source[i, plane + 2, pl.ds(PAD + at, size), :]
            value = (1.0 - RELAX) * centre + weight[i, plane, pl.ds(at, size), :] * (given + total)
            finish(plane, i, at, size, value)

    if planes is None:
        sweep(box.depth, *box.span(margin), smooth_again)
    else:
        sweep(
            planes,
            *box.span(margin),
            lambda plane, at, size, cache: smooth_again(base + plane, at, size, None),
        )


def coarse_scratch(box):
    half = box.depth // 2
    return [box.scratch(), box.scratch(half), box.scratch(half), box.scratch(half)]


def pair_body(box, own_end, other_end, starts, *rest):
    params, out, first_out, leaving = rest[:3], rest[3], rest[4], rest[5:7]
    source, trial, pairs, guess, residual = rest[7:]
    core = lax.axis_index("tm") % 2
    first, last = box.span(COARSE_REACH)
    clear_ends(source, first, last)

    def put(first_end, second_end):
        source[:, 2 : 2 + box.depth, PAD + first : PAD + last, :] = (
            first_end[...] - starts[1, :, :, first:last, :]
        )
        inner = slice(box.side - first, box.side - first + box.rows)
        out[...] = second_end[:, :, inner, :]
        first_out[...] = first_end[:, :, inner, :]

    @pl.when(core == 0)
    def _():
        put(own_end, other_end)

    @pl.when(core == 1)
    def _():
        put(other_end, own_end)

    def finish(plane, i, at, size, value):
        where = (i, plane, pl.ds(at - box.side, size), slice(None))
        out[where] = value + out[where]

    coarse_step_body(box, 0, source, trial, pairs, guess, residual, params, finish)
    pack(box, out, *leaving)


def pack(box, field, centre, edge):
    core, place = lax.axis_index("tm") % 2, lax.axis_index("coarse")
    half = box.depth // 2
    centre[...] = field[:, pl.ds(core * half, half)]
    width = edge.shape[1] // box.depth
    up = place % 2 == core
    for i in range(box.tiles):
        for plane in range(box.depth):
            edge[i, plane * width : (plane + 1) * width, :] = jnp.where(
                up, field[i, plane, box.rows - width :, :], field[i, plane, :width, :]
            )


def last_body(box, own_depth, turn, final, first_end, joined, *rest):
    arrived, rest = rest[:4], rest[4:]
    starts, params, result, leaving = rest[0], rest[1:4], rest[4], rest[5:-7]
    source, second, trial, pairs, guess, residual, total = rest[-7:]
    place = lax.axis_index("tm")
    core = place % 2
    active = place // 2 == turn
    side, rows = box.side, box.rows
    half = box.depth // 2
    clear_ends(source, *box.span(2 * COARSE_REACH))
    clear_ends(second, *box.span(COARSE_REACH))

    @pl.when(jnp.logical_not(active))
    def _():
        source[:, 2 : 2 + box.depth, PAD : PAD + box.height, :] = jnp.zeros(
            (box.tiles, box.depth, box.height, LANES), jnp.float32
        )

    @pl.when(active)
    def _():
        centre, edge, other_centre, other_edge = arrived
        for piece, rank in ((centre, core), (other_centre, 1 - core)):
            base = rank * half
            for i in range(box.tiles):
                for plane in range(half):
                    source[i, base + plane + 2, PAD + side : PAD + side + rows, :] = (
                        piece[i, plane] - starts[0, i, base + plane, side : side + rows, :]
                    )
        width = edge.shape[1] // box.depth
        row_place, count = lax.axis_index("coarse"), lax.axis_size("coarse")
        below = row_place % 2 != core

        def edges(low, high):
            for ref, at, valid in (
                (low, side - width, row_place > 0),
                (high, side + rows, row_place < count - 1),
            ):
                for i in range(box.tiles):
                    for plane in range(box.depth):
                        value = ref[i, plane * width : (plane + 1) * width, :]
                        source[i, plane + 2, PAD + at : PAD + at + width, :] = (
                            jnp.where(valid, value, 0.0) - starts[0, i, plane, at : at + width, :]
                        )

        @pl.when(below)
        def _():
            edges(edge, other_edge)

        @pl.when(jnp.logical_not(below))
        def _():
            edges(other_edge, edge)

    def finish_once(plane, i, at, size, value):
        second[i, plane + 2, pl.ds(PAD + at, size), :] = value

    coarse_step_body(
        box, COARSE_REACH, source, trial, pairs, guess, residual, params, finish_once
    )

    base = lax.axis_index("slab") * own_depth
    if final:

        def finish_result(plane, i, at, size, value):
            where = (i, plane, pl.ds(at - side, size), slice(None))
            once = second[i, plane + 2, pl.ds(PAD + at, size), :]
            result[0, plane - base, pl.ds(at - side, size), i * LANES : (i + 1) * LANES] = jnp.where(
                core == 1, value + joined[where], once + first_end[where]
            )

        coarse_step_body(
            box, 0, second, trial, pairs, guess, residual, params, finish_result, base, own_depth
        )
        return

    def finish_twice(plane, i, at, size, value):
        where = (i, plane, pl.ds(at - box.side, size), slice(None))
        total[where] = value + joined[where]

    coarse_step_body(box, 0, second, trial, pairs, guess, residual, params, finish_twice)

    @pl.when(core == 0)
    def _():
        for i in range(box.tiles):
            result[0, :, :, i * LANES : (i + 1) * LANES] = (
                first_end[i, pl.ds(base, own_depth)]
                + second[i, pl.ds(base + 2, own_depth), PAD + side : PAD + side + rows, :]
            )

    @pl.when(core == 1)
    def _():
        for i in range(box.tiles):
            result[0, :, :, i * LANES : (i + 1) * LANES] = total[i, pl.ds(base, own_depth)]

    pack(box, total, *leaving)


def run(body, outs, scratch, *args, aliases={}):
    return pl.pallas_call(
        body,
        out_shape=[jax.ShapeDtypeStruct(shape, jnp.float32) for shape in outs],
        in_specs=[pl.BlockSpec(memory_space=pltpu.VMEM)] * len(args),
        out_specs=[pl.BlockSpec(memory_space=pltpu.VMEM)] * len(outs),
        scratch_shapes=scratch,
        input_output_aliases=aliases,
        compiler_params=pltpu.CompilerParams(vmem_limit_bytes=20 * 1024 * 1024),
    )(*args)


def slab_blocks(block):
    count = lax.axis_size("slab")
    if count == 1:
        return [block]
    if count == 2:
        return [block, lax.ppermute(block, "slab", [(0, 1), (1, 0)])]
    gathered = lax.all_gather(block, "slab", axis=0)
    return [gathered[i] for i in range(count)]


def row_swaps(hop, away):
    windows, count = lax.axis_size("tm"), lax.axis_size("coarse")
    rounds = []
    for first in (0, 1):
        pairs = []
        for place in range(count):
            other = place + 1 if place % 2 == first else place - 1
            for t in range(windows):
                inside = 0 <= other < count
                target = (hop(t), other) if inside else (away(t), place)
                pairs.append((t * count + place, target[0] * count + target[1]))
        rounds.append(pairs)
    return rounds


def row_pieces(block, width, rounds):
    rows = block.shape[-2]
    axis = block.ndim - 2
    both = ("tm", "coarse")
    odd = lax.axis_index("coarse") % 2 == 1
    pieces = []
    up, down = block, block
    left = width
    while left > 0:
        size = min(rows, left)
        if size == rows and up is down:
            send_one = send_two = block
        else:
            high = lax.slice_in_dim(up, up.shape[axis] - size, None, axis=axis)
            low = lax.slice_in_dim(down, 0, size, axis=axis)
            send_one, send_two = jnp.where(odd, low, high), jnp.where(odd, high, low)
        got_two = lax.ppermute(send_two, both, rounds[1])
        got_one = lax.ppermute(send_one, both, rounds[0])
        pieces += [got_one, got_two]
        left -= size
        if left > 0:
            up, down = jnp.where(odd, got_one, got_two), jnp.where(odd, got_two, got_one)
    return pieces


def core_swapped(block):
    count = lax.axis_size("tm")
    assert count % 2 == 0
    return lax.ppermute(block, "tm", [(i, i ^ 1) for i in range(count)])


def per_device(states, diffusivity, velocity):
    windows = lax.axis_size("tm")
    place = lax.axis_index("tm")
    own_depth, rows, columns = diffusivity.shape
    side = round_up(FINE_REACH + COARSE_REACH, 8)
    depth = own_depth * lax.axis_size("slab")
    box = Box(depth, rows, side, columns)
    tiles, height, half = box.tiles, box.height, depth // 2

    second = place % 2 == 1
    slot = lax.broadcasted_iota(jnp.int32, (3, 1, 1, 1), 0)
    parcel = jnp.where(
        (slot == 0) != second, velocity, jnp.where(slot == 1, diffusivity[None], states)
    )
    rounds = row_swaps(lambda t: t, lambda t: t ^ 1)
    blocks = slab_blocks(parcel)
    swapped = [core_swapped(block) for block in blocks]
    near = row_pieces(blocks[0], side, rounds)
    near_swapped = [core_swapped(piece) for piece in near]
    count = len(blocks)
    shapes = [(n, tiles, depth, height, LANES) for n in (2, 4, 7)]
    placed = run(
        functools.partial(early_body, box, own_depth, count),
        shapes,
        [],
        *blocks,
        *near,
        *swapped,
        *near_swapped,
    )
    far = []
    for block in blocks[1:]:
        far += row_pieces(block, side, rounds)
    far = [piece for which in (0, 1) for piece in far[which::2]]
    far_swapped = [core_swapped(piece) for piece in far]
    cut = len(far) // 2
    if far:
        placed = run(
            functools.partial(late_body, box, own_depth, count),
            shapes,
            [],
            *far[:cut],
            *far_swapped[:cut],
            *placed,
            aliases={2 * cut + n: n for n in range(3)},
        )
    first, last = box.span(COARSE_REACH)
    end, starts, coeff, weights = run(
        functools.partial(fine_body, box, COARSE_REACH, own_depth, count),
        [(tiles, depth, last - first, LANES)] + shapes,
        [box.scratch(), box.scratch()],
        *far[cut:],
        *far_swapped[cut:],
        *placed,
        aliases={2 * cut + n: 1 + n for n in range(3)},
    )
    params = run(
        functools.partial(prepare_body, box),
        [(7, tiles, half, height, LANES), (tiles, depth, height, LANES)],
        [pltpu.VMEM((4, *box.scratch(half).shape), jnp.float32)],
        coeff,
    )
    params = [weights, *params]
    width = 2 * COARSE_REACH
    assert rows >= width
    leaving_shapes = [(tiles, half, rows, LANES), (tiles, depth * width, LANES)]
    joined, first_end, *leaving = run(
        functools.partial(pair_body, box),
        [(tiles, depth, rows, LANES)] * 2 + leaving_shapes,
        [box.scratch()] + coarse_scratch(box),
        end,
        core_swapped(end),
        starts,
        *params,
    )
    ends = jnp.where(place % 2 == 1, joined, first_end)
    ends = jnp.concatenate([ends[i] for i in range(tiles)], axis=-1)
    base = lax.axis_index("slab") * own_depth
    result = lax.dynamic_slice_in_dim(ends, base, own_depth, 0)[None]
    hop = lambda t: (t + 2) % windows
    one, two = row_swaps(hop, hop)
    across = [(t, hop(t)) for t in range(windows)]
    count = lax.axis_size("coarse")
    aside = [
        pair for pairs, core in ((one, 0), (two, 1)) for pair in pairs if pair[0] // count % 2 == core
    ]
    for turn in range(1, windows // 2):
        centre = lax.ppermute(leaving[0], "tm", across)
        edge = lax.ppermute(leaving[1], ("tm", "coarse"), aside)
        other_centre = core_swapped(centre)
        other_edge = core_swapped(edge)
        arrived = [centre, edge, other_centre, other_edge]
        final = turn == windows // 2 - 1
        out, *leaving = run(
            functools.partial(last_body, box, own_depth, turn, final),
            [(1, own_depth, rows, columns)] + ([] if final else leaving_shapes),
            [box.scratch()] * 2
            + coarse_scratch(box)
            + [pltpu.VMEM((tiles, depth, rows, LANES), jnp.float32)],
            first_end,
            joined,
            *arrived,
            starts,
            *params,
        )
        result = out if turn == 1 else jnp.where(place // 2 >= turn, out, result)
    return result


def solution(mesh):
    return jax.shard_map(
        per_device,
        mesh=mesh,
        in_specs=(
            P("tm", "slab", "coarse", None),
            P("slab", "coarse", None),
            P(None, "slab", "coarse", None),
        ),
        out_specs=P("tm", "slab", "coarse", None),
        check_vma=False,
    )
```

```python
import functools

import jax
import jax.numpy as jnp
from jax import lax
from jax.experimental import pallas as pl
from jax.experimental.pallas import tpu as pltpu
from jax.sharding import PartitionSpec as P

SECTIONS = 4
FINE_STEPS = 2
FINE_STEP = 1.0
RELAX = 0.8
INTERVAL = FINE_STEPS * FINE_STEP
LANES = 128
PAD = 8
COARSE_REACH = 6
FINE_REACH = SECTIONS * FINE_STEPS


def chebyshev_coefficients(sections):
    damping = 0.05
    centre_point = 1.0 + damping / (sections * sections)
    chebyshev = [1.0, centre_point]
    slopes = [0.0, 1.0]
    for degree in range(2, sections + 1):
        chebyshev.append(2.0 * centre_point * chebyshev[degree - 1] - chebyshev[degree - 2])
        slopes.append(
            2.0 * chebyshev[degree - 1]
            + 2.0 * centre_point * slopes[degree - 1]
            - slopes[degree - 2]
        )
    slope_ratio = chebyshev[sections] / slopes[sections]
    weights = [1.0 / entry for entry in chebyshev]
    scales = [0.0, 0.0]
    carries = [0.0, 0.0]
    tildes = [0.0, slope_ratio / centre_point]
    for degree in range(2, sections + 1):
        scales.append(2.0 * weights[degree] * centre_point / weights[degree - 1])
        carries.append(-weights[degree] / weights[degree - 2])
        tildes.append(2.0 * weights[degree] * slope_ratio / weights[degree - 1])
    return (scales, carries, tildes)


def round_up(value, unit):
    return -(-value // unit) * unit


class Box:
    def __init__(self, depth, rows, side, columns):
        self.depth, self.rows, self.side, self.columns = depth, rows, side, columns
        self.height = rows + 2 * side
        self.tiles = columns // LANES

    def scratch(self, depth=None):
        depth = self.depth if depth is None else depth
        return pltpu.VMEM(
            (self.tiles, depth + 4, self.height + 2 * PAD, LANES), jnp.float32
        )

    def span(self, margin):
        size = round_up(self.rows + 2 * margin, 8)
        first = self.side - (size - self.rows) // 2
        assert first >= 0 and first % 2 == 0
        return first, first + size


CHUNK = 8
FINE_CHUNK = 24
AFTER_DEPTH, BEFORE_DEPTH, AFTER_ROW, BEFORE_ROW, AFTER_COLUMN, BEFORE_COLUMN, CENTRE = range(7)


def chunks(first, last, most):
    at = first
    while at < last:
        size = min(most, last - at)
        yield at, size
        at += size


def sweep(count, first, last, body, most=CHUNK):
    if count <= 8:
        for at, size in chunks(first, last, most):
            cache = {}
            for plane in range(count):
                body(plane, at, size, cache)
    else:

        def step(plane, carry):
            for at, size in chunks(first, last, most):
                body(plane, at, size, None)
            return carry

        lax.fori_loop(0, count, step, 0)


def lane_index(size):
    return lax.broadcasted_iota(jnp.int32, (size, LANES), 1)


def row_index(size):
    return lax.broadcasted_iota(jnp.int32, (size, LANES), 0)


def sideways(values, step):
    lane = lane_index(values[0].shape[0])
    back = [pltpu.roll(entry, LANES - step, 1) for entry in values]
    forth = [pltpu.roll(entry, step, 1) for entry in values]
    count = len(values)
    after = [
        jnp.where(lane >= LANES - step, back[i + 1], back[i]) if i + 1 < count else back[i]
        for i in range(count)
    ]
    before = [jnp.where(lane < step, forth[i - 1], forth[i]) if i else forth[i] for i in range(count)]
    return after, before


def neighbours(field, weights, plane, at, size, step, cache):
    tiles = field.shape[0]

    def level(i, index):
        if cache is None:
            return field[i, index, pl.ds(PAD + at, size), :]
        if (i, index) not in cache:
            cache[i, index] = field[i, index, pl.ds(PAD + at, size), :]
        return cache[i, index]

    def weight(kind, i):
        return weights[kind, i, plane, pl.ds(at, size), :]

    centre = [level(i, plane + 2) for i in range(tiles)]
    after, before = sideways(centre, step)
    result = []
    for i in range(tiles):
        row_after = field[i, plane + 2, pl.ds(PAD + at + step, size), :]
        row_before = field[i, plane + 2, pl.ds(PAD + at - step, size), :]
        deep = weight(AFTER_DEPTH, i) * level(i, plane + 3) + weight(BEFORE_DEPTH, i) * level(
            i, plane + 1
        )
        down = weight(AFTER_ROW, i) * row_after + weight(BEFORE_ROW, i) * row_before
        along = weight(AFTER_COLUMN, i) * after[i] + weight(BEFORE_COLUMN, i) * before[i]
        result.append(((deep + down) + along, centre[i]))
    return result


def set_weights(weights, where, c, scale, drift_scale, tile, tiles, step):
    size = c[0].shape[-2]
    base = scale * c[0]
    for axis in range(3):
        drift = drift_scale * c[axis + 1]
        after, before = base - drift, base + drift
        if axis == 2 and tile == tiles - 1:
            after = jnp.where(lane_index(size) >= LANES - step, 0.0, after)
        if axis == 2 and tile == 0:
            before = jnp.where(lane_index(size) < step, 0.0, before)
        weights[(2 * axis,) + where] = after
        weights[(2 * axis + 1,) + where] = before


def clear_ends(field, first, last):
    tiles, planes = field.shape[:2]
    plane = jnp.zeros((tiles, 1, last - first, LANES), jnp.float32)
    field[:, 1:2, PAD + first : PAD + last, :] = plane
    field[:, planes - 2 : planes - 1, PAD + first : PAD + last, :] = plane


def fine_scheme():
    scales, carries, tildes = chebyshev_coefficients(SECTIONS)
    centre = INTERVAL / (tildes[1] * FINE_STEP)
    factors = [1.0]
    for degree in range(1, SECTIONS + 1):
        factors.append(factors[-1] * tildes[degree] * FINE_STEP / INTERVAL)
    back = [0.0, 0.0]
    for degree in range(2, SECTIONS + 1):
        back.append(carries[degree] * factors[degree - 2] / factors[degree])
    return centre, back, factors[SECTIONS]


def row_places(box, sizes):
    place, count = lax.axis_index("coarse"), lax.axis_size("coarse")
    odd = place % 2
    result = []
    gone = 0
    for step, size in enumerate(sizes, 1):
        below = pl.multiple_of(box.side - gone - size, 8)
        above = pl.multiple_of(box.side + box.rows + gone, 8)
        gone += size
        one = pl.multiple_of(jnp.where(odd == 1, below, above), 8)
        two = pl.multiple_of(jnp.where(odd == 1, above, below), 8)
        below_valid, above_valid = place >= step, place + step < count
        one_valid = jnp.where(odd == 1, below_valid, above_valid)
        two_valid = jnp.where(odd == 1, above_valid, below_valid)
        result.append(((one, one_valid), (two, two_valid)))
    return result


def place_pieces(box, own_depth, pieces, starts, coeff, weights):
    core = lax.axis_index("tm") % 2
    centre_constant = fine_scheme()[0]
    for own, other, block, blocks, at, valid in pieces:
        shift = lax.axis_index("slab") if blocks == 2 else 0
        base = (block + shift) % blocks * own_depth
        size = own.shape[-2]
        for plane in range(own_depth):
            for i in range(box.tiles):
                cols = slice(i * LANES, (i + 1) * LANES)
                where = (i, base + plane, pl.ds(at, size), slice(None))
                for ref, rank in ((own, core), (other, 1 - core)):
                    for slot, kind in ((2 - 2 * rank, None), (rank, 1 + rank), (1 + rank, 3 * rank)):
                        value = ref[slot, plane, :, cols]
                        if valid is not None:
                            value = jnp.where(valid, value, 0.0)
                        if kind is None:
                            starts[(rank,) + where] = value
                        else:
                            coeff[(kind,) + where] = value
                c = [coeff[(k,) + where] for k in range(4)]
                set_weights(weights, where, c, INTERVAL, 0.5 * INTERVAL, i, box.tiles, 1)
                weights[(CENTRE,) + where] = centre_constant - 6.0 * INTERVAL * c[0]


def early_body(box, own_depth, blocks, *refs):
    starts, coeff, weights = refs[-3:]
    half = (len(refs) - 3) // 2
    own, other = refs[:half], refs[half : 2 * half]
    places = row_places(box, [ref.shape[-2] for ref in own[blocks::2]])
    moves = [(own[block], other[block], block, blocks, box.side, None) for block in range(blocks)]
    for step, pair in enumerate(places):
        for which, (at, valid) in enumerate(pair):
            index = blocks + 2 * step + which
            moves.append((own[index], other[index], 0, blocks, at, valid))
    place_pieces(box, own_depth, moves, starts, coeff, weights)


def late_moves(box, blocks, own, other, which):
    if blocks == 1:
        return []
    steps = len(own) // (blocks - 1)
    places = row_places(box, [ref.shape[-2] for ref in own[:steps]])
    return [
        (own[n], other[n], 1 + n // steps, blocks, *places[n % steps][which]) for n in range(len(own))
    ]


def late_body(box, own_depth, blocks, *refs):
    half = (len(refs) - 6) // 2
    moves = late_moves(box, blocks, refs[:half], refs[half : 2 * half], 0)
    place_pieces(box, own_depth, moves, *refs[-3:])


def fine_body(box, margin, own_depth, blocks, *refs):
    end, starts, coeff, weights, one, two = refs[-6:]
    half = (len(refs) - 9) // 2
    core = lax.axis_index("tm") % 2
    moves = late_moves(box, blocks, refs[:half], refs[half : 2 * half], 1)
    place_pieces(box, own_depth, moves, starts, coeff, weights)
    clear_ends(one, 0, box.height)
    clear_ends(two, 0, box.height)
    one[:, 2 : 2 + box.depth, PAD : PAD + box.height, :] = starts[core]
    _, back, factor = fine_scheme()
    stage = 0
    current, other_field = one, two
    first, last = box.span(margin)
    for repeat in range(FINE_STEPS):
        for degree in range(1, SECTIONS + 1):
            stage += 1
            final = stage == FINE_REACH

            def body(plane, at, size, cache, current=current, old=other_field, degree=degree, final=final):
                values = neighbours(current, weights, plane, at, size, 1, cache)
                for i, (total, centre) in enumerate(values):
                    value = total + weights[CENTRE, i, plane, pl.ds(at, size), :] * centre
                    where = (i, plane + 2, pl.ds(PAD + at, size), slice(None))
                    if degree > 1:
                        value = value + back[degree] * old[where]
                    if final:
                        end[i, plane, pl.ds(at - first, size), :] = factor**FINE_STEPS * value
                    else:
                        old[where] = value

            sweep(box.depth, *box.span(margin + FINE_REACH - stage), body, FINE_CHUNK)
            current, other_field = other_field, current


def pair_columns(value):
    lane = lane_index(value.shape[0])
    other = jnp.where(
        lane % 2 == 0, pltpu.roll(value, LANES - 1, 1), pltpu.roll(value, 1, 1)
    )
    return value + other


def pair_rows(field, i, plane, at, size):
    row = row_index(size)
    other = jnp.where(
        row % 2 == 0,
        field[i, plane + 2, pl.ds(PAD + at + 1, size), :],
        field[i, plane + 2, pl.ds(PAD + at - 1, size), :],
    )
    return field[i, plane + 2, pl.ds(PAD + at, size), :] + other


def prepare_body(box, coeff, coarse, weight, work):
    half = box.depth // 2
    for k in range(4):
        def columns(plane, at, size, cache, k=k):
            for i in range(box.tiles):
                low = coeff[k, i, 2 * plane, pl.ds(at, size), :]
                high = coeff[k, i, 2 * plane + 1, pl.ds(at, size), :]
                work[k, i, plane + 2, pl.ds(PAD + at, size), :] = pair_columns(low + high)
                if k == 0:
                    for offset, value in ((0, low), (1, high)):
                        weight[i, 2 * plane + offset, pl.ds(at, size), :] = RELAX / (
                            1.0 + 6.0 * INTERVAL * value
                        )

        sweep(half, 0, box.height, columns)

    def rows(plane, at, size, cache):
        for i in range(box.tiles):
            where = (i, plane, pl.ds(at, size), slice(None))
            c = [0.125 * pair_rows(work.at[k], i, plane, at, size) for k in range(4)]
            set_weights(coarse, where, c, INTERVAL / 4.0, INTERVAL / 4.0, i, box.tiles, 2)
            coarse[(CENTRE,) + where] = RELAX / (1.0 + 6.0 * INTERVAL / 4.0 * c[0])

    sweep(half, 0, box.height, rows)


def coarse_step_body(
    box, margin, source, trial, pairs, guess, residual, params, finish, base=0, planes=None
):
    weights, coarse, weight = params
    half = box.depth // 2
    centre_constant = fine_scheme()[0]

    def smooth(plane, at, size, cache):
        values = neighbours(source, weights, plane, at, size, 1, cache)
        for i, (total, centre) in enumerate(values):
            trial[i, plane + 2, pl.ds(PAD + at, size), :] = (1.0 - RELAX) * centre + weight[
                i, plane, pl.ds(at, size), :
            ] * (centre + total)

    first, last = box.span(margin + 5)
    clear_ends(trial, first, last)
    sweep(box.depth, first, last, smooth)

    def restrict(plane, at, size, cache):
        sums = [None] * box.tiles
        for half_plane in range(2):
            fine_plane = 2 * plane + half_plane
            values = neighbours(trial, weights, fine_plane, at, size, 1, cache)
            for i, (total, centre) in enumerate(values):
                given = source[i, fine_plane + 2, pl.ds(PAD + at, size), :]
                inner = weights[CENTRE, i, fine_plane, pl.ds(at, size), :] - (1.0 + centre_constant)
                misfit = (given + total) + inner * centre
                sums[i] = misfit if sums[i] is None else sums[i] + misfit
        for i in range(box.tiles):
            pairs[i, plane + 2, pl.ds(PAD + at, size), :] = sums[i]

    first, last = box.span(margin + 4)
    sweep(half, first, last, restrict)

    def first_guess(plane, at, size, cache):
        for i in range(box.tiles):
            mean = 0.125 * pair_columns(pair_rows(pairs, i, plane, at, size))
            residual[i, plane + 2, pl.ds(PAD + at, size), :] = mean
            guess[i, plane + 2, pl.ds(PAD + at, size), :] = (
                coarse[CENTRE, i, plane, pl.ds(at, size), :] * mean
            )

    clear_ends(guess, first, last)
    sweep(half, first, last, first_guess)

    def correct(plane, at, size, cache):
        values = neighbours(guess, coarse, plane, at, size, 2, cache)
        for i, (total, centre) in enumerate(values):
            rest = residual[i, plane + 2, pl.ds(PAD + at, size), :] + total
            fix = (1.0 - RELAX) * centre + coarse[CENTRE, i, plane, pl.ds(at, size), :] * rest
            for half_plane in range(2):
                where = (i, 2 * plane + half_plane + 2, pl.ds(PAD + at, size), slice(None))
                trial[where] = trial[where] + fix

    sweep(half, *box.span(margin + 2), correct)

    def smooth_again(plane, at, size, cache):
        values = neighbours(trial, weights, plane, at, size, 1, cache)
        for i, (total, centre) in enumerate(values):
            given = source[i, plane + 2, pl.ds(PAD + at, size), :]
            value = (1.0 - RELAX) * centre + weight[i, plane, pl.ds(at, size), :] * (given + total)
            finish(plane, i, at, size, value)

    if planes is None:
        sweep(box.depth, *box.span(margin), smooth_again, 2 * CHUNK)
    else:
        sweep(
            planes,
            *box.span(margin),
            lambda plane, at, size, cache: smooth_again(base + plane, at, size, None),
        )


def coarse_scratch(box):
    half = box.depth // 2
    return [box.scratch(), box.scratch(half), box.scratch(half), box.scratch(half)]


def pair_body(box, own_end, other_end, starts, *rest):
    params, out, first_out, leaving = rest[:3], rest[3], rest[4], rest[5:7]
    source, trial, pairs, guess, residual = rest[7:]
    core = lax.axis_index("tm") % 2
    first, last = box.span(COARSE_REACH)
    clear_ends(source, first, last)

    def put(first_end, second_end):
        source[:, 2 : 2 + box.depth, PAD + first : PAD + last, :] = (
            first_end[...] - starts[1, :, :, first:last, :]
        )
        inner = slice(box.side - first, box.side - first + box.rows)
        out[...] = second_end[:, :, inner, :]
        first_out[...] = first_end[:, :, inner, :]

    @pl.when(core == 0)
    def _():
        put(own_end, other_end)

    @pl.when(core == 1)
    def _():
        put(other_end, own_end)

    def finish(plane, i, at, size, value):
        where = (i, plane, pl.ds(at - box.side, size), slice(None))
        out[where] = value + out[where]

    coarse_step_body(box, 0, source, trial, pairs, guess, residual, params, finish)
    pack(box, out, *leaving)


def pack(box, field, centre, edge):
    core, place = lax.axis_index("tm") % 2, lax.axis_index("coarse")
    half = box.depth // 2
    centre[...] = field[:, pl.ds(core * half, half)]
    width = edge.shape[1] // box.depth
    up = place % 2 == core
    for i in range(box.tiles):
        for plane in range(box.depth):
            edge[i, plane * width : (plane + 1) * width, :] = jnp.where(
                up, field[i, plane, box.rows - width :, :], field[i, plane, :width, :]
            )


def last_body(box, own_depth, turn, final, first_end, joined, *rest):
    arrived, rest = rest[:4], rest[4:]
    starts, params, result, leaving = rest[0], rest[1:4], rest[4], rest[5:-7]
    source, second, trial, pairs, guess, residual, total = rest[-7:]
    place = lax.axis_index("tm")
    core = place % 2
    active = place // 2 == turn
    side, rows = box.side, box.rows
    half = box.depth // 2
    clear_ends(source, *box.span(2 * COARSE_REACH))
    clear_ends(second, *box.span(COARSE_REACH))

    @pl.when(jnp.logical_not(active))
    def _():
        source[:, 2 : 2 + box.depth, PAD : PAD + box.height, :] = jnp.zeros(
            (box.tiles, box.depth, box.height, LANES), jnp.float32
        )

    @pl.when(active)
    def _():
        centre, edge, other_centre, other_edge = arrived
        for piece, rank in ((centre, core), (other_centre, 1 - core)):
            base = rank * half
            for i in range(box.tiles):
                for plane in range(half):
                    source[i, base + plane + 2, PAD + side : PAD + side + rows, :] = (
                        piece[i, plane] - starts[0, i, base + plane, side : side + rows, :]
                    )
        width = edge.shape[1] // box.depth
        row_place, count = lax.axis_index("coarse"), lax.axis_size("coarse")
        below = row_place % 2 != core

        def edges(low, high):
            for ref, at, valid in (
                (low, side - width, row_place > 0),
                (high, side + rows, row_place < count - 1),
            ):
                for i in range(box.tiles):
                    for plane in range(box.depth):
                        value = ref[i, plane * width : (plane + 1) * width, :]
                        source[i, plane + 2, PAD + at : PAD + at + width, :] = (
                            jnp.where(valid, value, 0.0) - starts[0, i, plane, at : at + width, :]
                        )

        @pl.when(below)
        def _():
            edges(edge, other_edge)

        @pl.when(jnp.logical_not(below))
        def _():
            edges(other_edge, edge)

    def finish_once(plane, i, at, size, value):
        second[i, plane + 2, pl.ds(PAD + at, size), :] = value

    coarse_step_body(
        box, COARSE_REACH, source, trial, pairs, guess, residual, params, finish_once
    )

    base = lax.axis_index("slab") * own_depth
    if final:

        def finish_result(plane, i, at, size, value):
            where = (i, plane, pl.ds(at - side, size), slice(None))
            once = second[i, plane + 2, pl.ds(PAD + at, size), :]
            result[0, plane - base, pl.ds(at - side, size), i * LANES : (i + 1) * LANES] = jnp.where(
                core == 1, value + joined[where], once + first_end[where]
            )

        coarse_step_body(
            box, 0, second, trial, pairs, guess, residual, params, finish_result, base, own_depth
        )
        return

    def finish_twice(plane, i, at, size, value):
        where = (i, plane, pl.ds(at - box.side, size), slice(None))
        total[where] = value + joined[where]

    coarse_step_body(box, 0, second, trial, pairs, guess, residual, params, finish_twice)

    @pl.when(core == 0)
    def _():
        for i in range(box.tiles):
            result[0, :, :, i * LANES : (i + 1) * LANES] = (
                first_end[i, pl.ds(base, own_depth)]
                + second[i, pl.ds(base + 2, own_depth), PAD + side : PAD + side + rows, :]
            )

    @pl.when(core == 1)
    def _():
        for i in range(box.tiles):
            result[0, :, :, i * LANES : (i + 1) * LANES] = total[i, pl.ds(base, own_depth)]

    pack(box, total, *leaving)


def run(body, outs, scratch, *args, aliases={}):
    return pl.pallas_call(
        body,
        out_shape=[jax.ShapeDtypeStruct(shape, jnp.float32) for shape in outs],
        in_specs=[pl.BlockSpec(memory_space=pltpu.VMEM)] * len(args),
        out_specs=[pl.BlockSpec(memory_space=pltpu.VMEM)] * len(outs),
        scratch_shapes=scratch,
        input_output_aliases=aliases,
        compiler_params=pltpu.CompilerParams(
            vmem_limit_bytes=20 * 1024 * 1024,
        ),
    )(*args)


def slab_blocks(block):
    count = lax.axis_size("slab")
    if count == 1:
        return [block]
    if count == 2:
        return [block, lax.ppermute(block, "slab", [(0, 1), (1, 0)])]
    gathered = lax.all_gather(block, "slab", axis=0)
    return [gathered[i] for i in range(count)]


def row_swaps(hop, away):
    windows, count = lax.axis_size("tm"), lax.axis_size("coarse")
    rounds = []
    for first in (0, 1):
        pairs = []
        for place in range(count):
            other = place + 1 if place % 2 == first else place - 1
            for t in range(windows):
                inside = 0 <= other < count
                target = (hop(t), other) if inside else (away(t), place)
                pairs.append((t * count + place, target[0] * count + target[1]))
        rounds.append(pairs)
    return rounds


def row_pieces(block, width, rounds):
    rows = block.shape[-2]
    axis = block.ndim - 2
    both = ("tm", "coarse")
    odd = lax.axis_index("coarse") % 2 == 1
    pieces = []
    up, down = block, block
    left = width
    while left > 0:
        size = min(rows, left)
        if size == rows and up is down:
            send_one = send_two = block
        else:
            high = lax.slice_in_dim(up, up.shape[axis] - size, None, axis=axis)
            low = lax.slice_in_dim(down, 0, size, axis=axis)
            send_one, send_two = jnp.where(odd, low, high), jnp.where(odd, high, low)
        got_two = lax.ppermute(send_two, both, rounds[1])
        got_one = lax.ppermute(send_one, both, rounds[0])
        pieces += [got_one, got_two]
        left -= size
        if left > 0:
            up, down = jnp.where(odd, got_one, got_two), jnp.where(odd, got_two, got_one)
    return pieces


def core_swapped(block):
    count = lax.axis_size("tm")
    assert count % 2 == 0
    return lax.ppermute(block, "tm", [(i, i ^ 1) for i in range(count)])


def per_device(states, diffusivity, velocity):
    windows = lax.axis_size("tm")
    place = lax.axis_index("tm")
    own_depth, rows, columns = diffusivity.shape
    side = round_up(FINE_REACH + COARSE_REACH, 8)
    depth = own_depth * lax.axis_size("slab")
    box = Box(depth, rows, side, columns)
    tiles, height, half = box.tiles, box.height, depth // 2

    second = place % 2 == 1
    slot = lax.broadcasted_iota(jnp.int32, (3, 1, 1, 1), 0)
    parcel = jnp.where(
        (slot == 0) != second, velocity, jnp.where(slot == 1, diffusivity[None], states)
    )
    rounds = row_swaps(lambda t: t, lambda t: t ^ 1)
    blocks = slab_blocks(parcel)
    swapped = [core_swapped(block) for block in blocks]
    near = row_pieces(blocks[0], side, rounds)
    near_swapped = [core_swapped(piece) for piece in near]
    count = len(blocks)
    shapes = [(n, tiles, depth, height, LANES) for n in (2, 4, 7)]
    placed = run(
        functools.partial(early_body, box, own_depth, count),
        shapes,
        [],
        *blocks,
        *near,
        *swapped,
        *near_swapped,
    )
    far = []
    for block in blocks[1:]:
        far += row_pieces(block, side, rounds)
    far = [piece for which in (0, 1) for piece in far[which::2]]
    far_swapped = [core_swapped(piece) for piece in far]
    cut = len(far) // 2
    if far:
        placed = run(
            functools.partial(late_body, box, own_depth, count),
            shapes,
            [],
            *far[:cut],
            *far_swapped[:cut],
            *placed,
            aliases={2 * cut + n: n for n in range(3)},
        )
    first, last = box.span(COARSE_REACH)
    end, starts, coeff, weights = run(
        functools.partial(fine_body, box, COARSE_REACH, own_depth, count),
        [(tiles, depth, last - first, LANES)] + shapes,
        [box.scratch(), box.scratch()],
        *far[cut:],
        *far_swapped[cut:],
        *placed,
        aliases={2 * cut + n: 1 + n for n in range(3)},
    )
    params = run(
        functools.partial(prepare_body, box),
        [(7, tiles, half, height, LANES), (tiles, depth, height, LANES)],
        [pltpu.VMEM((4, *box.scratch(half).shape), jnp.float32)],
        coeff,
    )
    params = [weights, *params]
    width = 2 * COARSE_REACH
    assert rows >= width
    leaving_shapes = [(tiles, half, rows, LANES), (tiles, depth * width, LANES)]
    joined, first_end, *leaving = run(
        functools.partial(pair_body, box),
        [(tiles, depth, rows, LANES)] * 2 + leaving_shapes,
        [box.scratch()] + coarse_scratch(box),
        end,
        core_swapped(end),
        starts,
        *params,
    )
    ends = jnp.where(place % 2 == 1, joined, first_end)
    ends = jnp.concatenate([ends[i] for i in range(tiles)], axis=-1)
    base = lax.axis_index("slab") * own_depth
    result = lax.dynamic_slice_in_dim(ends, base, own_depth, 0)[None]
    hop = lambda t: (t + 2) % windows
    one, two = row_swaps(hop, hop)
    across = [(t, hop(t)) for t in range(windows)]
    count = lax.axis_size("coarse")
    aside = [
        pair for pairs, core in ((one, 0), (two, 1)) for pair in pairs if pair[0] // count % 2 == core
    ]
    for turn in range(1, windows // 2):
        arrived = [
            lax.ppermute(leaving[0], "tm", across),
            lax.ppermute(leaving[1], ("tm", "coarse"), aside),
        ]
        arrived += [core_swapped(piece) for piece in arrived]
        final = turn == windows // 2 - 1
        out, *leaving = run(
            functools.partial(last_body, box, own_depth, turn, final),
            [(1, own_depth, rows, columns)] + ([] if final else leaving_shapes),
            [box.scratch()] * 2
            + coarse_scratch(box)
            + [pltpu.VMEM((tiles, depth, rows, LANES), jnp.float32)],
            first_end,
            joined,
            *arrived,
            starts,
            *params,
        )
        result = out if turn == 1 else jnp.where(place // 2 >= turn, out, result)
    return result


def solution(mesh):
    return jax.shard_map(
        per_device,
        mesh=mesh,
        in_specs=(
            P("tm", "slab", "coarse", None),
            P("slab", "coarse", None),
            P(None, "slab", "coarse", None),
        ),
        out_specs=P("tm", "slab", "coarse", None),
        check_vma=False,
    )
```
